32 devices in a mesh: dp: 16 (over z, y, x), head: 2 (over core).
Axes of the slice: x: 2, y: 2, z: 4, core: 2. Of those that a mesh axis runs over, the one named last changes fastest.
Arguments:
- inputs: bfloat16 [128, 200, 768], P(('dp', 'head')), may hold values from -6 to 6
- masked: int32 [128, 200], P(('dp', 'head')), may hold values 0 or 1
- key_valid: int32 [128, 200], P('dp'), may hold values from 0 to 1, as said below
- rel_index: int32 [200, 200], replicated, may hold values from 0 to 731
- mask_token: float32 [768], replicated, may hold values from -6 to 6
- ln1_gain: float32 [768], replicated, may hold values from 0.25 to 1.75
- ln1_bias: float32 [768], replicated, may hold values from -1.75 to 1.75
- w_qkv: bfloat16 [768, 3, 768], P(None, None, 'head'), may hold values from -0.21875 to 0.21875
- qv_bias: float32 [2, 768], P(None, 'head'), may hold values from -1.75 to 1.75
- rel_table: float32 [732, 12], P(None, 'head'), may hold values from -3 to 3
- w_proj: bfloat16 [768, 768], P('head'), may hold values from -0.875 to 0.875
- proj_bias: float32 [768], replicated, may hold values from -1.75 to 1.75
- gamma1: float32 [768], replicated, may hold values from 0.5 to 1.5
- ln2_gain: float32 [768], replicated, may hold values from 0.25 to 1.75
- ln2_bias: float32 [768], replicated, may hold values from -1.75 to 1.75
- w_fc1: bfloat16 [768, 3072], P(None, ('dp', 'head')), may hold values from -0.21875 to 0.21875
- fc1_bias: bfloat16 [3072], P(('dp', 'head')), may hold values from -1.75 to 1.75
- w_fc2: bfloat16 [3072, 768], P(('dp', 'head')), may hold values from -0.109375 to 0.109375
- fc2_bias: float32 [768], replicated, may hold values from -1.75 to 1.75
- gamma2: float32 [768], replicated, may hold values from 0.5 to 1.5
- cotangent: bfloat16 [128, 200, 768], P(('dp', 'head')), may hold values from -6 to 6
Outputs:
- out: bfloat16 [128, 200, 768], P(('dp', 'head'))
- grad_input: float32 [128, 200, 768], P(('dp', 'head'))
- grad_mask_token: float32 [768], replicated
- grad_ln1_gain: float32 [768], replicated
- grad_ln1_bias: float32 [768], replicated
- grad_qkv: float32 [768, 3, 768], P(None, None, 'head')
- grad_qv_bias: float32 [2, 768], P(None, 'head')
- grad_rel_table: float32 [732, 12], P(None, 'head')
- grad_proj: float32 [768, 768], P('head')
- grad_proj_bias: float32 [768], replicated
- grad_gamma1: float32 [768], replicated
- grad_ln2_gain: float32 [768], replicated
- grad_ln2_bias: float32 [768], replicated
- grad_fc1: float32 [768, 3072], P(None, ('dp', 'head'))
- grad_fc1_bias: float32 [3072], P(('dp', 'head'))
- grad_fc2: float32 [3072, 768], P(('dp', 'head'))
- grad_fc2_bias: float32 [768], replicated
- grad_gamma2: float32 [768], replicated
The draws below stay inside these ranges and needn't reach their ends.
Inputs may be any that keep to these rules, and one draw needn't show every extreme that they name: In each image the ones of key_valid are a leading run of rows, at least 100 long.
All inputs are finite; a program needn't handle non-finite values. No bound on the sum of `masked` on one device may be relied on, other than what follows from the above.
Results may differ from the reference program's by a relative error of at most 0.012.
The reference program's roundings to bfloat16 on the way count: a program that leaves them out, or rounds other values in their place, can miss the bound.
Values may be sent and summed in bfloat16 or wider, within the bound.
A program may use at most 256 MiB of HBM per device.

```python
import jax
import jax.numpy as jnp
from jax import lax

D = 768
HEADS = 12
FF = 3072
NREL = 732
ROWS = 200
IMG_DEV = 8
HEAD_DIM = 64
IMAGES = 128


def draw_key_valid(key, part):
    lengths = jax.random.randint(key, (IMAGES, 1), ROWS // 2, ROWS + 1)
    return (jnp.arange(ROWS)[None, :] < lengths).astype(jnp.int32)


def with_ends(values, own_key, least, high):
    place = [jax.random.randint(jax.random.fold_in(own_key, axis), (), 0, length) for axis, length in enumerate(values.shape)]
    longest = values.shape.index(max(values.shape))
    beside = place[:longest] + [(place[longest] + 1) % values.shape[longest]] + place[longest + 1:]
    return values.at[tuple(place)].set(least).at[tuple(beside)].set(high)


def level_of(own_key, dims, shards, smallest, high):
    def one(dim, parts):
        draws = jax.random.uniform(jax.random.fold_in(jax.random.fold_in(own_key, 6), dim), (parts,), jnp.float32, smallest / len(shards), high / len(shards))
        return jnp.repeat(jnp.exp(draws), dims[dim] // parts).reshape((-1,) + (1,) * (len(dims) - dim - 1))

    loudness = one(*shards[0])
    for cut in shards[1:]:
        loudness = loudness * one(*cut)
    return loudness


def noise(stream_key, dims, scale, reach, cuts=(), kind=jnp.bfloat16):
    level = level_of(stream_key, dims, cuts, -0.22, 0.18) if cuts else 1.0
    values = jax.random.normal(stream_key, dims, jnp.float32) * scale * level
    return jnp.minimum(jnp.maximum(values, -reach), reach).astype(kind)


def setup_inputs(seed: int = 0) -> dict:
    key_list = jax.random.split(jax.random.key(seed), 22)
    return {
        "inputs": noise(key_list[0], (IMAGES, ROWS, D), 1.0, 6.0, ((0, 32),)),
        "masked": with_ends((jax.random.randint(key_list[1], (IMAGES, ROWS), 0, 5) < 2).astype(jnp.int32), jax.random.fold_in(key_list[1], 1), 0, 1),
        "key_valid": draw_key_valid(jax.random.fold_in(key_list[21], 71), 0),
        "rel_index": with_ends(jax.random.randint(key_list[3], (ROWS, ROWS), 0, NREL), jax.random.fold_in(key_list[3], 1), 0, NREL - 1).astype(jnp.int32),
        "mask_token": noise(key_list[4], (D,), 1.0, 6.0, (), jnp.float32),
        "ln1_gain": jnp.clip(1.0 + 0.15 * jax.random.normal(key_list[5], (D,), jnp.float32), 0.25, 1.75),
        "ln1_bias": noise(key_list[6], (D,), 0.3, 1.75, (), jnp.float32),
        "w_qkv": noise(key_list[7], (D, 3, D), D ** -0.5, 0.21875, ((2, 2),)),
        "qv_bias": noise(key_list[8], (2, D), 0.3, 1.75, ((1, 2),), jnp.float32),
        "rel_table": noise(key_list[9], (NREL, HEADS), 0.5, 3.0, ((1, 2),), jnp.float32),
        "w_proj": noise(key_list[10], (D, D), (D // 16) ** -0.5, 0.875, ((0, 2),)),
        "proj_bias": noise(key_list[11], (D,), 0.3, 1.75, (), jnp.float32),
        "gamma1": jnp.clip(jax.random.uniform(key_list[12], (D,), jnp.float32, 0.5, 1.5), 0.5, 1.5),
        "ln2_gain": jnp.clip(1.0 + 0.15 * jax.random.normal(key_list[13], (D,), jnp.float32), 0.25, 1.75),
        "ln2_bias": noise(key_list[14], (D,), 0.3, 1.75, (), jnp.float32),
        "w_fc1": noise(key_list[15], (D, FF), D ** -0.5, 0.21875, ((1, 32),)),
        "fc1_bias": noise(key_list[16], (FF,), 0.3, 1.75, ((0, 32),)),
        "w_fc2": noise(key_list[17], (FF, D), FF ** -0.5, 0.109375, ((0, 32),)),
        "fc2_bias": noise(key_list[18], (D,), 0.3, 1.75, (), jnp.float32),
        "gamma2": jnp.clip(jax.random.uniform(key_list[19], (D,), jnp.float32, 0.5, 1.5), 0.5, 1.5),
        "cotangent": noise(key_list[20], (IMAGES, ROWS, D), 1.0, 6.0, ((0, 32),)),
    }


epsilon = 1e-06
root_half = 0.7071067811865476
highest = lax.Precision.HIGHEST

@jax.custom_vjp
def low(v):
    return lax.optimization_barrier(v.astype(jnp.bfloat16)).astype(jnp.float32)

@jax.custom_vjp
def low_back(v):
    return v

def low_keep(v):
    return (low(v), None)

def low_pass(kept, grad):
    return (grad,)

def back_keep(v):
    return (v, None)

def back_low(kept, grad):
    return (low(grad),)
low.defvjp(low_keep, low_pass)
low_back.defvjp(back_keep, back_low)

def layer_norm(values, scale_vec, offset_vec):
    center = values - lax.optimization_barrier(jnp.mean(values, axis=-1, keepdims=True))
    spread = lax.optimization_barrier(jnp.mean(center * center, axis=-1, keepdims=True))
    return center * lax.rsqrt(spread + epsilon) * scale_vec + offset_vec

def gelu_exact(values):
    return 0.5 * values * (1.0 + jax.scipy.special.erf(values * root_half))

def forward(images, mask_token, ln1_gain, ln1_bias, w_qkv, qv_bias, rel_table, w_proj, proj_bias, gamma1, ln2_gain, ln2_bias, w_fc1, fc1_bias, w_fc2, fc2_bias, gamma2, chosen, valid_block, rel_index):
    count = images.shape[0]
    hidden = images * (1.0 - chosen) + chosen * mask_token
    normed = low(layer_norm(hidden, ln1_gain, ln1_bias))
    projected = jnp.einsum('gtd,dce->gtce', normed, w_qkv, precision=highest)
    queries = low_back(low(projected[:, :, 0] + qv_bias[0]))
    keyset = low_back(low(projected[:, :, 1]))
    valueset = low_back(low(projected[:, :, 2] + qv_bias[1]))
    shaped = (count, ROWS, HEADS, HEAD_DIM)
    scores = jnp.einsum('gqhe,gkhe->ghqk', queries.reshape(shaped), keyset.reshape(shaped), precision=highest) * HEAD_DIM ** (-0.5)
    bias_table = jnp.transpose(rel_table[rel_index], (2, 0, 1))
    scores = low_back(scores + bias_table[None])
    scores = jnp.where(valid_block[:, None, None, :] > 0, scores, -1e+30)
    weights = low(jax.nn.softmax(scores, axis=-1))
    attended = jnp.einsum('ghqk,gkhe->gqhe', weights, valueset.reshape(shaped), precision=highest)
    attended = low_back(low(attended.reshape(count, ROWS, D)))
    attn_branch = low_back(jnp.einsum('gtc,cd->gtd', attended, w_proj, precision=highest) + proj_bias)
    residual = hidden + gamma1 * attn_branch
    normed2 = low(layer_norm(residual, ln2_gain, ln2_bias))
    pre_gelu = low_back(jnp.einsum('gtd,df->gtf', normed2, w_fc1, precision=highest) + fc1_bias)
    active = low(gelu_exact(pre_gelu))
    branch = low_back(jnp.einsum('gtf,fd->gtd', active, w_fc2, precision=highest) + fc2_bias)
    return residual + gamma2 * branch

def reference(inputs, masked, key_valid, rel_index, mask_token, ln1_gain, ln1_bias, w_qkv, qv_bias, rel_table, w_proj, proj_bias, gamma1, ln2_gain, ln2_bias, w_fc1, fc1_bias, w_fc2, fc2_bias, gamma2, cotangent):
    params = (mask_token, ln1_gain, ln1_bias, w_qkv.astype(jnp.float32), qv_bias, rel_table, w_proj.astype(jnp.float32), proj_bias, gamma1, ln2_gain, ln2_bias, w_fc1.astype(jnp.float32), fc1_bias.astype(jnp.float32), w_fc2.astype(jnp.float32), fc2_bias, gamma2)
    blocks = IMAGES // IMG_DEV

    def regroup(array):
        return array.reshape((blocks, IMG_DEV) + array.shape[1:])

    def block_step(totals, block):
        images, chosen_int, valid_block, cot_block = block
        chosen = chosen_int.astype(jnp.float32)[..., None]

        def closed(image_values, *weight_list):
            return forward(image_values, *weight_list, chosen, valid_block, rel_index)
        result, pullback = jax.vjp(closed, images.astype(jnp.float32), *params)
        grads = pullback(cot_block.astype(jnp.float32))
        totals = tuple((total + grad for total, grad in zip(totals, grads[1:])))
        return (totals, (result.astype(jnp.bfloat16), grads[0]))
    start = tuple((jnp.zeros_like(param) for param in params))
    totals, (outputs, grad_input) = lax.scan(block_step, start, (regroup(inputs), regroup(masked), regroup(key_valid), regroup(cotangent)))
    g_mask, g_ln1g, g_ln1b, g_qkv, g_qvb, g_table, g_proj, g_projb, g_gamma1, g_ln2g, g_ln2b, g_fc1, g_fc1b, g_fc2, g_fc2b, g_gamma2 = totals
    return (outputs.reshape(inputs.shape), grad_input.reshape(inputs.shape), g_mask, g_ln1g, g_ln1b, g_qkv, g_qvb, g_table, g_proj, g_projb, g_gamma1, g_ln2g, g_ln2b, g_fc1, g_fc1b, g_fc2, g_fc2b, g_gamma2)
```

```python
import functools
import jax
import jax.numpy as jnp
from jax import lax
from jax.experimental import pallas as pl
from jax.experimental.pallas import tpu as pltpu
from jax.sharding import PartitionSpec as P

F32 = jnp.float32
BF16 = jnp.bfloat16
EPS = 1e-06
LANES = 128
V_MASK, V_G1, V_B1, V_PB, V_GA1, V_G2, V_B2, V_FB2, V_GA2, V_QB, V_VB = range(11)
S_GA2, S_FB2, S_LG2, S_LB2, S_GA1, S_PB = range(6)
T_MASK, T_LG1, T_LB1, T_QB, T_VB = range(5)


def dot(a, b):
    return jnp.dot(a, b, preferred_element_type=F32)


def dot_nt(a, b):
    return lax.dot_general(a, b, (((1,), (1,)), ((), ())), preferred_element_type=F32)


def dot_tn(a, b):
    return lax.dot_general(a, b, (((0,), (0,)), ((), ())), preferred_element_type=F32)


def norm_parts(v):
    c = v - jnp.mean(v, axis=-1, keepdims=True)
    r = lax.rsqrt(jnp.mean(c * c, axis=-1, keepdims=True) + EPS)
    return c * r, r


def norm_back(n, r, y, gain):
    yg = y * gain
    return r * (
        yg - jnp.mean(yg, axis=-1, keepdims=True) - n * jnp.mean(yg * n, axis=-1, keepdims=True)
    )


def low_half(shape):
    return lax.broadcasted_iota(jnp.int32, shape, 1) < (LANES // 2)


def attn_forward_kernel(
    x_ref, ch_ref, valid_ref, idx_ref, tab_ref, vec_ref, w_ref, wp_ref,
    normed_ref, q_ref, k_ref, v_ref, p_ref, att_ref, attn_ref, res_ref, n2_ref,
    bias_ref,
):
    images, rows, width = x_ref.shape
    rp = normed_ref.shape[0] // images
    keys = k_ref.shape[1]
    heads = bias_ref.shape[0]
    hw = width // heads
    scale = hw ** -0.5
    chunks = tab_ref.shape[1]

    def gather_head(h, carry):
        for half in range(keys // LANES):
            idx = idx_ref[:, half * LANES:(half + 1) * LANES]
            low = idx & (LANES - 1)
            high = idx >> 7
            acc = jnp.zeros(idx.shape, F32)
            for c in range(chunks):
                row = jnp.broadcast_to(tab_ref[h, c:c + 1, :], idx.shape)
                got = jnp.take_along_axis(row, low, axis=1)
                acc = jnp.where(high == c, got, acc)
            bias_ref[h, :, half * LANES:(half + 1) * LANES] = acc
        return carry

    lax.fori_loop(0, heads, gather_head, 0)

    normed_ref[...] = jnp.zeros_like(normed_ref)
    n2_ref[...] = jnp.zeros_like(n2_ref)
    res_ref[...] = jnp.zeros_like(res_ref)

    def hidden_of(i):
        ch = ch_ref[i]
        return x_ref[i].astype(F32) * (1.0 - ch) + ch * vec_ref[V_MASK:V_MASK + 1, :]

    def first_norm(i, carry):
        n, _ = norm_parts(hidden_of(i))
        out = n * vec_ref[V_G1:V_G1 + 1, :] + vec_ref[V_B1:V_B1 + 1, :]
        normed_ref[pl.ds(pl.multiple_of(i * rp, 16), rows), :] = out.astype(BF16)
        return carry

    lax.fori_loop(0, images, first_norm, 0)

    zeros_tail = jnp.zeros((images, keys - rp, width), BF16)
    k_ref[:, rp:, :] = zeros_tail
    v_ref[:, rp:, :] = zeros_tail
    for c, (dst, brow) in enumerate(((q_ref, V_QB), (k_ref, None), (v_ref, V_VB))):
        for nb in range(width // 256):
            cols = slice(nb * 256, (nb + 1) * 256)
            acc = dot(normed_ref[...], w_ref[c, :, cols])
            if brow is not None:
                acc = acc + vec_ref[brow:brow + 1, cols]
            acc = acc.astype(BF16)
            for i in range(images):
                dst[i, :rp, cols] = acc[i * rp:(i + 1) * rp]

    def attend(t, carry):
        i = t // (heads // 2)
        j = t % (heads // 2)
        lanes = pl.ds(pl.multiple_of(j * LANES, LANES), LANES)
        qp = q_ref[i, :, lanes]
        kp = k_ref[i, :, lanes]
        vp = v_ref[i, :, lanes]
        lo = low_half((rp, LANES))
        ok = valid_ref[i] > 0
        outs = []
        for s in range(2):
            qs = jnp.where(lo if s == 0 else jnp.logical_not(lo), qp, jnp.zeros_like(qp))
            sc = dot_nt(qs, kp) * scale + bias_ref[2 * j + s]
            sc = jnp.where(ok, sc, -1e30)
            e = jnp.exp(sc - jnp.max(sc, axis=-1, keepdims=True))
            prob = e * (1.0 / jnp.sum(e, axis=-1, keepdims=True))
            p_ref[i, 2 * j + s] = prob
            outs.append(dot(prob.astype(BF16), vp))
        att = jnp.where(lo, outs[0], outs[1]).astype(BF16)
        att_ref[pl.ds(pl.multiple_of(i * rp, 16), rp), lanes] = att
        return carry

    lax.fori_loop(0, images * (heads // 2), attend, 0)

    def finish(i, carry):
        at = pl.multiple_of(i * rp, 16)
        branch = dot(att_ref[pl.ds(at, rp), :], wp_ref[...]) + vec_ref[V_PB:V_PB + 1, :]
        attn_ref[pl.ds(at, rp), :] = branch
        res = hidden_of(i) + vec_ref[V_GA1:V_GA1 + 1, :] * branch[:rows]
        res_ref[pl.ds(at, rows), :] = res
        n, _ = norm_parts(res)
        out = n * vec_ref[V_G2:V_G2 + 1, :] + vec_ref[V_B2:V_B2 + 1, :]
        n2_ref[pl.ds(at, rows), :] = out.astype(BF16)
        return carry

    lax.fori_loop(0, images, finish, 0)


def vmem(n):
    return [pl.BlockSpec(memory_space=pltpu.VMEM)] * n


def attn_forward(x, ch, valid, idx, tab, vec, w, wp, heads):
    images, rows, width = x.shape
    rp, keys = idx.shape
    flat = images * rp
    sd = jax.ShapeDtypeStruct
    return pl.pallas_call(
        attn_forward_kernel,
        name="attn_forward",
        out_shape=(
            sd((flat, width), BF16), sd((images, rp, width), BF16), sd((images, keys, width), BF16),
            sd((images, keys, width), BF16), sd((images, heads, rp, keys), F32),
            sd((flat, width), BF16), sd((flat, width), F32), sd((flat, width), F32),
            sd((flat, width), BF16),
        ),
        in_specs=vmem(8), out_specs=vmem(9),
        scratch_shapes=[pltpu.VMEM((heads, rp, keys), F32)],
        compiler_params=pltpu.CompilerParams(vmem_limit_bytes=60 * 2**20),
    )(x, ch, valid, idx, tab, vec, w, wp)


def mlp_kernel(
    n2_ref, res_ref, attn_ref, cot_ref, vec_ref, b1_ref, w1_ref, w2_ref,
    g1_ref, g2_ref, gb1_ref, out_ref, dres_ref, dproj_ref, small_ref,
    db_ref, act_ref, dpre_ref, branch_ref, dn_ref,
):
    images, rows, width = cot_ref.shape
    flat = n2_ref.shape[0]
    rp = flat // images
    step = pl.program_id(0)
    steps = pl.num_programs(0)

    @pl.when(step == 0)
    def _():
        db_ref[...] = jnp.zeros_like(db_ref)
        branch_ref[...] = jnp.zeros_like(branch_ref)
        dn_ref[...] = jnp.zeros_like(dn_ref)

        def fill(i, carry):
            up = cot_ref[i].astype(F32) * vec_ref[V_GA2:V_GA2 + 1, :]
            db_ref[pl.ds(pl.multiple_of(i * rp, 16), rows), :] = up.astype(BF16)
            return carry

        lax.fori_loop(0, images, fill, 0)

    def tile(i, gb1):
        at = pl.ds(pl.multiple_of(i * rp, 16), rp)
        pre = dot_nt(n2_ref[at, :], w1_ref[...]) + b1_ref[...]
        cdf = 0.5 * (1.0 + lax.erf(pre * 0.7071067811865476))
        slope = cdf + pre * (0.3989422804014327 * jnp.exp(-0.5 * pre * pre))
        act = (pre * cdf).astype(BF16)
        act_ref[at, :] = act
        dpre = (dot_nt(db_ref[at, :], w2_ref[...]) * slope).astype(BF16)
        dpre_ref[at, :] = dpre
        branch_ref[at, :] += dot(act, w2_ref[...])
        dn_ref[at, :] += dot(dpre, w1_ref[...])
        return gb1 + jnp.sum(dpre.astype(F32), axis=0, keepdims=True)

    gb1_ref[...] = lax.fori_loop(0, images, tile, jnp.zeros(gb1_ref.shape, F32))
    g2_ref[...] = dot_tn(act_ref[...], db_ref[...]).astype(BF16)
    g1_ref[...] = dot_tn(dpre_ref[...], n2_ref[...]).astype(BF16)

    @pl.when(step == steps - 1)
    def _():
        dproj_ref[...] = jnp.zeros_like(dproj_ref)
        dres_ref[...] = jnp.zeros_like(dres_ref)
        small_ref[...] = jnp.zeros_like(small_ref)

        def add(row, value):
            small_ref[row:row + 1, :] += jnp.sum(value, axis=0, keepdims=True)

        def finish(i, carry):
            at = pl.multiple_of(i * rp, 16)
            here = pl.ds(at, rows)
            up = cot_ref[i].astype(F32)
            branch = branch_ref[here, :] + vec_ref[V_FB2:V_FB2 + 1, :]
            res = res_ref[here, :]
            out_ref[i] = (res + vec_ref[V_GA2:V_GA2 + 1, :] * branch).astype(BF16)
            add(S_GA2, up * branch)
            add(S_FB2, (up * vec_ref[V_GA2:V_GA2 + 1, :]).astype(BF16).astype(F32))
            n, r = norm_parts(res)
            dn = dn_ref[here, :]
            add(S_LG2, dn * n)
            add(S_LB2, dn)
            dres = up + norm_back(n, r, dn, vec_ref[V_G2:V_G2 + 1, :])
            dres_ref[here, :] = dres
            add(S_GA1, dres * attn_ref[here, :])
            dproj = (dres * vec_ref[V_GA1:V_GA1 + 1, :]).astype(BF16)
            dproj_ref[here, :] = dproj
            add(S_PB, dproj.astype(F32))
            return carry

        lax.fori_loop(0, images, finish, 0)


def mlp(n2, res, attn, cot, vec, b1, w1, w2, block):
    images, rows, width = cot.shape
    flat = n2.shape[0]
    ff = w1.shape[0]
    sd = jax.ShapeDtypeStruct
    whole = lambda a: pl.BlockSpec(a.shape, lambda s: (0,) * a.ndim, pipeline_mode=pl.Buffered(1))
    outs = (
        sd((ff, width), BF16), sd((ff, width), BF16), sd((1, ff), F32), sd(cot.shape, BF16),
        sd((flat, width), F32), sd((flat, width), BF16), sd((8, width), F32),
    )
    part = pl.BlockSpec((block, width), lambda s: (s, 0))
    return pl.pallas_call(
        mlp_kernel,
        name="mlp",
        grid=(ff // block,),
        out_shape=outs,
        in_specs=[whole(n2), whole(res), whole(attn), whole(cot), whole(vec),
                  pl.BlockSpec((1, block), lambda s: (0, s)), part, part],
        out_specs=[part, part, pl.BlockSpec((1, block), lambda s: (0, s)), whole(outs[3]),
                   whole(outs[4]), whole(outs[5]), whole(outs[6])],
        scratch_shapes=[
            pltpu.VMEM((flat, width), BF16), pltpu.VMEM((flat, block), BF16),
            pltpu.VMEM((flat, block), BF16), pltpu.VMEM((flat, width), F32),
            pltpu.VMEM((flat, width), F32),
        ],
        compiler_params=pltpu.CompilerParams(vmem_limit_bytes=60 * 2**20),
    )(n2, res, attn, cot, vec, b1, w1, w2)


def attn_backward_kernel(
    x_ref, ch_ref, idx_ref, vec_ref, w_ref, wp_ref, normed_ref, q_ref, k_ref, v_ref, p_ref,
    att_ref, dres_ref, dproj_ref,
    gx_ref, gw_ref, gt_ref, small_ref,
    dat_ref, dqkv_ref, ds_ref, nt_ref, dpt_ref,
):
    images, rows, width = x_ref.shape
    flat = normed_ref.shape[0]
    rp = flat // images
    keys = k_ref.shape[1]
    heads = ds_ref.shape[0]
    scale = (width // heads) ** -0.5
    j = pl.program_id(0)
    pairs = pl.num_programs(0)

    @pl.when(j == 0)
    def _():
        for i in range(images):
            at = slice(i * rp, (i + 1) * rp)
            dat_ref[at, :] = dot_nt(dproj_ref[at, :], wp_ref[...]).astype(BF16)
        nt_ref[...] = normed_ref[...].T
        dpt_ref[...] = dproj_ref[...].T
        small_ref[...] = jnp.zeros_like(small_ref)

    lanes = pl.ds(pl.multiple_of(j * LANES, LANES), LANES)
    ds_ref[2 * j] = jnp.zeros((rp, keys), F32)
    ds_ref[2 * j + 1] = jnp.zeros((rp, keys), F32)

    def image(i, carry):
        at = pl.ds(pl.multiple_of(i * rp, 16), rp)
        qp = q_ref[i, :, lanes]
        kp = k_ref[i, :, lanes]
        vp = v_ref[i, :, lanes]
        da = dat_ref[at, lanes]
        lo = low_half((rp, LANES))
        dv, dq, dk = [], [], []
        for s in range(2):
            das = jnp.where(lo if s == 0 else jnp.logical_not(lo), da, jnp.zeros_like(da))
            prob = p_ref[i, s]
            dp = dot_nt(das, vp)
            dsc = prob * (dp - jnp.sum(prob * dp, axis=-1, keepdims=True))
            dsb = dsc.astype(BF16)
            ds_ref[2 * j + s] += dsb.astype(F32)
            dv.append(dot_tn(prob.astype(BF16), da))
            dq.append(dot(dsb, kp))
            dk.append(dot_tn(dsb, qp))
        lok = low_half((keys, LANES))
        dqkv_ref[0, at, lanes] = (jnp.where(lo, dq[0], dq[1]) * scale).astype(BF16)
        dqkv_ref[1, at, lanes] = (jnp.where(lok, dk[0], dk[1]) * scale)[:rp].astype(BF16)
        dqkv_ref[2, at, lanes] = jnp.where(lok, dv[0], dv[1])[:rp].astype(BF16)
        return carry

    lax.fori_loop(0, images, image, 0)
    for c in range(3):
        gw_ref[0, c] = dot(nt_ref[...], dqkv_ref[c, :, lanes]).astype(BF16)
    gw_ref[0, 3] = dot(dpt_ref[...], att_ref[:, lanes]).astype(BF16)

    @pl.when(j == pairs - 1)
    def _():
        def column(row, c):
            def body(i, acc):
                part = dqkv_ref[c, pl.ds(pl.multiple_of(i * rp, 16), rp), :].astype(F32)
                return acc + jnp.sum(part, axis=0, keepdims=True)
            small_ref[row:row + 1, :] = lax.fori_loop(0, images, body, jnp.zeros((1, width), F32))

        column(T_QB, 0)
        column(T_VB, 2)

        def finish(i, carry):
            at = pl.multiple_of(i * rp, 16)
            here = pl.ds(at, rp)
            dn = dot_nt(dqkv_ref[0, here, :], w_ref[0])
            dn += dot_nt(dqkv_ref[1, here, :], w_ref[1])
            dn += dot_nt(dqkv_ref[2, here, :], w_ref[2])
            dn = dn[:rows]
            ch = ch_ref[i]
            hidden = x_ref[i].astype(F32) * (1.0 - ch) + ch * vec_ref[V_MASK:V_MASK + 1, :]
            n, r = norm_parts(hidden)
            dh = dres_ref[pl.ds(at, rows), :] + norm_back(n, r, dn, vec_ref[V_G1:V_G1 + 1, :])
            gx_ref[i] = dh * (1.0 - ch)
            for row, value in ((T_MASK, dh * ch), (T_LG1, dn * n), (T_LB1, dn)):
                small_ref[row:row + 1, :] += jnp.sum(value, axis=0, keepdims=True)
            return carry

        lax.fori_loop(0, images, finish, 0)

        a_iota = lax.broadcasted_iota(jnp.int32, (8, keys), 0)
        b_iota = lax.broadcasted_iota(jnp.int32, (LANES, keys), 0)

        def scatter(t, acc):
            idx = jnp.broadcast_to(idx_ref[pl.ds(t, 1), :], (8, keys))
            pick = (idx >> 7) == a_iota
            low = jnp.broadcast_to(idx_ref[pl.ds(t, 1), :] & (LANES - 1), (LANES, keys))
            one = (low == b_iota).astype(F32).astype(BF16)
            tiles = []
            for h in range(heads):
                row = jnp.broadcast_to(ds_ref[h, pl.ds(t, 1), :], (8, keys))
                tiles.append(jnp.where(pick, row, 0.0))
            left = jnp.concatenate(tiles, axis=0)
            high = left.astype(BF16)
            rest = (left - high.astype(F32)).astype(BF16)
            return acc + dot_nt(high, one) + dot_nt(rest, one)

        gt_ref[...] = lax.fori_loop(0, rows, scatter, jnp.zeros((heads * 8, LANES), F32))


def attn_backward(x, ch, idx, vec, w, wp, normed, q, k, v, p, att, dres, dproj, heads):
    images, rows, width = x.shape
    rp, keys = idx.shape
    flat = images * rp
    sd = jax.ShapeDtypeStruct
    whole = lambda a: pl.BlockSpec(a.shape, lambda s: (0,) * a.ndim, pipeline_mode=pl.Buffered(1))
    outs = (
        sd((images, rows, width), F32), sd((heads // 2, 4, width, LANES), BF16),
        sd((heads * 8, LANES), F32), sd((8, width), F32),
    )
    args = (x, ch, idx, vec, w, wp, normed, q, k, v)
    return pl.pallas_call(
        attn_backward_kernel,
        name="attn_backward",
        grid=(heads // 2,),
        out_shape=outs,
        in_specs=[whole(a) for a in args]
        + [pl.BlockSpec((images, 2, rp, keys), lambda s: (0, s, 0, 0)), whole(att), whole(dres), whole(dproj)],
        out_specs=[whole(outs[0]), pl.BlockSpec((1, 4, width, LANES), lambda s: (s, 0, 0, 0)),
                   whole(outs[2]), whole(outs[3])],
        scratch_shapes=[
            pltpu.VMEM((flat, width), BF16), pltpu.VMEM((3, flat, width), BF16),
            pltpu.VMEM((heads, rp, keys), F32), pltpu.VMEM((width, flat), BF16),
            pltpu.VMEM((width, flat), BF16),
        ],
        compiler_params=pltpu.CompilerParams(vmem_limit_bytes=60 * 2**20),
    )(*args, p, att, dres, dproj)


MESHID = pl.DeviceIdType.MESH


def here():
    dp = lax.axis_index("dp")
    head = lax.axis_index("head")
    return dp // 4, (dp // 2) % 2, dp % 2, head


def at_dp(z, y, x):
    return {"dp": (z * 2 + y) * 2 + x}


def partners(depth):
    z, y, x, head = here()
    found = [at_dp(z, y, 1 - x), at_dp(z, 1 - y, x), {"head": 1 - head}]
    for k in range(1, depth):
        found.append(at_dp((z + k) % depth, y, x))
    return found


def greet(depth):
    barrier = pltpu.get_barrier_semaphore()
    found = partners(depth)
    for dev in found:
        pl.semaphore_signal(barrier, inc=1, device_id=dev, device_id_type=MESHID)
    pl.semaphore_wait(barrier, len(found))


class Wire:
    def __init__(self, send, recv):
        self.send, self.recv, self.next, self.open = send, recv, 0, []

    def slot(self):
        self.next += 1
        return self.next - 1

    def start(self, i, src, dst, dev):
        copy = pltpu.make_async_remote_copy(
            src_ref=src, dst_ref=dst, send_sem=self.send.at[i], recv_sem=self.recv.at[i],
            device_id=dev, device_id_type=MESHID,
        )
        copy.start()
        self.open.append(copy)

    def arrived(self, i, ref, dev):
        pltpu.make_async_remote_copy(
            src_ref=ref, dst_ref=ref, send_sem=self.send.at[i], recv_sem=self.recv.at[i],
            device_id=dev, device_id_type=MESHID,
        ).wait_recv()

    def sent(self):
        for copy in self.open:
            copy.wait_send()
        self.open = []


def hops(p, y, x):
    ey, ex = (1 - y, x), (y, 1 - x)
    return (ey, ex) if p == 0 else (ex, ey)


def gather_stages(wire, depth, own, slot, column=None):
    z, y, x, head = here()
    ids = {}
    for p in range(2):
        for k in range(depth):
            for kind in "zabc":
                ids[p, kind, k] = wire.slot()
        if column is not None:
            for kind in range(4):
                ids[p, "s", kind] = wire.slot()
    zk = lambda k: (z + depth - k) % depth

    def start_square(p, k, src):
        (ay, ax), (by, bx) = hops(p, y, x)
        src = slot(p, zk(k), y, x) if src is None else src
        wire.start(ids[p, "a", k], src, slot(p, zk(k), y, x), at_dp(z, ay, ax))
        wire.start(ids[p, "b", k], src, slot(p, zk(k), y, x), at_dp(z, by, bx))

    def begin():
        for k in range(1, depth):
            for p in range(2):
                wire.start(ids[p, "z", k], own(p), slot(p, z, y, x), at_dp((z + k) % depth, y, x))
        for p in range(2):
            start_square(p, 0, own(p))

    def from_column(k):
        def run():
            for p in range(2):
                wire.arrived(ids[p, "z", k], slot(p, zk(k), y, x), at_dp(zk(k), y, x))
                start_square(p, k, None)
        return run

    def from_first(k):
        def run():
            for p in range(2):
                (ay, ax), (by, bx) = hops(p, y, x)
                wire.arrived(ids[p, "a", k], slot(p, zk(k), ay, ax), at_dp(z, ay, ax))
                wire.start(ids[p, "c", k], slot(p, zk(k), ay, ax), slot(p, zk(k), ay, ax), at_dp(z, by, bx))
        return run

    def from_second(kind):
        def run():
            for p in range(2):
                (ay, ax), (by, bx) = hops(p, y, x)
                cy, cx = (by, bx) if kind == "b" else (1 - y, 1 - x)
                for k in range(depth):
                    wire.arrived(ids[p, kind, k], slot(p, zk(k), cy, cx), at_dp(z, by, bx))
        return run

    def across(which):
        def run():
            for p in range(2):
                (ay, ax), (by, bx) = hops(p, y, x)
                cy, cx = ((y, x), (ay, ax), (by, bx), (1 - y, 1 - x))[which]
                block = column(p, cy, cx, head)
                wire.start(ids[p, "s", which], block, block, {"head": 1 - head})
        return run

    def crossed():
        for which in range(4):
            for p in range(2):
                (ay, ax), (by, bx) = hops(p, y, x)
                cy, cx = ((y, x), (ay, ax), (by, bx), (1 - y, 1 - x))[which]
                wire.arrived(ids[p, "s", which], column(p, cy, cx, 1 - head), {"head": 1 - head})

    stages = [begin]
    stages += [from_column(k) for k in range(1, depth)]
    if column is not None:
        stages.append(across(0))
    stages += [from_first(k) for k in range(depth)]
    if column is not None:
        stages.append(across(1))
    stages.append(from_second("b"))
    if column is not None:
        stages.append(across(2))
    stages.append(from_second("c"))
    if column is not None:
        stages.append(across(3))
        stages.append(crossed)
    return stages


def add_into(dst, src):
    total = dst[...].astype(F32) + src[...].astype(F32)
    dst[...] = total.astype(dst.dtype)


class ScatterSum:
    def __init__(self, wire, depth, theirs, pair_in, mine, square_in, line_in, column_in, store):
        self.__dict__.update(locals())
        self.ids = {}
        for p in range(2):
            for kind in ["h", "a", "b"] + list(range(1, depth)):
                self.ids[p, kind] = wire.slot()

    def pair(self):
        head = here()[3]
        for p in range(2):
            self.wire.start(self.ids[p, "h"], self.theirs(p), self.pair_in(p), {"head": 1 - head})

    def first(self):
        z, y, x, head = here()
        for p in range(2):
            self.wire.arrived(self.ids[p, "h"], self.pair_in(p), {"head": 1 - head})
            add_into(self.mine(p, None, None, None), self.pair_in(p))
            if p == 0:
                self.wire.start(self.ids[p, "a"], self.mine(p, None, None, 1 - x), self.square_in(p), at_dp(z, y, 1 - x))
            else:
                self.wire.start(self.ids[p, "a"], self.mine(p, None, 1 - y, None), self.square_in(p), at_dp(z, 1 - y, x))

    def second(self):
        z, y, x, head = here()
        for p in range(2):
            if p == 0:
                self.wire.arrived(self.ids[p, "a"], self.square_in(p), at_dp(z, y, 1 - x))
                add_into(self.mine(p, None, None, x), self.square_in(p))
                self.wire.start(self.ids[p, "b"], self.mine(p, None, 1 - y, x), self.line_in(p), at_dp(z, 1 - y, x))
            else:
                self.wire.arrived(self.ids[p, "a"], self.square_in(p), at_dp(z, 1 - y, x))
                add_into(self.mine(p, None, y, None), self.square_in(p))
                self.wire.start(self.ids[p, "b"], self.mine(p, None, y, 1 - x), self.line_in(p), at_dp(z, y, 1 - x))

    def third(self):
        z, y, x, head = here()
        for p in range(2):
            self.wire.arrived(self.ids[p, "b"], self.line_in(p), at_dp(z, 1 - y, x) if p == 0 else at_dp(z, y, 1 - x))
            add_into(self.mine(p, None, y, x), self.line_in(p))
            for k in range(1, self.depth):
                to = (z + k) % self.depth
                self.wire.start(self.ids[p, k], self.mine(p, to, y, x), self.column_in(p, k), at_dp(to, y, x))

    def last(self):
        z, y, x, head = here()
        for p in range(2):
            total = self.mine(p, z, y, x)[...].astype(F32)
            for k in range(1, self.depth):
                self.wire.arrived(self.ids[p, k], self.column_in(p, k), at_dp((z + self.depth - k) % self.depth, y, x))
                total = total + self.column_in(p, k)[...].astype(F32)
            self.store(p, total)


class SmallSum:
    def __init__(self, wire, depth, bufs, line):
        self.wire, self.depth, self.bufs, self.line = wire, depth, bufs, line
        self.ids = [wire.slot() for _ in range(3 + depth)]

    def devices(self):
        z, y, x, head = here()
        return [{"head": 1 - head}, at_dp(z, y, 1 - x), at_dp(z, 1 - y, x)]

    def send(self, n):
        self.wire.start(self.ids[n], self.bufs.at[2 * n], self.bufs.at[2 * n + 1], self.devices()[n])

    def take(self, n):
        self.wire.arrived(self.ids[n], self.bufs.at[2 * n + 1], self.devices()[n])
        self.bufs[2 * n + 2] = self.bufs[2 * n] + self.bufs[2 * n + 1]

    def stages(self):
        def begin():
            self.send(0)

        def middle(n):
            def run():
                self.take(n - 1)
                self.send(n)
            return run

        def column():
            z, y, x, head = here()
            self.take(2)
            self.line[z] = self.bufs[6]
            for k in range(1, self.depth):
                self.wire.start(self.ids[2 + k], self.bufs.at[6], self.line.at[z], at_dp((z + k) % self.depth, y, x))

        return [begin, middle(1), middle(2), column]

    def result(self):
        z, y, x, head = here()
        for k in range(1, self.depth):
            back = (z + self.depth - k) % self.depth
            self.wire.arrived(self.ids[2 + k], self.line.at[back], at_dp(back, y, x))
        total = self.line[0]
        for n in range(1, self.depth):
            total = total + self.line[n]
        return total


def ag_kernel(own_ref, bias_ref, b1_ref, b2_ref, bsum_ref, bufs, line, send, recv, lsem):
    depth = b1_ref.shape[0]
    z, y, x, head = here()
    full = (b1_ref, b2_ref)
    own = lambda p: own_ref.at[p]
    slot = lambda p, zz, yy, xx: full[p].at[zz, yy, xx, head]
    column = lambda p, yy, xx, hd: full[p].at[:, yy, xx, hd]
    greet(depth)
    local = [pltpu.make_async_copy(own(p), slot(p, z, y, x), lsem.at[p]) for p in range(2)]
    for c in local:
        c.start()
    wire = Wire(send, recv)
    bufs[0] = bias_ref[...]
    small = SmallSum(wire, depth, bufs, line)
    stages = gather_stages(wire, depth, own, slot, column)
    extra = small.stages()
    for n, s in enumerate(stages):
        if n == 1:
            for c in local:
                c.wait()
        s()
        if n < len(extra):
            extra[n]()
    bsum_ref[...] = small.result()
    wire.sent()


def ag(own, bias, depth, heads):
    shape = jax.ShapeDtypeStruct((depth, 2, 2, heads) + own.shape[1:], own.dtype)
    any_ = pl.BlockSpec(memory_space=pl.ANY)
    n = 2 * (4 * depth + 4) + 3 + depth
    return pl.pallas_call(
        ag_kernel, name="gather_ff", out_shape=(shape, shape, jax.ShapeDtypeStruct(bias.shape, F32)),
        in_specs=[any_] + vmem(1), out_specs=[any_, any_] + vmem(1),
        scratch_shapes=[pltpu.VMEM((7,) + bias.shape, F32), pltpu.VMEM((depth,) + bias.shape, F32), pltpu.SemaphoreType.DMA((n,)), pltpu.SemaphoreType.DMA((n,)), pltpu.SemaphoreType.DMA((2,))],
        compiler_params=pltpu.CompilerParams(collective_id=1, has_side_effects=True),
    )(own, bias)


def rs_kernel(chunk, g1_ref, g2_ref, o_ref, mine, pair_in, square_in, line_in, column_in, send, recv, lsem):
    depth = g1_ref.shape[0]
    z, y, x, head = here()
    gs = (g1_ref, g2_ref)
    greet(depth)
    local = [pltpu.make_async_copy(gs[p].at[:, :, :, head], mine.at[p], lsem.at[p]) for p in range(2)]
    for c in local:
        c.start()
    wire = Wire(send, recv)
    every = lambda v: slice(None) if v is None else v
    sums = []
    for r in range(mine.shape[4] // chunk):
        rows = pl.ds(r * chunk, chunk)

        def store(p, total, rows=rows):
            o_ref[p, rows, :] = total
        sums.append(ScatterSum(
            wire, depth,
            theirs=lambda p, rows=rows: gs[p].at[:, :, :, 1 - head, rows],
            pair_in=lambda p, rows=rows: pair_in.at[p, :, :, :, rows],
            mine=lambda p, zz, yy, xx, rows=rows: mine.at[p, every(zz), every(yy), every(xx), rows],
            square_in=lambda p, r=r: square_in.at[p, r],
            line_in=lambda p, r=r: line_in.at[p, r],
            column_in=lambda p, k, r=r: column_in.at[p, r, k - 1],
            store=store,
        ))
    for s in sums:
        s.pair()
    for c in local:
        c.wait()
    for name in ("first", "second", "third", "last"):
        for s in sums:
            getattr(s, name)()
    wire.sent()


def rs(g1, g2, chunk):
    depth, heads, rows, width = g1.shape[0], g1.shape[3], g1.shape[4], g1.shape[5]
    pieces = rows // chunk
    any_ = pl.BlockSpec(memory_space=pl.ANY)
    n = 2 * pieces * (2 + depth)
    return pl.pallas_call(
        functools.partial(rs_kernel, chunk), name="scatter_ff",
        out_shape=jax.ShapeDtypeStruct((2, rows, width), F32),
        in_specs=[any_, any_], out_specs=pl.BlockSpec(memory_space=pltpu.VMEM),
        scratch_shapes=[
            pltpu.VMEM((2, depth, 2, 2, rows, width), BF16), pltpu.VMEM((2, depth, 2, 2, rows, width), BF16),
            pltpu.VMEM((2, pieces, depth, 2, chunk, width), BF16), pltpu.VMEM((2, pieces, depth, chunk, width), BF16),
            pltpu.VMEM((2, pieces, depth - 1, chunk, width), BF16),
            pltpu.SemaphoreType.DMA((n,)), pltpu.SemaphoreType.DMA((n,)), pltpu.SemaphoreType.DMA((2,))],
        compiler_params=pltpu.CompilerParams(collective_id=2, has_side_effects=True, vmem_limit_bytes=50 * 2**20),
    )(g1, g2)


def ar_kernel(g_ref, small_ref, full_ref, sum_ref, mine, pair_in, square_in, line_in, column_in, bufs, line, send, recv, lsem):
    pieces, depth = mine.shape[0], mine.shape[3]
    z, y, x, head = here()
    greet(depth)
    local = [pltpu.make_async_copy(g_ref.at[head, m], mine.at[m], lsem.at[m]) for m in range(pieces)]
    for c in local:
        c.start()
    wire = Wire(send, recv)
    every = lambda v: slice(None) if v is None else v
    bufs[0] = small_ref[...]
    small = SmallSum(wire, depth, bufs, line)
    sums = []
    for m in range(pieces):
        def store(p, total, m=m):
            full_ref[m, p, :, z, y, x] = total.astype(BF16)
        sums.append(ScatterSum(
            wire, depth,
            theirs=lambda p, m=m: g_ref.at[1 - head, m, p],
            pair_in=lambda p, m=m: pair_in.at[m, p],
            mine=lambda p, zz, yy, xx, m=m: mine.at[m, p, :, every(zz), every(yy), every(xx)],
            square_in=lambda p, m=m: square_in.at[p, m],
            line_in=lambda p, m=m: line_in.at[p, m],
            column_in=lambda p, k, m=m: column_in.at[p, m, k - 1],
            store=store,
        ))
    extra = small.stages()
    for s in sums:
        s.pair()
    for c in local:
        c.wait()
    for n, name in enumerate(("first", "second", "third", "last")):
        extra[n]()
        for s in sums:
            getattr(s, name)()
    stages = gather_stages(
        wire, depth,
        own=lambda p: full_ref.at[:, p, :, z, y, x],
        slot=lambda p, zz, yy, xx: full_ref.at[:, p, :, zz, yy, xx],
    )
    for s in stages:
        s()
    sum_ref[...] = small.result()
    wire.sent()


def ar(g, small, depth):
    pieces, (rows, lanes) = g.shape[1], g.shape[-2:]
    any_ = pl.BlockSpec(memory_space=pl.ANY)
    n = 2 * pieces * (2 + depth) + 2 * 4 * depth + 3 + depth
    one = (pieces, 2, 2, depth, 2, 2, rows, lanes)
    return pl.pallas_call(
        ar_kernel, name="sum_weights",
        out_shape=(jax.ShapeDtypeStruct(one, BF16), jax.ShapeDtypeStruct(small.shape, F32)),
        in_specs=[any_] + vmem(1), out_specs=vmem(2),
        scratch_shapes=[
            pltpu.VMEM(one, BF16), pltpu.VMEM(one, BF16),
            pltpu.VMEM((2, pieces, 2, depth, 2, rows, lanes), BF16), pltpu.VMEM((2, pieces, 2, depth, rows, lanes), BF16),
            pltpu.VMEM((2, pieces, depth - 1, 2, rows, lanes), BF16),
            pltpu.VMEM((7,) + small.shape, F32), pltpu.VMEM((depth,) + small.shape, F32),
            pltpu.SemaphoreType.DMA((n,)), pltpu.SemaphoreType.DMA((n,)), pltpu.SemaphoreType.DMA((pieces,))],
        compiler_params=pltpu.CompilerParams(collective_id=3, has_side_effects=True, vmem_limit_bytes=50 * 2**20),
    )(g, small)


def pack(rows, count):
    width = rows[0].shape[0]
    return jnp.concatenate([jnp.stack(rows), jnp.zeros((count - len(rows), width), F32)])


def shards(
    inputs, masked, key_valid, rel_index, mask_token, ln1_gain, ln1_bias, w_qkv, qv_bias, rel_table,
    w_proj, proj_bias, gamma1, ln2_gain, ln2_bias, w_fc1, fc1_bias, w_fc2, fc2_bias, gamma2, cotangent,
):
    images, rows, width = inputs.shape
    dp, hn = lax.axis_size("dp"), lax.axis_size("head")
    me, head = lax.axis_index("dp"), lax.axis_index("head")
    depth = dp // 4
    share = w_fc2.shape[0]
    ff = share * dp * hn
    entries, heads = rel_table.shape[0], rel_table.shape[1] * hn
    rp, keys = -(-rows // 16) * 16, -(-rows // LANES) * LANES
    direct = hn == 2 and dp == 16 and share % 32 == 0 and width % (16 * dp) == 0

    w = lax.all_gather(jnp.transpose(w_qkv, (1, 0, 2)), "head", axis=2, tiled=True)
    wp = lax.all_gather(w_proj, "head", axis=0, tiled=True)
    tab_rows = -(-entries // LANES)
    tab = jnp.pad(rel_table.T, ((0, 0), (0, tab_rows * LANES - entries)))
    mixed = jnp.concatenate([tab.reshape(-1), qv_bias.reshape(-1)])
    mixed = lax.all_gather(mixed, "head", axis=0)
    cut = tab.size
    tab = mixed[:, :cut].reshape(heads, tab_rows, LANES)
    qvb = jnp.transpose(mixed[:, cut:].reshape(hn, 2, width // hn), (1, 0, 2)).reshape(2, width)
    vec = pack([mask_token, ln1_gain, ln1_bias, proj_bias, gamma1, ln2_gain, ln2_bias, fc2_bias, gamma2, qvb[0], qvb[1]], 16)
    ch = masked.astype(F32)[..., None]
    valid = lax.dynamic_slice_in_dim(key_valid, head * images, images, 0)
    valid = jnp.pad(valid, ((0, 0), (0, keys - rows)))[:, None, :]
    idx = jnp.pad(rel_index, ((0, rp - rows), (0, keys - rows)))

    if direct:
        own = jnp.stack([w_fc1.T, w_fc2])
        spot = jnp.zeros((ff,), F32)
        spot = lax.dynamic_update_slice(spot, fc1_bias.astype(F32), ((me * hn + head) * share,))
        w1, w2, b1 = ag(own, spot.reshape(8, ff // 8), depth, hn)
        w1, w2, b1 = w1.reshape(ff, width), w2.reshape(ff, width), b1.reshape(1, ff)
    else:
        w1 = lax.all_gather(w_fc1.T, ("dp", "head"), axis=0, tiled=True)
        w2 = lax.all_gather(w_fc2, ("dp", "head"), axis=0, tiled=True)
        b1 = lax.all_gather(fc1_bias, ("dp", "head"), axis=0, tiled=True).astype(F32)[None]

    normed, q, k, v, p, att, attn, res, n2 = attn_forward(inputs, ch, valid, idx, tab, vec, w, wp, heads)
    block = ff // 4
    g1, g2, gb1, out, dres, dproj, small2 = mlp(n2, res, attn, cotangent, vec, b1, w1, w2, block)
    gx, gw, gt, small1 = attn_backward(inputs, ch, idx, vec, w, wp, normed, q, k, v, p, att, dres, dproj, heads)

    small = jnp.concatenate([small1, small2, gt.reshape(-1, width), gb1.reshape(-1, width)])
    if direct:
        cut_ff = (depth, 2, 2, hn, share, width)
        gff = rs(g1.reshape(cut_ff), g2.reshape(cut_ff), 32)
        g_fc1, g_fc2 = gff[0], gff[1]
        per = heads // 2 // hn
        full, small = ar(gw.reshape(hn, per, 2, 2, depth, 2, 2, width // dp, LANES), small, depth)
        full = full.reshape(per, 4, width, LANES).astype(F32)
    else:
        g_fc1 = lax.psum_scatter(g1.astype(F32), ("dp", "head"), scatter_dimension=0, tiled=True)
        g_fc2 = lax.psum_scatter(g2.astype(F32), ("dp", "head"), scatter_dimension=0, tiled=True)
        full = lax.psum(lax.psum_scatter(gw.astype(F32), "head", scatter_dimension=0, tiled=True), "dp")
        small = lax.psum(small, ("dp", "head"))
    g_qkv = jnp.transpose(full[:, :3], (2, 1, 0, 3)).reshape(width, 3, -1)
    g_proj = jnp.transpose(full[:, 3], (0, 2, 1)).reshape(-1, width)
    s1, s2 = small[:8], small[8:16]
    tables = small[16:16 + gt.size // width].reshape(hn, heads // hn, -1)
    g_table = lax.dynamic_index_in_dim(tables, head, 0, keepdims=False)[:, :entries].T
    g_b1 = lax.dynamic_slice_in_dim(small[16 + gt.size // width:].reshape(-1), (me * hn + head) * share, share)
    g_qvb = lax.dynamic_slice_in_dim(s1[T_QB:T_VB + 1], head * (width // hn), width // hn, 1)
    return (
        out, gx, s1[T_MASK], s1[T_LG1], s1[T_LB1], g_qkv, g_qvb, g_table, g_proj, s2[S_PB], s2[S_GA1],
        s2[S_LG2], s2[S_LB2], g_fc1.T, g_b1, g_fc2, s2[S_FB2], s2[S_GA2],
    )


def solution(mesh):
    in_specs = (
        P(("dp", "head"), None, None),
        P(("dp", "head"), None),
        P("dp", None),
        P(),
        P(),
        P(),
        P(),
        P(None, None, "head"),
        P(None, "head"),
        P(None, "head"),
        P("head", None),
        P(),
        P(),
        P(),
        P(),
        P(None, ("dp", "head")),
        P(("dp", "head")),
        P(("dp", "head"), None),
        P(),
        P(),
        P(("dp", "head"), None, None),
    )
    out_specs = (
        P(("dp", "head"), None, None),
        P(("dp", "head"), None, None),
        P(),
        P(),
        P(),
        P(None, None, "head"),
        P(None, "head"),
        P(None, "head"),
        P("head", None),
        P(),
        P(),
        P(),
        P(),
        P(None, ("dp", "head")),
        P(("dp", "head")),
        P(("dp", "head"), None),
        P(),
        P(),
    )
    return jax.shard_map(shards, mesh=mesh, in_specs=in_specs, out_specs=out_specs, check_vma=False)
```

```python
import functools
import types
import jax
import jax.numpy as jnp
from jax import lax
from jax.experimental import pallas as pl
from jax.experimental.pallas import tpu as pltpu
from jax.sharding import PartitionSpec as P

F32 = jnp.float32
BF16 = jnp.bfloat16
EPS = 1e-06
LANES = 128
V_MASK, V_G1, V_B1, V_PB, V_GA1, V_G2, V_B2, V_FB2, V_GA2 = range(9)
S_GA2, S_FB2, S_LG2, S_LB2, S_GA1, S_PB = range(6)
T_MASK, T_LG1, T_LB1, T_QB, T_VB = range(5)


def dot(a, b):
    return jnp.dot(a, b, preferred_element_type=F32)


def dot_nt(a, b):
    return lax.dot_general(a, b, (((1,), (1,)), ((), ())), preferred_element_type=F32)


def dot_tn(a, b):
    return lax.dot_general(a, b, (((0,), (0,)), ((), ())), preferred_element_type=F32)


def norm_parts(v):
    c = v - jnp.mean(v, axis=-1, keepdims=True)
    r = lax.rsqrt(jnp.mean(c * c, axis=-1, keepdims=True) + EPS)
    return c * r, r


def norm_back(n, r, y, gain):
    yg = y * gain
    return r * (
        yg - jnp.mean(yg, axis=-1, keepdims=True) - n * jnp.mean(yg * n, axis=-1, keepdims=True)
    )


def low_half(shape):
    return lax.broadcasted_iota(jnp.int32, shape, 1) < (LANES // 2)

MESHID = pl.DeviceIdType.MESH


def here():
    dp = lax.axis_index("dp")
    return dp // 4, (dp // 2) % 2, dp % 2, lax.axis_index("head")


def at_dp(z, y, x):
    return {"dp": (z * 2 + y) * 2 + x}


def greet(depth):
    z, y, x, head = here()
    found = [at_dp(z, y, 1 - x), at_dp(z, 1 - y, x), {"head": 1 - head}]
    found += [at_dp((z + k) % depth, y, x) for k in range(1, depth)]
    barrier = pltpu.get_barrier_semaphore()
    for dev in found:
        pl.semaphore_signal(barrier, inc=1, device_id=dev, device_id_type=MESHID)
    pl.semaphore_wait(barrier, len(found))


class Wire:
    def __init__(self, send, recv):
        self.send, self.recv, self.next, self.open = send, recv, 0, []

    def slot(self):
        self.next += 1
        return self.next - 1

    def copy(self, i, src, dst, dev):
        return pltpu.make_async_remote_copy(
            src_ref=src, dst_ref=dst, send_sem=self.send.at[i], recv_sem=self.recv.at[i],
            device_id=dev, device_id_type=MESHID,
        )

    def start(self, i, make):
        self.copy(i, *make()).start()
        self.open.append((i, make))

    def arrived(self, i, ref, dev):
        self.copy(i, ref, ref, dev).wait_recv()

    def sent(self):
        for i, make in self.open:
            self.copy(i, *make()).wait_send()
        self.open = []


class Local:
    def __init__(self, sems):
        self.sems, self.next, self.open = sems, 0, []

    def start(self, make):
        i = self.next
        self.next += 1
        pltpu.make_async_copy(*make(), self.sems.at[i]).start()
        wait = lambda: pltpu.make_async_copy(*make(), self.sems.at[i]).wait()
        self.open.append(wait)
        return wait


def hops(p, y, x):
    ey, ex = (1 - y, x), (y, 1 - x)
    return (ey, ex) if p == 0 else (ex, ey)


def gather_stages(wire, depth, own, slot, column=None):
    z, y, x, head = here()
    ids = {}
    for p in range(2):
        for k in range(depth):
            for kind in "zabc":
                ids[p, kind, k] = wire.slot()
        for kind in range(0 if column is None else 4):
            ids[p, "s", kind] = wire.slot()
    up = lambda k: (z + k) % depth
    down = lambda k: (z + depth - k) % depth

    def columns(p):
        (ay, ax), (by, bx) = hops(p, y, x)
        return (y, x), (ay, ax), (by, bx), (1 - y, 1 - x)

    def send_up(p, k):
        wire.start(ids[p, "z", k], lambda: (own(p), slot(p, z, y, x), at_dp(up(k), y, x)))

    def send_square(p, k, kind, col, to, first=False):
        def make():
            cs = columns(p)
            dst = slot(p, down(k), *cs[col])
            return own(p) if first else dst, dst, at_dp(z, *cs[to])
        wire.start(ids[p, kind, k], make)

    def wait(p, k, kind, col, frm):
        cs = columns(p)
        dev = at_dp(down(k), y, x) if frm is None else at_dp(z, *cs[frm])
        wire.arrived(ids[p, kind, k], slot(p, down(k), *cs[col]), dev)

    def begin():
        for k in range(1, depth):
            for p in range(2):
                send_up(p, k)
        for p in range(2):
            send_square(p, 0, "a", 0, 1, True)
            send_square(p, 0, "b", 0, 2, True)

    def from_column(k):
        for p in range(2):
            wait(p, k, "z", 0, None)
            send_square(p, k, "a", 0, 1)
            send_square(p, k, "b", 0, 2)

    def from_first(k):
        for p in range(2):
            wait(p, k, "a", 1, 1)
            send_square(p, k, "c", 1, 2)

    def from_second(kind, col):
        for p in range(2):
            for k in range(depth):
                wait(p, k, kind, col, 2)

    def across(which):
        for p in range(2):
            def make(p=p):
                block = column(p, *columns(p)[which], head)
                return block, block, {"head": 1 - head}
            wire.start(ids[p, "s", which], make)

    def crossed():
        for which in range(4):
            for p in range(2):
                wire.arrived(ids[p, "s", which], column(p, *columns(p)[which], 1 - head), {"head": 1 - head})

    part = functools.partial
    stages = {"begin": begin, "b": part(from_second, "b", 2), "c": part(from_second, "c", 3), "crossed": crossed}
    for k in range(depth):
        stages["z%d" % k] = part(from_column, k)
        stages["a%d" % k] = part(from_first, k)
        stages["s%d" % k] = part(across, k)
    return stages


def add_into(dst, src):
    dst[...] = (dst[...].astype(F32) + src[...].astype(F32)).astype(dst.dtype)


class SquareSum:
    def __init__(self, wire, theirs, mine, pair_in, square_in, line_in):
        self.wire, self.theirs, self.mine = wire, theirs, mine
        self.pair_in, self.square_in, self.line_in = pair_in, square_in, line_in
        self.ids = {(p, kind): wire.slot() for p in range(2) for kind in "hab"}
        self.place = here()

    def devices(self, p):
        z, y, x, head = self.place
        ex, ey = at_dp(z, y, 1 - x), at_dp(z, 1 - y, x)
        return (ex, ey) if p == 0 else (ey, ex)

    def pair(self):
        for p in range(2):
            self.wire.start(self.ids[p, "h"], lambda p=p: (self.theirs(p), self.pair_in(p), {"head": 1 - self.place[3]}))

    def first(self):
        z, y, x, head = self.place
        for p in range(2):
            self.wire.arrived(self.ids[p, "h"], self.pair_in(p), {"head": 1 - head})
            add_into(self.mine(p, None, None), self.pair_in(p))

            def make(p=p):
                src = self.mine(p, None, 1 - x) if p == 0 else self.mine(p, 1 - y, None)
                return src, self.square_in(p), self.devices(p)[0]
            self.wire.start(self.ids[p, "a"], make)

    def second(self):
        z, y, x, head = self.place
        for p in range(2):
            self.wire.arrived(self.ids[p, "a"], self.square_in(p), self.devices(p)[0])
            add_into(self.mine(p, None, x) if p == 0 else self.mine(p, y, None), self.square_in(p))

            def make(p=p):
                src = self.mine(p, 1 - y, x) if p == 0 else self.mine(p, y, 1 - x)
                return src, self.line_in(p), self.devices(p)[1]
            self.wire.start(self.ids[p, "b"], make)

    def third(self):
        z, y, x, head = self.place
        for p in range(2):
            self.wire.arrived(self.ids[p, "b"], self.line_in(p), self.devices(p)[1])
            add_into(self.mine(p, y, x), self.line_in(p))


class ColumnSum:
    def __init__(self, wire, depth, part, column_in):
        self.wire, self.depth, self.part, self.column_in = wire, depth, part, column_in
        self.ids = {(p, k): wire.slot() for p in range(2) for k in range(1, depth)}
        self.place = here()

    def make(self, p, k):
        z, y, x, head = self.place
        to = (z + k) % self.depth
        return self.part(p, to), self.column_in(p, k), at_dp(to, y, x)

    def send(self, when=None):
        z = self.place[0]
        for p in range(2):
            for k in range(1, self.depth):
                go = lambda p=p, k=k: self.wire.copy(self.ids[p, k], *self.make(p, k)).start()
                if when is None:
                    go()
                else:
                    pl.when(when((z + k) % self.depth))(go)

    def opened(self):
        for p in range(2):
            for k in range(1, self.depth):
                self.wire.open.append((self.ids[p, k], functools.partial(self.make, p, k)))

    def total(self, p):
        z, y, x, head = self.place
        acc = self.part(p, z)[...].astype(F32)
        for k in range(1, self.depth):
            back = at_dp((z + self.depth - k) % self.depth, y, x)
            self.wire.arrived(self.ids[p, k], self.column_in(p, k), back)
            acc = acc + self.column_in(p, k)[...].astype(F32)
        return acc


class TargetSum:
    def __init__(self, wire, depth, t, part, column_in):
        self.wire, self.depth, self.t, self.part, self.column_in = wire, depth, t, part, column_in
        self.ids = [wire.slot() for _ in range(2 * (depth - 1))]
        self.place = here()

    def copy(self, p):
        z, y, x, head = self.place
        k = (z + self.depth - self.t) % self.depth - 1
        k = jnp.maximum(k, 0)
        return self.wire.copy(self.ids[p * (self.depth - 1)] + k, self.part(p), self.column_in.at[p, k], at_dp(self.t, y, x))

    def away(self, action):
        @pl.when(self.place[0] != self.t)
        def _():
            for p in range(2):
                action(self.copy(p))

    def send(self):
        self.away(lambda copy: copy.start())

    def sent(self):
        self.away(lambda copy: copy.wait_send())

    def total(self, store):
        z, y, x, head = self.place

        @pl.when(z == self.t)
        def _():
            for p in range(2):
                acc = self.part(p)[...].astype(F32)
                for k in range(self.depth - 1):
                    back = at_dp((self.t + k + 1) % self.depth, y, x)
                    self.wire.arrived(self.ids[p * (self.depth - 1) + k], self.column_in.at[p, k], back)
                    acc = acc + self.column_in[p, k].astype(F32)
                store(p, acc)


class SmallSum:
    def __init__(self, wire, depth, bufs, line):
        self.wire, self.depth, self.bufs, self.line = wire, depth, bufs, line
        self.ids = [wire.slot() for _ in range(2 + depth)]
        self.place = here()

    def devices(self):
        z, y, x, head = self.place
        return [{"head": 1 - head}, at_dp(z, y, 1 - x), at_dp(z, 1 - y, x)]

    def send(self, n):
        self.wire.start(self.ids[n], lambda: (self.bufs.at[2 * n], self.bufs.at[2 * n + 1], self.devices()[n]))

    def take(self, n):
        self.wire.arrived(self.ids[n], self.bufs.at[2 * n + 1], self.devices()[n])
        self.bufs[2 * n + 2] = self.bufs[2 * n] + self.bufs[2 * n + 1]

    def begin(self):
        self.send(0)

    def middle(self, n):
        self.take(n - 1)
        self.send(n)

    def column(self):
        z, y, x, head = self.place
        self.take(2)
        self.line[z] = self.bufs[6]
        for k in range(1, self.depth):
            self.wire.start(
                self.ids[2 + k],
                lambda k=k: (self.bufs.at[6], self.line.at[z], at_dp((z + k) % self.depth, y, x)),
            )

    def result(self):
        z, y, x, head = self.place
        for k in range(1, self.depth):
            back = (z + self.depth - k) % self.depth
            self.wire.arrived(self.ids[2 + k], self.line.at[back], at_dp(back, y, x))
        total = self.line[0]
        for n in range(1, self.depth):
            total = total + self.line[n]
        return total


def bind(names, refs):
    assert len(names) == len(refs)
    return types.SimpleNamespace(**dict(zip(names, refs)))


def spread_mask(masked, tmp, ch):
    images, rows = masked.shape
    tmp[...] = jnp.zeros_like(tmp)
    tmp[0:images, 0:rows] = masked[...].astype(F32)
    turned = tmp[...].T
    for i in range(images):
        ch[i] = turned[0:rows, i:i + 1]


def pad_index(raw, idx):
    idx[...] = jnp.zeros_like(idx)
    idx[0:raw.shape[0], 0:raw.shape[1]] = raw[...]


def run_all(stages):
    for stage in stages:
        stage()


def vmem(n):
    return [pl.BlockSpec(memory_space=pltpu.VMEM)] * n


ANY = pl.BlockSpec(memory_space=pl.ANY)
sd = jax.ShapeDtypeStruct
dma = lambda n: pltpu.SemaphoreType.DMA((n,))


def whole(a):
    return pl.BlockSpec(a.shape, lambda s: (0,) * len(a.shape), pipeline_mode=pl.Buffered(1))


FWD_IN = ("x", "masked", "kv", "raw", "vec")
FWD_OUT = ("normed", "q", "k", "v", "p", "att", "attn", "res", "n2")
FWD_SCR = ("bias", "idx", "valid", "tmp", "ch", "lsem")


def attn_forward_kernel(direct, *refs):
    hbm = tuple(n + "_hbm" for n in FWD_OUT[:6])
    if direct:
        names = FWD_IN + ("mixown", "wown", "wpown", "own1", "own2", "spot") + hbm + FWD_OUT[6:]
        names += ("w", "wp", "w1", "w2", "b1") + FWD_OUT[:6] + FWD_SCR + ("mix", "bufs", "line", "send", "recv")
    else:
        names = FWD_IN + ("mix", "w", "wp") + hbm + FWD_OUT[6:] + FWD_OUT[:6] + FWD_SCR
    r = bind(names, refs)
    images, rows, width = r.x.shape
    rp = r.normed.shape[0] // images
    keys = r.k.shape[1]
    heads = r.bias.shape[0]
    scale = (width // heads) ** -0.5
    here_heads = heads // r.mix.shape[0]
    own_tiles = width // r.mix.shape[0] // LANES
    chunks = (r.mix.shape[1] - 2 * own_tiles) // here_heads

    plan = {}
    local = Local(r.lsem)
    head = lax.axis_index("head")
    if direct:
        depth = r.w1.shape[0]
        z, y, x, head = here()
        half = r.wown.shape[2]
        cols = pl.ds(pl.multiple_of(head * half, LANES), half)
        prows = pl.ds(pl.multiple_of(head * half, LANES), half)
        full = (r.w1, r.w2)
        wire = Wire(r.send, r.recv)
        greet(depth)
        other = {"head": 1 - head}
        swaps = [
            (r.mixown, r.mix.at[head], r.mix.at[1 - head]),
            (r.wown, r.w.at[:, :, cols], r.w.at[:, :, pl.ds(pl.multiple_of((1 - head) * half, LANES), half)]),
            (r.wpown, r.wp.at[prows], r.wp.at[pl.ds(pl.multiple_of((1 - head) * half, LANES), half)]),
        ]
        swap_ids = [wire.slot() for _ in swaps]
        for i, (src, dst, back) in zip(swap_ids, swaps):
            wire.start(i, lambda src=src, dst=dst: (src, dst, other))
        for src, dst, back in swaps:
            local.start(lambda src=src, dst=dst: (src, dst))
        slot = lambda p, zz, yy, xx: full[p].at[zz, yy, xx, head]
        own = (r.own1, r.own2)
        for p in range(2):
            local.start(lambda p=p: (own[p], slot(p, z, y, x)))
        r.bufs[0] = r.spot[...]
        small = SmallSum(wire, depth, r.bufs, r.line)
        g = gather_stages(
            wire, depth, own=lambda p: own[p], slot=slot,
            column=lambda p, yy, xx, hd: full[p].at[:, yy, xx, hd],
        )
        g["begin"]()
        small.begin()
        middle = functools.partial
        plan = {
            "g1": [g["z1"], g["a0"]], "g2": [middle(small.middle, 1)],
            "p1": [g["z2"], g["a1"], middle(small.middle, 2)],
            "t1": [g["z3"], g["a2"], g["s0"], small.column], "t4": [g["a3"], g["s1"]],
            "t5": [g["b"], g["s2"]], "t6": [g["c"], g["s3"]],
        }

    def tick(point):
        run_all(plan.get(point, ()))

    spread_mask(r.masked, r.tmp, r.ch)
    pad_index(r.raw, r.idx)
    r.valid[...] = jnp.zeros_like(r.valid)
    r.valid[0:r.kv.shape[0], 0:rows] = r.kv[...]
    r.normed[...] = jnp.zeros_like(r.normed)
    r.n2[...] = jnp.zeros_like(r.n2)
    r.res[...] = jnp.zeros_like(r.res)

    def hidden_of(i):
        ch = r.ch[i]
        return r.x[i].astype(F32) * (1.0 - ch) + ch * r.vec[V_MASK:V_MASK + 1, :]

    def first_norm(i, carry):
        n, _ = norm_parts(hidden_of(i))
        out = n * r.vec[V_G1:V_G1 + 1, :] + r.vec[V_B1:V_B1 + 1, :]
        r.normed[pl.ds(pl.multiple_of(i * rp, 16), rows), :] = out.astype(BF16)
        return carry

    lax.fori_loop(0, images, first_norm, 0)
    if direct:
        for wait in local.open:
            wait()
        local.open = []
        wire.arrived(swap_ids[0], swaps[0][2], other)
    send_out = lambda name, at=slice(None): local.start(
        lambda: (getattr(r, name).at[at], getattr(r, name + "_hbm").at[at]))
    send_out("normed")

    def gather_head(h, carry):
        for half in range(keys // LANES):
            idx = r.idx[:, half * LANES:(half + 1) * LANES]
            low = idx & (LANES - 1)
            high = idx >> 7
            acc = jnp.zeros(idx.shape, F32)
            for c in range(chunks):
                row = r.mix[h // here_heads, pl.ds((h % here_heads) * chunks + c, 1), :]
                got = jnp.take_along_axis(jnp.broadcast_to(row, idx.shape), low, axis=1)
                acc = jnp.where(high == c, got, acc)
            r.bias[h, :, half * LANES:(half + 1) * LANES] = acc
        return carry

    groups = 3
    for n in range(groups):
        lax.fori_loop(n * heads // groups, (n + 1) * heads // groups, gather_head, 0)
        tick("g%d" % n)

    if direct:
        for n in (1, 2):
            wire.arrived(swap_ids[n], swaps[n][2], other)
    zeros_tail = jnp.zeros((images, keys - rp, width), BF16)
    r.k[:, rp:, :] = zeros_tail
    r.v[:, rp:, :] = zeros_tail

    def bias_row(kind, nb):
        tiles = []
        for t in (2 * nb, 2 * nb + 1):
            at = here_heads * chunks + kind * own_tiles + t % own_tiles
            tiles.append(r.mix[t // own_tiles, at:at + 1, :])
        return jnp.concatenate(tiles, axis=1)

    for c, (dst, kind) in enumerate(((r.q, 0), (r.k, None), (r.v, 1))):
        for nb in range(width // 256):
            cols = slice(nb * 256, (nb + 1) * 256)
            acc = dot(r.normed[...], r.w[c, :, cols])
            if kind is not None:
                acc = acc + bias_row(kind, nb)
            acc = acc.astype(BF16)
            for i in range(images):
                dst[i, :rp, cols] = acc[i * rp:(i + 1) * rp]
        send_out("qkv"[c])
        tick("p%d" % c)

    def attend(t, carry):
        i = t // (heads // 2)
        j = t % (heads // 2)
        lanes = pl.ds(pl.multiple_of(j * LANES, LANES), LANES)
        qp = r.q[i, :, lanes]
        kp = r.k[i, :, lanes]
        vp = r.v[i, :, lanes]
        lo = low_half((rp, LANES))
        ok = r.valid[pl.ds(head * images + i, 1), :] > 0
        outs = []
        for s in range(2):
            qs = jnp.where(lo if s == 0 else jnp.logical_not(lo), qp, jnp.zeros_like(qp))
            sc = dot_nt(qs, kp) * scale + r.bias[2 * j + s]
            sc = jnp.where(ok, sc, -1e30)
            e = jnp.exp(sc - jnp.max(sc, axis=-1, keepdims=True))
            prob = e * (1.0 / jnp.sum(e, axis=-1, keepdims=True))
            r.p[i, 2 * j + s] = prob
            outs.append(dot(prob.astype(BF16), vp))
        att = jnp.where(lo, outs[0], outs[1]).astype(BF16)
        r.att[pl.ds(pl.multiple_of(i * rp, 16), rp), lanes] = att
        return carry

    work = images * (heads // 2)
    for n in range(2 * images):
        lax.fori_loop(n * work // (2 * images), (n + 1) * work // (2 * images), attend, 0)
        if n % 2:
            send_out("p", n // 2)
        tick("t%d" % n)
    send_out("att")

    def finish(i, carry):
        at = pl.multiple_of(i * rp, 16)
        branch = dot(r.att[pl.ds(at, rp), :], r.wp[...]) + r.vec[V_PB:V_PB + 1, :]
        r.attn[pl.ds(at, rp), :] = branch
        res = hidden_of(i) + r.vec[V_GA1:V_GA1 + 1, :] * branch[:rows]
        r.res[pl.ds(at, rows), :] = res
        n, _ = norm_parts(res)
        out = n * r.vec[V_G2:V_G2 + 1, :] + r.vec[V_B2:V_B2 + 1, :]
        r.n2[pl.ds(at, rows), :] = out.astype(BF16)
        return carry

    lax.fori_loop(0, images, finish, 0)
    if direct:
        g["crossed"]()
        r.b1[...] = small.result()
        wire.sent()
    for wait in local.open:
        wait()


def attn_forward(direct, x, masked, kv, raw, vec, heads, extra, rp, keys, depth):
    images, rows, width = x.shape
    flat = images * rp
    outs = [
        sd((flat, width), BF16), sd((images, rp, width), BF16), sd((images, keys, width), BF16),
        sd((images, keys, width), BF16), sd((images, heads, rp, keys), F32),
        sd((flat, width), BF16), sd((flat, width), F32), sd((flat, width), F32), sd((flat, width), BF16),
    ]
    tall = -(-max(kv.shape[0], images) // 8) * 8
    scratch = [pltpu.VMEM(o.shape, o.dtype) for o in outs[:6]] + [
        pltpu.VMEM((heads, rp, keys), F32), pltpu.VMEM((rp, keys), jnp.int32), pltpu.VMEM((tall, keys), jnp.int32),
        pltpu.VMEM((tall, keys), F32), pltpu.VMEM((images, rows, 1), F32), dma(16),
    ]
    in_specs, out_specs = vmem(5), [ANY] * 6 + vmem(3)
    params = {}
    if direct:
        mixown, wown, wpown, own1, own2, spot = extra
        part = sd((depth, 2, 2, 2) + own1.shape, BF16)
        outs += [sd((3, width, width), BF16), sd((width, width), BF16), part, part, sd(spot.shape, F32)]
        in_specs += vmem(6)
        out_specs += vmem(2) + [ANY, ANY] + vmem(1)
        n = 3 + 2 * (4 * depth + 4) + 2 + depth
        scratch += [
            pltpu.VMEM((2,) + mixown.shape, F32), pltpu.VMEM((7,) + spot.shape, F32),
            pltpu.VMEM((depth,) + spot.shape, F32), dma(n), dma(n),
        ]
        params = dict(collective_id=1, has_side_effects=True)
    else:
        in_specs += vmem(3)
    return pl.pallas_call(
        functools.partial(attn_forward_kernel, direct), name="attn_forward",
        out_shape=tuple(outs), in_specs=in_specs, out_specs=out_specs, scratch_shapes=scratch,
        compiler_params=pltpu.CompilerParams(vmem_limit_bytes=60 * 2**20, **params),
    )(x, masked, kv, raw, vec, *extra)


MLP_IN = ("n2", "res", "attn", "cot", "vec", "b1", "w1", "w2")
MLP_OUT = ("gb1", "out", "dres", "dproj", "small")
MLP_SCR = ("db", "act", "dpre", "branch", "dn")
MLP_COMM = ("g", "pair_in", "square_in", "line_in", "column", "column_in", "send", "recv", "lsem")


def level_of(step, steps):
    return jnp.where(step == 0, 0, jnp.where(step == 1, steps - 1, step - 1))


def mlp_kernel(direct, *refs):
    if direct:
        r = bind(MLP_IN + ("sums", "glast", "gff") + MLP_OUT + MLP_SCR + MLP_COMM, refs)
    else:
        r = bind(MLP_IN + ("g1", "g2") + MLP_OUT + MLP_SCR, refs)
    images, rows, width = r.cot.shape
    flat = r.n2.shape[0]
    rp = flat // images
    step = pl.program_id(0)
    steps = pl.num_programs(0)
    plan = {}
    if direct:
        depth = r.g.shape[0]
        done = depth - 1
        wire = Wire(r.send, r.recv)
        z, y, x, head = here()
        every = lambda v: slice(None) if v is None else v
        chunks = [
            SquareSum(
                wire,
                theirs=lambda p, t=t: r.g.at[t, p, :, :, 1 - head],
                mine=lambda p, yy, xx, t=t: r.g.at[t, p, every(yy), every(xx), head],
                pair_in=lambda p, t=t: r.pair_in.at[t, p],
                square_in=lambda p, t=t: r.square_in.at[t, p],
                line_in=lambda p, t=t: r.line_in.at[t, p],
            )
            for t in range(done)
        ]
        ends = [
            TargetSum(wire, depth, t, part=lambda p, n=n: r.column.at[n, p], column_in=r.column_in.at[n])
            for n, t in enumerate((0, depth - 1))
        ]

        def close(n):
            chunks[n].third()
            for p in range(2):
                if n < 2:
                    r.column[n, p] = r.g[n, p, y, x, head]
                else:
                    r.sums[p] = r.g[n, p, y, x, head]
            if n < 2:
                ends[n].send()

        def last_block():
            return pltpu.make_async_copy(r.g.at[done], r.glast, r.lsem.at[0])

        def end():
            r.gff[...] = jnp.zeros_like(r.gff)

            def keep(p, value):
                r.gff[p] = value
            for t in ends:
                t.total(keep)
                t.sent()
            wire.sent()
            last_block().wait()

        part = functools.partial
        plan = {
            (0, 0): [part(greet, depth)], (0, 4): [chunks[0].pair],
            (1, 1): [chunks[0].first], (1, 4): [chunks[1].pair, chunks[0].second],
            (2, 1): [chunks[1].first], (2, 2): [part(close, 0)], (2, 4): [chunks[2].pair, chunks[1].second],
            (3, 1): [chunks[2].first], (3, 2): [part(close, 1)], (3, 4): [lambda: last_block().start(), chunks[2].second],
            (3, 5): [part(close, 2)], (3, 6): [end],
        }

    def tick(point):
        for (s, at), stages in sorted(plan.items(), key=lambda kv: kv[0]):
            if at == point:
                pl.when(step == s)(functools.partial(run_all, stages))

    tick(0)

    @pl.when(step == 0)
    def _():
        r.db[...] = jnp.zeros_like(r.db)
        r.branch[...] = jnp.zeros_like(r.branch)
        r.dn[...] = jnp.zeros_like(r.dn)

        def fill(i, carry):
            up = r.cot[i].astype(F32) * r.vec[V_GA2:V_GA2 + 1, :]
            r.db[pl.ds(pl.multiple_of(i * rp, 16), rows), :] = up.astype(BF16)
            return carry

        lax.fori_loop(0, images, fill, 0)

    def tile(i, gb1):
        at = pl.ds(pl.multiple_of(i * rp, 16), rp)
        pre = dot_nt(r.n2[at, :], r.w1[...]) + r.b1[...]
        cdf = 0.5 * (1.0 + lax.erf(pre * 0.7071067811865476))
        slope = cdf + pre * (0.3989422804014327 * jnp.exp(-0.5 * pre * pre))
        act = (pre * cdf).astype(BF16)
        r.act[at, :] = act
        dpre = (dot_nt(r.db[at, :], r.w2[...]) * slope).astype(BF16)
        r.dpre[at, :] = dpre
        r.branch[at, :] += dot(act, r.w2[...])
        r.dn[at, :] += dot(dpre, r.w1[...])
        return gb1 + jnp.sum(dpre.astype(F32), axis=0, keepdims=True)

    gb1 = lax.fori_loop(0, images // 2, tile, jnp.zeros(r.gb1.shape, F32))
    tick(1)
    r.gb1[...] = lax.fori_loop(images // 2, images, tile, gb1)
    tick(2)

    def store(p, value):
        if not direct:
            (r.g1, r.g2)[p][...] = value
            return
        r.g[step, p] = value.reshape(r.g.shape[2:])

    store(1, dot_tn(r.act[...], r.db[...]).astype(BF16))
    tick(3)
    store(0, dot_tn(r.dpre[...], r.n2[...]).astype(BF16))
    tick(4)

    @pl.when(step == steps - 1)
    def _():
        r.dproj[...] = jnp.zeros_like(r.dproj)
        r.dres[...] = jnp.zeros_like(r.dres)
        r.small[...] = jnp.zeros_like(r.small)

        def add(row, value):
            r.small[row:row + 1, :] += jnp.sum(value, axis=0, keepdims=True)

        def finish(i, carry):
            at = pl.multiple_of(i * rp, 16)
            span = pl.ds(at, rows)
            up = r.cot[i].astype(F32)
            branch = r.branch[span, :] + r.vec[V_FB2:V_FB2 + 1, :]
            res = r.res[span, :]
            r.out[i] = (res + r.vec[V_GA2:V_GA2 + 1, :] * branch).astype(BF16)
            add(S_GA2, up * branch)
            add(S_FB2, (up * r.vec[V_GA2:V_GA2 + 1, :]).astype(BF16).astype(F32))
            n, inv = norm_parts(res)
            dn = r.dn[span, :]
            add(S_LG2, dn * n)
            add(S_LB2, dn)
            dres = up + norm_back(n, inv, dn, r.vec[V_G2:V_G2 + 1, :])
            r.dres[span, :] = dres
            add(S_GA1, dres * r.attn[span, :])
            dproj = (dres * r.vec[V_GA1:V_GA1 + 1, :]).astype(BF16)
            r.dproj[span, :] = dproj
            add(S_PB, dproj.astype(F32))
            return carry

        lax.fori_loop(0, images, finish, 0)

    tick(5)
    tick(6)


def mlp(direct, n2, res, attn, cot, vec, b1, w1, w2, steps):
    images, rows, width = cot.shape
    flat = n2.shape[0]
    ff = w1.shape[0]
    block = ff // steps
    share = block // 8
    part = pl.BlockSpec((block, width), lambda s: (level_of(s, steps), 0))
    line = pl.BlockSpec((1, block), lambda s: (0, level_of(s, steps)))
    outs = [sd((1, ff), F32), sd(cot.shape, BF16), sd((flat, width), F32), sd((flat, width), BF16), sd((8, width), F32)]
    specs = [line] + [whole(o) for o in outs[1:]]
    scratch = [
        pltpu.VMEM((flat, width), BF16), pltpu.VMEM((flat, block), BF16), pltpu.VMEM((flat, block), BF16),
        pltpu.VMEM((flat, width), F32), pltpu.VMEM((flat, width), F32),
    ]
    params = {}
    if direct:
        first = [sd((2, share, width), BF16), sd((2, 2, 2, 2, share, width), BF16), sd((2, share, width), F32)]
        outs, specs = first + outs, [whole(first[0]), ANY, whole(first[2])] + specs
        n = 6 * (steps - 1) + 4 * (steps - 1)
        scratch += [
            pltpu.VMEM((steps, 2, 2, 2, 2, share, width), BF16), pltpu.VMEM((steps - 1, 2, 2, 2, share, width), BF16),
            pltpu.VMEM((steps - 1, 2, 2, share, width), BF16), pltpu.VMEM((steps - 1, 2, share, width), BF16),
            pltpu.VMEM((2, 2, share, width), BF16), pltpu.VMEM((2, 2, steps - 1, share, width), BF16),
            dma(n), dma(n), dma(1),
        ]
        params = dict(collective_id=2, has_side_effects=True)
    else:
        outs, specs = [sd((ff, width), BF16)] * 2 + outs, [part, part] + specs
    return pl.pallas_call(
        functools.partial(mlp_kernel, direct), name="mlp", grid=(steps,), out_shape=tuple(outs),
        in_specs=[whole(n2), whole(res), whole(attn), whole(cot), whole(vec), line, part, part],
        out_specs=specs, scratch_shapes=scratch,
        compiler_params=pltpu.CompilerParams(vmem_limit_bytes=60 * 2**20, **params),
    )(n2, res, attn, cot, vec, b1, w1, w2)


BWD_IN = ("x", "masked", "raw", "vec", "w", "wp", "normed", "q", "k", "v", "p", "att", "dres", "dproj")
BWD_SCR = ("dat", "dqkv", "ds", "nt", "dpt", "idx", "tmp", "ch")
BWD_COMM = ("g", "pair_in", "square_in", "line_in", "column_in", "ff", "ffpair", "ffsquare", "ffline", "ffcol", "ffcolumn")


def attn_backward_kernel(direct, *refs):
    if direct:
        names = BWD_IN + ("sums", "glast", "gffin", "s2", "gb1", "gx", "full", "gff", "small") + BWD_SCR + BWD_COMM
        r = bind(names + ("bufs", "line", "tsum", "gathered", "send", "recv", "lsem"), refs)
    else:
        r = bind(BWD_IN + ("gx", "gw", "gt", "tsum") + BWD_SCR, refs)
    images, rows, width = r.x.shape
    flat = r.normed.shape[0]
    rp = flat // images
    keys = r.k.shape[1]
    heads = r.ds.shape[0]
    scale = (width // heads) ** -0.5
    step = pl.program_id(0)
    pairs = heads // 2
    per = pairs // 2
    j = (step % 2) * per + step // 2
    plan = {}

    if direct:
        z, y, x, head = here()
        depth = r.g.shape[4]
        wire = Wire(r.send, r.recv)
        every = lambda v: slice(None) if v is None else v
        ff = SquareSum(
            wire,
            theirs=lambda p: r.glast.at[p, :, :, 1 - head],
            mine=lambda p, yy, xx: r.ff.at[p, every(yy), every(xx)],
            pair_in=lambda p: r.ffpair.at[p], square_in=lambda p: r.ffsquare.at[p], line_in=lambda p: r.ffline.at[p],
        )
        between = [
            TargetSum(wire, depth, n + 1, part=lambda p, n=n: r.ffcol.at[n, p], column_in=r.ffcolumn.at[n])
            for n in range(2)
        ]
        squares, lines, gathers = [], [], []
        for m in range(per):
            squares.append(SquareSum(
                wire,
                theirs=lambda p, m=m: r.g.at[m, 1 - head, p],
                mine=lambda p, yy, xx, m=m: r.g.at[m, head, p, :, :, every(yy), every(xx)],
                pair_in=lambda p, m=m: r.pair_in.at[m, p],
                square_in=lambda p, m=m: r.square_in.at[m, p], line_in=lambda p, m=m: r.line_in.at[m, p],
            ))
            lines.append(ColumnSum(
                wire, depth, part=lambda p, zz, m=m: r.g.at[m, head, p, :, zz, y, x],
                column_in=lambda p, k, m=m: r.column_in.at[m, p, k - 1],
            ))
            lanes_m = slice(m * LANES, (m + 1) * LANES)
            slot = lambda p, zz, yy, xx, lanes_m=lanes_m: r.gathered.at[p, :, zz, yy, xx, :, lanes_m]
            gathers.append(gather_stages(wire, depth, own=lambda p, slot=slot: slot(p, z, y, x), slot=slot))
        small = SmallSum(wire, depth, r.bufs, r.line)
        part = functools.partial

        def ff_begin():
            greet(depth)
            ff.pair()
            for p in range(2):
                own_block(p).start()
                r.ffcol[0, p] = r.sums[p]
            between[0].send()

        def own_block(p):
            return pltpu.make_async_copy(r.glast.at[p, :, :, head], r.ff.at[p], r.lsem.at[p])

        def ff_first():
            for p in range(2):
                own_block(p).wait()
            ff.first()

        def ff_third():
            ff.third()
            for p in range(2):
                r.ffcol[1, p] = r.ff[p, y, x]
            between[1].send()

        def ff_last():
            r.gff[...] = r.gffin[...]

            def keep(p, value):
                r.gff[p] = value
            for t in between:
                t.total(keep)
                t.sent()

        def third(m):
            squares[m].third()
            lines[m].send()
            lines[m].opened()

        def last(m):
            for p in range(2):
                r.gathered[p, :, z, y, x, :, m * LANES:(m + 1) * LANES] = lines[m].total(p).astype(BF16)
            gathers[m]["begin"]()

        g0, g1, g2 = gathers
        plan = {
            (0, 0): [ff_begin], (0, 1): [ff_first], (1, 2): [ff.second], (1, 4): [squares[0].pair],
            (2, 3): [ff_third, squares[0].first], (3, 4): [squares[1].pair, squares[0].second],
            (4, 3): [squares[1].first], (4, 4): [part(third, 0)],
            (5, 4): [squares[2].pair, squares[1].second, part(last, 0)],
            (5, 6): [squares[2].first, part(third, 1)], (5, 7): [g0["z1"], g0["z2"], g0["z3"]], (5, 8): [part(last, 1)],
            (5, 9): [squares[2].second, g0["a0"], g0["a1"], g0["a2"], g0["a3"]], (5, 10): [g1["z1"], g1["z2"], g1["z3"]],
            (5, 11): [part(third, 2), g0["b"], g0["c"]], (5, 12): [g1["a0"], g1["a1"], g1["a2"], g1["a3"]], (5, 13): [ff_last],
        }

    def tick(point):
        for (s, at), stages in plan.items():
            if at == point:
                pl.when(step == s)(functools.partial(run_all, stages))

    tick(0)

    @pl.when(step == 0)
    def _():
        for i in range(images):
            at = slice(i * rp, (i + 1) * rp)
            r.dat[at, :] = dot_nt(r.dproj[at, :], r.wp[...]).astype(BF16)
        spread_mask(r.masked, r.tmp, r.ch)
        pad_index(r.raw, r.idx)
        r.nt[...] = r.normed[...].T
        r.dpt[...] = r.dproj[...].T
        r.tsum[...] = jnp.zeros_like(r.tsum)

    tick(1)
    lanes = pl.ds(pl.multiple_of(j * LANES, LANES), LANES)
    r.ds[2 * j] = jnp.zeros((rp, keys), F32)
    r.ds[2 * j + 1] = jnp.zeros((rp, keys), F32)

    def image(i, carry):
        at = pl.ds(pl.multiple_of(i * rp, 16), rp)
        qp = r.q[i, :, lanes]
        kp = r.k[i, :, lanes]
        vp = r.v[i, :, lanes]
        da = r.dat[at, lanes]
        lo = low_half((rp, LANES))
        dv, dq, dk = [], [], []
        for s in range(2):
            das = jnp.where(lo if s == 0 else jnp.logical_not(lo), da, jnp.zeros_like(da))
            prob = r.p[i, s]
            dp = dot_nt(das, vp)
            dsc = prob * (dp - jnp.sum(prob * dp, axis=-1, keepdims=True))
            dsb = dsc.astype(BF16)
            r.ds[2 * j + s] += dsb.astype(F32)
            dv.append(dot_tn(prob.astype(BF16), da))
            dq.append(dot(dsb, kp))
            dk.append(dot_tn(dsb, qp))
        lok = low_half((keys, LANES))
        r.dqkv[0, at, lanes] = (jnp.where(lo, dq[0], dq[1]) * scale).astype(BF16)
        r.dqkv[1, at, lanes] = (jnp.where(lok, dk[0], dk[1]) * scale)[:rp].astype(BF16)
        r.dqkv[2, at, lanes] = jnp.where(lok, dv[0], dv[1])[:rp].astype(BF16)
        return carry

    lax.fori_loop(0, images // 2, image, 0)
    tick(2)
    lax.fori_loop(images // 2, images, image, 0)
    tick(3)

    def store(c, value):
        value = value.astype(BF16)
        if direct:
            r.g[step // 2, step % 2, c // 2, c % 2] = value.reshape(r.g.shape[4:])
        else:
            r.gw[0, c] = value

    for c in range(3):
        store(c, dot(r.nt[...], r.dqkv[c, :, lanes]))
    store(3, dot(r.dpt[...], r.att[:, lanes]))
    tick(4)

    @pl.when(step == pairs - 1)
    def _():
        def now(point):
            if direct:
                run_all(plan.get((pairs - 1, point), ()))

        def column(row, c):
            def body(i, acc):
                piece = r.dqkv[c, pl.ds(pl.multiple_of(i * rp, 16), rp), :].astype(F32)
                return acc + jnp.sum(piece, axis=0, keepdims=True)
            r.tsum[row:row + 1, :] = lax.fori_loop(0, images, body, jnp.zeros((1, width), F32))

        column(T_QB, 0)
        column(T_VB, 2)

        def finish(i, carry):
            at = pl.multiple_of(i * rp, 16)
            span = pl.ds(at, rp)
            dn = dot_nt(r.dqkv[0, span, :], r.w[0])
            dn += dot_nt(r.dqkv[1, span, :], r.w[1])
            dn += dot_nt(r.dqkv[2, span, :], r.w[2])
            dn = dn[:rows]
            ch = r.ch[i]
            hidden = r.x[i].astype(F32) * (1.0 - ch) + ch * r.vec[V_MASK:V_MASK + 1, :]
            n, inv = norm_parts(hidden)
            dh = r.dres[pl.ds(at, rows), :] + norm_back(n, inv, dn, r.vec[V_G1:V_G1 + 1, :])
            r.gx[i] = dh * (1.0 - ch)
            for row, value in ((T_MASK, dh * ch), (T_LG1, dn * n), (T_LB1, dn)):
                r.tsum[row:row + 1, :] += jnp.sum(value, axis=0, keepdims=True)
            return carry

        for i in range(images):
            lax.fori_loop(i, i + 1, finish, 0)
            now(5 + i)

        a_iota = lax.broadcasted_iota(jnp.int32, (8, keys), 0)
        b_iota = lax.broadcasted_iota(jnp.int32, (LANES, keys), 0)

        def scatter(t, acc):
            at = pl.ds(pl.multiple_of(t * 8, 8), 8)
            idx = r.idx[at, :]
            high, low = idx >> 7, idx & (LANES - 1)
            tiles = [r.ds[h, at, :] for h in range(heads)]
            lefts, rests, ones = [], [], []
            for s in range(8):
                pick = jnp.broadcast_to(high[s:s + 1], (8, keys)) == a_iota
                ones.append((jnp.broadcast_to(low[s:s + 1], (LANES, keys)) == b_iota).astype(F32).astype(BF16))
                left = jnp.concatenate(
                    [jnp.where(pick, jnp.broadcast_to(tile[s:s + 1], (8, keys)), 0.0) for tile in tiles], axis=0)
                top = left.astype(BF16)
                lefts.append(top)
                rests.append((left - top.astype(F32)).astype(BF16))
            one = jnp.concatenate(ones, axis=1)
            return acc + dot_nt(jnp.concatenate(lefts, axis=1), one) + dot_nt(jnp.concatenate(rests, axis=1), one)

        table = jnp.zeros((heads * 8, LANES), F32)
        blocks = rp // 8
        for part_ in range(5):
            table = lax.fori_loop(part_ * blocks // 5, (part_ + 1) * blocks // 5, scatter, table)
            now(9 + part_)
        if not direct:
            r.gt[...] = table
            return
        wide = width // LANES
        tall = heads * 8 // wide
        r.bufs[0, 0:8] = r.tsum[...]
        r.bufs[0, 8:16] = r.s2[...]
        at = 16
        for t in range(wide):
            r.bufs[0, at:at + tall, t * LANES:(t + 1) * LANES] = table[t * tall:(t + 1) * tall]
        at += tall
        r.bufs[0, at:at + r.gb1.shape[0]] = r.gb1[...]
        small.begin()
        last(2)
        small.middle(1)
        run_all([g1["b"], g1["c"]])
        run_all(g2["z%d" % k] for k in range(1, depth))
        small.middle(2)
        run_all(g2["a%d" % k] for k in range(depth))
        small.column()
        run_all([g2["b"], g2["c"]])
        r.full[...] = r.gathered[...]
        r.small[...] = small.result()
        wire.sent()


def attn_backward(direct, args, heads, extra, rp, keys, depth):
    x, masked, raw, vec, w, wp, normed, q, k, v, p, att, dres, dproj = args
    images, rows, width = x.shape
    flat = images * rp
    pairs = heads // 2
    per = pairs // 2
    order = lambda s: (s % 2) * per + s // 2
    outs = [sd((images, rows, width), F32)]
    specs = [whole(outs[0])]
    scratch = [
        pltpu.VMEM((flat, width), BF16), pltpu.VMEM((3, flat, width), BF16), pltpu.VMEM((heads, rp, keys), F32),
        pltpu.VMEM((width, flat), BF16), pltpu.VMEM((width, flat), BF16), pltpu.VMEM((rp, keys), jnp.int32),
        pltpu.VMEM((-(-images // 8) * 8, keys), F32), pltpu.VMEM((images, rows, 1), F32),
    ]
    params = {}
    if direct:
        sums, glast, gffin, s2, gb1 = extra
        share = glast.shape[-2]
        own = width // (4 * depth)
        total = 16 + heads * 8 * LANES // width + gb1.shape[0]
        more = [sd((2, 2, depth, 2, 2, own, per * LANES), BF16), sd((2, share, width), F32), sd((total, width), F32)]
        outs += more
        specs += [whole(o) for o in more]
        n = 6 + 4 * (depth - 1) + per * (6 + 2 * (depth - 1) + 8 * depth) + 2 + depth
        scratch += [pltpu.VMEM(s, BF16) for s in (
            (per, 2, 2, 2, depth, 2, 2, own, LANES), (per, 2, 2, depth, 2, 2, own, LANES),
            (per, 2, 2, depth, 2, own, LANES), (per, 2, 2, depth, own, LANES), (per, 2, depth - 1, 2, own, LANES),
            (2, 2, 2, share, width), (2, 2, 2, share, width), (2, 2, share, width), (2, share, width),
            (2, 2, share, width), (2, 2, depth - 1, share, width),
        )]
        scratch += [pltpu.VMEM(s, F32) for s in ((7, total, width), (depth, total, width), (8, width))]
        scratch += [pltpu.VMEM(more[0].shape, BF16), dma(n), dma(n), dma(2)]
        params = dict(collective_id=3, has_side_effects=True)
    else:
        more = [sd((pairs, 4, width, LANES), BF16), sd((heads * 8, LANES), F32), sd((8, width), F32)]
        outs += more
        specs += [pl.BlockSpec((1, 4, width, LANES), lambda s: (order(s), 0, 0, 0)), whole(more[1]), whole(more[2])]
    return pl.pallas_call(
        functools.partial(attn_backward_kernel, direct), name="attn_backward", grid=(pairs,), out_shape=tuple(outs),
        in_specs=[whole(a) for a in args[:10]]
        + [pl.BlockSpec((images, 2, rp, keys), lambda s: (0, order(s), 0, 0))] + [whole(a) for a in args[11:]]
        + [ANY if n == 1 else whole(a) for n, a in enumerate(extra)],
        out_specs=specs, scratch_shapes=scratch,
        compiler_params=pltpu.CompilerParams(vmem_limit_bytes=62 * 2**20, **params),
    )(*args, *extra)


def pack(rows, count):
    width = rows[0].shape[0]
    return jnp.concatenate(rows + [jnp.zeros(((count - len(rows)) * width,), F32)]).reshape(count, width)


def shards(
    inputs, masked, key_valid, rel_index, mask_token, ln1_gain, ln1_bias, w_qkv, qv_bias, rel_table,
    w_proj, proj_bias, gamma1, ln2_gain, ln2_bias, w_fc1, fc1_bias, w_fc2, fc2_bias, gamma2, cotangent,
):
    images, rows, width = inputs.shape
    dp, hn = lax.axis_size("dp"), lax.axis_size("head")
    me, head = lax.axis_index("dp"), lax.axis_index("head")
    depth = dp // 4
    share = w_fc2.shape[0]
    ff = share * dp * hn
    entries, heads = rel_table.shape[0], rel_table.shape[1] * hn
    rp, keys = -(-rows // 16) * 16, -(-rows // LANES) * LANES
    direct = hn == 2 and dp == 16 and ff % (8 * share) == 0 and share % 16 == 0 and width % (16 * dp) == 0

    tab_rows = -(-entries // LANES)
    tab = jnp.pad(rel_table.T, ((0, 0), (0, tab_rows * LANES - entries)))
    mix = jnp.concatenate([tab.reshape(-1, LANES), qv_bias.reshape(-1, LANES)])
    vec = pack([mask_token, ln1_gain, ln1_bias, proj_bias, gamma1, ln2_gain, ln2_bias, fc2_bias, gamma2], 16)
    w3 = jnp.transpose(w_qkv, (1, 0, 2))

    if direct:
        spot_shape = (8, ff // 8)
        owner = (lax.broadcasted_iota(jnp.int32, spot_shape, 0) * (ff // 8) + lax.broadcasted_iota(jnp.int32, spot_shape, 1)) // share
        spot = jnp.where(owner == me * hn + head, jnp.tile(fc1_bias.astype(F32), ff // 8 // share)[None], 0.0)
        extra = (mix, w3, w_proj, w_fc1.T, w_fc2, spot)
        got = attn_forward(True, inputs, masked, key_valid, rel_index, vec, heads, extra, rp, keys, depth)
        normed, q, k, v, p, att, attn, res, n2, w, wp, w1, w2, b1 = got
        w1, w2, b1 = w1.reshape(ff, width), w2.reshape(ff, width), b1.reshape(1, ff)
    else:
        w = lax.all_gather(w3, "head", axis=2, tiled=True)
        wp = lax.all_gather(w_proj, "head", axis=0, tiled=True)
        w1 = lax.all_gather(w_fc1.T, ("dp", "head"), axis=0, tiled=True)
        w2 = lax.all_gather(w_fc2, ("dp", "head"), axis=0, tiled=True)
        b1 = lax.all_gather(fc1_bias, ("dp", "head"), axis=0, tiled=True).astype(F32)[None]
        extra = (lax.all_gather(mix, "head", axis=0), w, wp)
        got = attn_forward(False, inputs, masked, key_valid, rel_index, vec, heads, extra, rp, keys, depth)
        normed, q, k, v, p, att, attn, res, n2 = got

    steps = 4
    got = mlp(direct, n2, res, attn, cotangent, vec, b1, w1, w2, steps)
    gb1, out, dres, dproj, s2 = got[-5:]
    args = (inputs, masked, rel_index, vec, w, wp, normed, q, k, v, p, att, dres, dproj)
    if direct:
        extra = got[:3] + (s2, gb1.reshape(-1, width))
        gx, full, gff, small = attn_backward(True, args, heads, extra, rp, keys, depth)
        g_fc1, g_fc2 = gff[0], gff[1]
        full = full.reshape(4, width, -1).astype(F32)
        g_qkv, g_proj = full[:3], full[3].T
        s1, s2 = small[:8], small[8:16]
        wide = width // LANES
        tall = heads * 8 // wide
        table = jnp.transpose(small[16:16 + tall].reshape(tall, wide, LANES), (1, 0, 2)).reshape(heads, -1)
        g_b1 = small[16 + tall:].reshape(-1)
    else:
        ga, gb = got[:2]
        gx, gw, gt, s1 = attn_backward(False, args, heads, (), rp, keys, depth)
        g_fc1 = lax.psum_scatter(ga.astype(F32), ("dp", "head"), scatter_dimension=0, tiled=True)
        g_fc2 = lax.psum_scatter(gb.astype(F32), ("dp", "head"), scatter_dimension=0, tiled=True)
        full = lax.psum(lax.psum_scatter(gw.astype(F32), "head", scatter_dimension=0, tiled=True), "dp")
        full = jnp.transpose(full, (1, 2, 0, 3)).reshape(4, width, -1)
        g_qkv, g_proj = full[:3], full[3].T
        s1, s2, table, g_b1 = lax.psum((s1, s2, gt.reshape(heads, -1), gb1.reshape(-1)), ("dp", "head"))
    g_table = lax.dynamic_slice_in_dim(table, head * (heads // hn), heads // hn, 0)[:, :entries].T
    g_b1 = lax.dynamic_slice_in_dim(g_b1, (me * hn + head) * share, share)
    g_qvb = lax.dynamic_slice_in_dim(s1[T_QB:T_VB + 1], head * (width // hn), width // hn, 1)
    return (
        out, gx, s1[T_MASK], s1[T_LG1], s1[T_LB1], jnp.transpose(g_qkv, (1, 0, 2)), g_qvb, g_table, g_proj,
        s2[S_PB], s2[S_GA1], s2[S_LG2], s2[S_LB2], g_fc1.T, g_b1, g_fc2, s2[S_FB2], s2[S_GA2],
    )


def solution(mesh):
    in_specs = (
        P(("dp", "head"), None, None),
        P(("dp", "head"), None),
        P("dp", None),
        P(),
        P(),
        P(),
        P(),
        P(None, None, "head"),
        P(None, "head"),
        P(None, "head"),
        P("head", None),
        P(),
        P(),
        P(),
        P(),
        P(None, ("dp", "head")),
        P(("dp", "head")),
        P(("dp", "head"), None),
        P(),
        P(),
        P(("dp", "head"), None, None),
    )
    out_specs = (
        P(("dp", "head"), None, None),
        P(("dp", "head"), None, None),
        P(),
        P(),
        P(),
        P(None, None, "head"),
        P(None, "head"),
        P(None, "head"),
        P("head", None),
        P(),
        P(),
        P(),
        P(),
        P(None, ("dp", "head")),
        P(("dp", "head")),
        P(("dp", "head"), None),
        P(),
        P(),
    )
    return jax.shard_map(shards, mesh=mesh, in_specs=in_specs, out_specs=out_specs, check_vma=False)
```

```python
import functools
import types
import jax
import jax.numpy as jnp
from jax import lax
from jax.experimental import pallas as pl
from jax.experimental.pallas import tpu as pltpu
from jax.sharding import PartitionSpec as P

F32 = jnp.float32
BF16 = jnp.bfloat16
EPS = 1e-06
LANES = 128
S_GA2, S_FB2, S_LG2, S_LB2, S_GA1, S_PB = range(6)
T_MASK, T_LG1, T_LB1, T_QB, T_VB = range(5)


def dot(a, b):
    return jnp.dot(a, b, preferred_element_type=F32)


def dot_nt(a, b):
    return lax.dot_general(a, b, (((1,), (1,)), ((), ())), preferred_element_type=F32)


def dot_tn(a, b):
    return lax.dot_general(a, b, (((0,), (0,)), ((), ())), preferred_element_type=F32)


def norm_parts(v):
    c = v - jnp.mean(v, axis=-1, keepdims=True)
    r = lax.rsqrt(jnp.mean(c * c, axis=-1, keepdims=True) + EPS)
    return c * r, r


def norm_back(n, r, y, gain):
    yg = y * gain
    return r * (
        yg - jnp.mean(yg, axis=-1, keepdims=True) - n * jnp.mean(yg * n, axis=-1, keepdims=True)
    )


def low_half(shape):
    return lax.broadcasted_iota(jnp.int32, shape, 1) < (LANES // 2)

MESHID = pl.DeviceIdType.MESH


def here():
    dp = lax.axis_index("dp")
    return dp // 4, (dp // 2) % 2, dp % 2, lax.axis_index("head")


def at_dp(z, y, x):
    return {"dp": (z * 2 + y) * 2 + x}


def greet(depth):
    z, y, x, head = here()
    found = [at_dp(z, y, 1 - x), at_dp(z, 1 - y, x), {"head": 1 - head}]
    found += [at_dp((z + k) % depth, y, x) for k in range(1, depth)]
    barrier = pltpu.get_barrier_semaphore()
    for dev in found:
        pl.semaphore_signal(barrier, inc=1, device_id=dev, device_id_type=MESHID)
    pl.semaphore_wait(barrier, len(found))


class Wire:
    def __init__(self, send, recv):
        self.send, self.recv, self.next, self.open = send, recv, 0, []

    def slot(self):
        self.next += 1
        return self.next - 1

    def copy(self, i, src, dst, dev):
        return pltpu.make_async_remote_copy(
            src_ref=src, dst_ref=dst, send_sem=self.send.at[i], recv_sem=self.recv.at[i],
            device_id=dev, device_id_type=MESHID,
        )

    def start(self, i, make):
        self.copy(i, *make()).start()
        self.open.append((i, make))

    def arrived(self, i, ref, dev):
        self.copy(i, ref, ref, dev).wait_recv()

    def sent(self):
        for i, make in self.open:
            self.copy(i, *make()).wait_send()
        self.open = []


class Local:
    def __init__(self, sems):
        self.sems, self.next, self.open = sems, 0, []

    def start(self, make):
        i = self.next
        self.next += 1
        pltpu.make_async_copy(*make(), self.sems.at[i]).start()
        wait = lambda: pltpu.make_async_copy(*make(), self.sems.at[i]).wait()
        self.open.append(wait)
        return wait


def hops(p, y, x):
    ey, ex = (1 - y, x), (y, 1 - x)
    return (ey, ex) if p == 0 else (ex, ey)


def gather_stages(wire, depth, own, slot, column=None):
    z, y, x, head = here()
    ids = {}
    for p in range(2):
        for k in range(depth):
            for kind in "zabc":
                ids[p, kind, k] = wire.slot()
        for kind in range(0 if column is None else 4):
            ids[p, "s", kind] = wire.slot()
    up = lambda k: (z + k) % depth
    down = lambda k: (z + depth - k) % depth

    def columns(p):
        (ay, ax), (by, bx) = hops(p, y, x)
        return (y, x), (ay, ax), (by, bx), (1 - y, 1 - x)

    def send_up(p, k):
        wire.start(ids[p, "z", k], lambda: (own(p), slot(p, z, y, x), at_dp(up(k), y, x)))

    def send_square(p, k, kind, col, to, first=False):
        def make():
            cs = columns(p)
            dst = slot(p, down(k), *cs[col])
            return own(p) if first else dst, dst, at_dp(z, *cs[to])
        wire.start(ids[p, kind, k], make)

    def wait(p, k, kind, col, frm):
        cs = columns(p)
        dev = at_dp(down(k), y, x) if frm is None else at_dp(z, *cs[frm])
        wire.arrived(ids[p, kind, k], slot(p, down(k), *cs[col]), dev)

    def begin():
        for k in range(1, depth):
            for p in range(2):
                send_up(p, k)
        for p in range(2):
            send_square(p, 0, "a", 0, 1, True)
            send_square(p, 0, "b", 0, 2, True)

    def from_column(k):
        for p in range(2):
            wait(p, k, "z", 0, None)
            send_square(p, k, "a", 0, 1)
            send_square(p, k, "b", 0, 2)

    def from_first(k):
        for p in range(2):
            wait(p, k, "a", 1, 1)
            send_square(p, k, "c", 1, 2)

    def from_second(kind, col):
        for p in range(2):
            for k in range(depth):
                wait(p, k, kind, col, 2)

    def across(which):
        for p in range(2):
            def make(p=p):
                block = column(p, *columns(p)[which], head)
                return block, block, {"head": 1 - head}
            wire.start(ids[p, "s", which], make)

    def crossed():
        for which in range(4):
            for p in range(2):
                wire.arrived(ids[p, "s", which], column(p, *columns(p)[which], 1 - head), {"head": 1 - head})

    part = functools.partial
    stages = {"begin": begin, "b": part(from_second, "b", 2), "c": part(from_second, "c", 3), "crossed": crossed}
    for k in range(depth):
        stages["z%d" % k] = part(from_column, k)
        stages["a%d" % k] = part(from_first, k)
        stages["s%d" % k] = part(across, k)
    return stages


def add_into(dst, src):
    dst[...] = (dst[...].astype(F32) + src[...].astype(F32)).astype(dst.dtype)


class SquareSum:
    def __init__(self, wire, theirs, mine, pair_in, square_in, line_in):
        self.wire, self.theirs, self.mine = wire, theirs, mine
        self.pair_in, self.square_in, self.line_in = pair_in, square_in, line_in
        self.ids = {(p, kind): wire.slot() for p in range(2) for kind in "hab"}
        self.place = here()

    def devices(self, p):
        z, y, x, head = self.place
        ex, ey = at_dp(z, y, 1 - x), at_dp(z, 1 - y, x)
        return (ex, ey) if p == 0 else (ey, ex)

    def copy(self, p, kind):
        z, y, x, head = self.place
        if kind == "h":
            src, dst, dev = self.theirs(p), self.pair_in(p), {"head": 1 - head}
        elif kind == "a":
            src = self.mine(p, None, 1 - x) if p == 0 else self.mine(p, 1 - y, None)
            dst, dev = self.square_in(p), self.devices(p)[0]
        else:
            src = self.mine(p, 1 - y, x) if p == 0 else self.mine(p, y, 1 - x)
            dst, dev = self.line_in(p), self.devices(p)[1]
        return self.wire.copy(self.ids[p, kind], src, dst, dev)

    def pair(self):
        for p in range(2):
            self.copy(p, "h").start()

    def first(self):
        for p in range(2):
            self.wire.arrived(self.ids[p, "h"], self.pair_in(p), {"head": 1 - self.place[3]})
            add_into(self.mine(p, None, None), self.pair_in(p))
            self.copy(p, "a").start()

    def second(self):
        z, y, x, head = self.place
        for p in range(2):
            self.wire.arrived(self.ids[p, "a"], self.square_in(p), self.devices(p)[0])
            add_into(self.mine(p, None, x) if p == 0 else self.mine(p, y, None), self.square_in(p))
            self.copy(p, "b").start()

    def third(self):
        z, y, x, head = self.place
        for p in range(2):
            self.wire.arrived(self.ids[p, "b"], self.line_in(p), self.devices(p)[1])
            add_into(self.mine(p, y, x), self.line_in(p))

    def sent(self):
        for p in range(2):
            for kind in "hab":
                self.copy(p, kind).wait_send()


class ColumnSum:
    def __init__(self, wire, depth, part, column_in):
        self.wire, self.depth, self.part, self.column_in = wire, depth, part, column_in
        self.ids = {(p, k): wire.slot() for p in range(2) for k in range(1, depth)}
        self.place = here()

    def send(self, k):
        def make(p):
            z, y, x, head = self.place
            to = (z + self.depth - k) % self.depth
            return self.part(p, to), self.column_in(p, k), at_dp(to, y, x)

        for p in range(2):
            self.wire.start(self.ids[p, k], functools.partial(make, p))

    def total(self, p):
        z, y, x, head = self.place
        acc = self.part(p, z)[...].astype(F32)
        for k in range(1, self.depth):
            back = at_dp((z + k) % self.depth, y, x)
            self.wire.arrived(self.ids[p, k], self.column_in(p, k), back)
            acc = acc + self.column_in(p, k)[...].astype(F32)
        return acc


class SmallSum:
    def __init__(self, wire, depth, bufs, line):
        self.wire, self.depth, self.bufs, self.line = wire, depth, bufs, line
        self.ids = [wire.slot() for _ in range(2 + depth)]
        self.place = here()

    def devices(self):
        z, y, x, head = self.place
        return [{"head": 1 - head}, at_dp(z, y, 1 - x), at_dp(z, 1 - y, x)]

    def send(self, n):
        self.wire.start(self.ids[n], lambda: (self.bufs.at[2 * n], self.bufs.at[2 * n + 1], self.devices()[n]))

    def take(self, n):
        self.wire.arrived(self.ids[n], self.bufs.at[2 * n + 1], self.devices()[n])
        self.bufs[2 * n + 2] = self.bufs[2 * n] + self.bufs[2 * n + 1]

    def begin(self):
        self.send(0)

    def middle(self, n):
        self.take(n - 1)
        self.send(n)

    def column(self):
        z, y, x, head = self.place
        self.take(2)
        self.line[z] = self.bufs[6]
        for k in range(1, self.depth):
            self.wire.start(
                self.ids[2 + k],
                lambda k=k: (self.bufs.at[6], self.line.at[z], at_dp((z + k) % self.depth, y, x)),
            )

    def result(self):
        z, y, x, head = self.place
        for k in range(1, self.depth):
            back = (z + self.depth - k) % self.depth
            self.wire.arrived(self.ids[2 + k], self.line.at[back], at_dp(back, y, x))
        total = self.line[0]
        for n in range(1, self.depth):
            total = total + self.line[n]
        return total


def bind(names, refs):
    assert len(names) == len(refs)
    return types.SimpleNamespace(**dict(zip(names, refs)))


def spread_mask(masked, tmp, ch):
    images, rows = masked.shape
    tmp[...] = jnp.zeros_like(tmp)
    tmp[0:images, 0:rows] = masked[...].astype(F32)
    turned = tmp[...].T
    for i in range(images):
        ch[i] = turned[0:rows, i:i + 1]


def pad_index(raw, idx):
    idx[...] = jnp.zeros_like(idx)
    idx[0:raw.shape[0], 0:raw.shape[1]] = raw[...]


def run_all(stages):
    for stage in stages:
        stage()


def vmem(n):
    return [pl.BlockSpec(memory_space=pltpu.VMEM)] * n

ANY = pl.BlockSpec(memory_space=pl.ANY)
sd = jax.ShapeDtypeStruct
dma = lambda n: pltpu.SemaphoreType.DMA((n,))
VECTORS = ("mask_token", "ln1_gain", "ln1_bias", "proj_bias", "gamma1", "ln2_gain", "ln2_bias", "fc2_bias", "gamma2")
GIVEN = ("x", "masked", "kv", "raw") + VECTORS + ("cot",)
KEPT = (
    "idx", "valid", "tmp", "ch", "bias", "nt", "q", "k", "v", "att", "res", "n2", "db", "act", "dpre", "dn",
    "small1", "small2", "gb1", "lsem",
)
SHARED = (
    "w", "wp", "mix", "b1", "b1line", "g", "pair_in", "square_in", "line_in", "column", "column_in",
    "ar_pair", "ar_square", "ar_line", "ar_column", "gathered", "bufs", "line", "send", "recv",
)


class Row:
    def __init__(self, ref):
        self.ref = ref

    def __getitem__(self, at):
        return self.ref[...].reshape(1, -1)


def layer_kernel(direct, *refs):
    if direct:
        names = GIVEN + ("mixown", "wown", "wpown", "own1", "own2", "spot")
        names += ("out", "gx", "p", "w1", "w2", "full", "gff", "small") + KEPT + SHARED
    else:
        names = GIVEN + ("mix", "w", "wp", "w1", "w2", "b1")
        names += ("out", "gx", "p", "g1", "g2", "gw", "gt", "small1_out", "small2_out", "gb1_out") + KEPT
    r = bind(names, refs)
    for name in VECTORS:
        setattr(r, name, Row(getattr(r, name)))
    images, rows, width = r.x.shape
    heads, rp, keys = r.bias.shape
    flat = images * rp
    scale = (width // heads) ** -0.5
    pairs, per = heads // 2, heads // 4
    steps, block = r.b1.shape[-2:]
    own_heads = heads // r.mix.shape[0]
    own_tiles = width // r.mix.shape[0] // LANES
    chunks = (r.mix.shape[1] - 2 * own_tiles) // own_heads
    local = Local(r.lsem)
    z, y, x, head = here()
    plan = {}
    part = functools.partial
    every = lambda v: slice(None) if v is None else v
    level = lambda b: (z + 2 * steps - 1 - b) % steps
    at_image = lambda i: pl.multiple_of(i * rp, 16)

    if direct:
        depth = r.w1.shape[0]
        half = r.wown.shape[2]
        lanes_of = lambda hd: pl.ds(pl.multiple_of(hd * half, LANES), half)
        full = (r.w1, r.w2)
        wire = Wire(r.send, r.recv)
        greet(depth)
        other = {"head": 1 - head}
        swaps = [
            (r.mixown, lambda hd: r.mix.at[hd]),
            (r.wown, lambda hd: r.w.at[:, :, lanes_of(hd)]),
            (r.wpown, lambda hd: r.wp.at[lanes_of(hd)]),
        ]
        swap_ids = [wire.slot() for _ in swaps]
        for i, (src, place) in zip(swap_ids, swaps):
            wire.start(i, lambda src=src, place=place: (src, place(head), other))
        for src, place in swaps:
            local.start(lambda src=src, place=place: (src, place(head)))
        slot = lambda p, zz, yy, xx: full[p].at[zz, yy, xx, head]
        own = (r.own1, r.own2)
        for p in range(2):
            local.start(lambda p=p: (own[p], slot(p, z, y, x)))
        r.b1[0] = r.spot[...]
        bias_sum = SmallSum(wire, depth, r.b1, r.b1line)
        ag = gather_stages(
            wire, depth, own=lambda p: own[p], slot=slot,
            column=lambda p, yy, xx, hd: full[p].at[:, yy, xx, hd],
        )
        ag["begin"]()
        bias_sum.begin()
        squares = [
            SquareSum(
                wire,
                theirs=lambda p, b=b: r.g.at[b % 2, p, :, :, 1 - head],
                mine=lambda p, yy, xx, b=b: r.g.at[b % 2, p, every(yy), every(xx), head],
                pair_in=lambda p, b=b: r.pair_in.at[b % 2, p],
                square_in=lambda p, b=b: r.square_in.at[b % 2, p],
                line_in=lambda p, b=b: r.line_in.at[b % 2, p],
            )
            for b in range(steps)
        ]
        column = ColumnSum(wire, depth, part=lambda p, zz: r.column.at[p, zz], column_in=lambda p, k: r.column_in.at[p, k - 1])

        def close(b):
            squares[b].third()
            for p in range(2):
                r.column[p, level(b)] = r.g[b % 2, p, y, x, head]
            if b < steps - 1:
                column.send(b + 1)
            squares[b].sent()

        small = SmallSum(wire, depth, r.bufs, r.line)
        plan = {
            "g1": [ag["z1"], ag["a0"]], "g2": [part(bias_sum.middle, 1)],
            "p1": [ag["z2"], ag["a1"], part(bias_sum.middle, 2)],
            "t1": [ag["z3"], ag["a2"], ag["s0"], bias_sum.column], "t4": [ag["a3"], ag["s1"]],
            "t5": [ag["b"], ag["s2"]], "t6": [ag["c"], ag["s3"]],
        }

    def tick(point):
        run_all(plan.get(point, ()))

    def tick_in(step, point):
        for key, stages in plan.items():
            if isinstance(key, tuple) and key[1] == point:
                pl.when(step == key[0])(part(run_all, stages))

    spread_mask(r.masked, r.tmp, r.ch)
    pad_index(r.raw, r.idx)
    r.valid[...] = jnp.zeros_like(r.valid)
    r.valid[0:r.kv.shape[0], 0:rows] = r.kv[...]

    def hidden_of(i):
        ch = r.ch[i]
        return r.x[i].astype(F32) * (1.0 - ch) + ch * r.mask_token[...]

    def attention_forward(normed, pring):
        normed[...] = jnp.zeros_like(normed)
        r.n2[...] = jnp.zeros_like(r.n2)
        r.res[...] = jnp.zeros_like(r.res)

        def first_norm(i, carry):
            n, _ = norm_parts(hidden_of(i))
            normed[pl.ds(at_image(i), rows), :] = (n * r.ln1_gain[...] + r.ln1_bias[...]).astype(BF16)
            return carry

        lax.fori_loop(0, images, first_norm, 0)
        if direct:
            for wait in local.open:
                wait()
            local.open = []
            wire.arrived(swap_ids[0], swaps[0][1](1 - head), other)

        def gather_head(h, carry):
            for side in range(keys // LANES):
                idx = r.idx[:, side * LANES:(side + 1) * LANES]
                low = idx & (LANES - 1)
                high = idx >> 7
                acc = jnp.zeros(idx.shape, F32)
                for c in range(chunks):
                    row = r.mix[h // own_heads, pl.ds((h % own_heads) * chunks + c, 1), :]
                    got = jnp.take_along_axis(jnp.broadcast_to(row, idx.shape), low, axis=1)
                    acc = jnp.where(high == c, got, acc)
                r.bias[h, :, side * LANES:(side + 1) * LANES] = acc
            return carry

        for n in range(3):
            lax.fori_loop(n * heads // 3, (n + 1) * heads // 3, gather_head, 0)
            tick("g%d" % n)
        if direct:
            for n in (1, 2):
                wire.arrived(swap_ids[n], swaps[n][1](1 - head), other)
        zeros_tail = jnp.zeros((images, keys - rp, width), BF16)
        r.k[:, rp:, :] = zeros_tail
        r.v[:, rp:, :] = zeros_tail

        def bias_row(kind, nb):
            tiles = []
            for t in (2 * nb, 2 * nb + 1):
                at = own_heads * chunks + kind * own_tiles + t % own_tiles
                tiles.append(r.mix[t // own_tiles, at:at + 1, :])
            return jnp.concatenate(tiles, axis=1)

        for c, (dst, kind) in enumerate(((r.q, 0), (r.k, None), (r.v, 1))):
            for nb in range(width // 256):
                cols = slice(nb * 256, (nb + 1) * 256)
                acc = dot(normed[...], r.w[c, :, cols])
                if kind is not None:
                    acc = acc + bias_row(kind, nb)
                acc = acc.astype(BF16)
                for i in range(images):
                    dst[i, :rp, cols] = acc[i * rp:(i + 1) * rp]
            tick("p%d" % c)
        r.nt[...] = normed[...].T

        def attend(t, carry):
            i = t // pairs
            j = t % pairs
            lanes = pl.ds(pl.multiple_of(j * LANES, LANES), LANES)
            qp = r.q[i, :, lanes]
            kp = r.k[i, :, lanes]
            vp = r.v[i, :, lanes]
            lo = low_half((rp, LANES))
            ok = r.valid[pl.ds(head * images + i, 1), :] > 0
            outs = []
            for s in range(2):
                qs = jnp.where(lo if s == 0 else jnp.logical_not(lo), qp, jnp.zeros_like(qp))
                sc = dot_nt(qs, kp) * scale + r.bias[2 * j + s]
                sc = jnp.where(ok, sc, -1e30)
                e = jnp.exp(sc - jnp.max(sc, axis=-1, keepdims=True))
                prob = e * (1.0 / jnp.sum(e, axis=-1, keepdims=True))
                pring[i % 2, 2 * j + s] = prob
                outs.append(dot(prob.astype(BF16), vp))
            r.att[pl.ds(at_image(i), rp), lanes] = jnp.where(lo, outs[0], outs[1]).astype(BF16)
            return carry

        stored = {}
        for n in range(2 * images):
            i = n // 2
            if n % 2 == 0 and i >= 2:
                stored[i - 2]()
            lax.fori_loop(n * pairs // 2, (n + 1) * pairs // 2, attend, 0)
            if n % 2:
                stored[i] = local.start(lambda i=i: (pring.at[i % 2], r.p.at[i]))
            tick("t%d" % n)

        def finish(i, carry):
            branch = dot(r.att[pl.ds(at_image(i), rp), :], r.wp[...]) + r.proj_bias[...]
            res = hidden_of(i) + r.gamma1[...] * branch[:rows]
            r.res[pl.ds(at_image(i), rows), :] = res
            n, _ = norm_parts(res)
            r.n2[pl.ds(at_image(i), rows), :] = (n * r.ln2_gain[...] + r.ln2_bias[...]).astype(BF16)
            return carry

        lax.fori_loop(0, images, finish, 0)
        stored[images - 2]()
        stored[images - 1]()

    pl.run_scoped(attention_forward, pltpu.VMEM((flat, width), BF16), pltpu.VMEM((2, heads, rp, keys), F32))

    if direct:
        ag["crossed"]()
        r.b1[1] = bias_sum.result()
        plan = {
            (0, 4): [squares[0].pair],
            (1, 1): [squares[0].first], (1, 4): [squares[1].pair, squares[0].second],
            (2, 1): [squares[1].first], (2, 2): [part(close, 0)], (2, 4): [squares[2].pair, squares[1].second],
            (3, 1): [squares[2].first], (3, 2): [part(close, 1)], (3, 4): [squares[3].pair, squares[2].second],
        }

    def feed_forward(cot, out, branch, slots, sems):
        def weights(b, into):
            copies = []
            for p, src in enumerate((r.w1, r.w2)):
                if direct:
                    view = src.at[level(b)]
                else:
                    view = src.at[pl.ds(pl.multiple_of(level(b) * block, 16), block)]
                copies.append(pltpu.make_async_copy(view, slots.at[into, p], sems.at[into, p]))
            return copies

        for copy in weights(0, 0):
            copy.start()
        fetch = pltpu.make_async_copy(r.cot, cot, sems.at[2, 0])
        fetch.start()
        r.db[...] = jnp.zeros_like(r.db)
        branch[...] = jnp.zeros_like(branch)
        r.dn[...] = jnp.zeros_like(r.dn)
        fetch.wait()

        def fill(i, carry):
            r.db[pl.ds(at_image(i), rows), :] = (cot[i].astype(F32) * r.gamma2[...]).astype(BF16)
            return carry

        lax.fori_loop(0, images, fill, 0)

        def step(b, carry):
            slot = b % 2
            t = level(b)
            for copy in weights(b, slot):
                copy.wait()

            @pl.when(b + 1 < steps)
            def _():
                for copy in weights(b + 1, 1 - slot):
                    copy.start()

            w1 = lambda: slots[slot, 0].reshape(block, width)
            w2 = lambda: slots[slot, 1].reshape(block, width)
            b1 = r.b1[1, pl.ds(t, 1), :] if direct else r.b1[pl.ds(t, 1), :]

            def tile(i, gb1):
                at = pl.ds(at_image(i), rp)
                pre = dot_nt(r.n2[at, :], w1()) + b1
                cdf = 0.5 * (1.0 + lax.erf(pre * 0.7071067811865476))
                slope = cdf + pre * (0.3989422804014327 * jnp.exp(-0.5 * pre * pre))
                act = (pre * cdf).astype(BF16)
                r.act[at, :] = act
                dpre = (dot_nt(r.db[at, :], w2()) * slope).astype(BF16)
                r.dpre[at, :] = dpre
                branch[at, :] += dot(act, w2())
                r.dn[at, :] += dot(dpre, w1())
                return gb1 + jnp.sum(dpre.astype(F32), axis=0, keepdims=True)

            gb1 = lax.fori_loop(0, images // 2, tile, jnp.zeros((1, block), F32))
            tick_in(b, 1)
            r.gb1[pl.ds(t, 1), :] = lax.fori_loop(images // 2, images, tile, gb1)
            tick_in(b, 2)

            def store(p, value):
                value = value.astype(BF16)
                if direct:
                    r.g[slot, p] = value.reshape(r.g.shape[2:])
                else:
                    slots[slot, p] = value
                    dst = (r.g1, r.g2)[p].at[pl.ds(pl.multiple_of(t * block, 16), block)]
                    copy = pltpu.make_async_copy(slots.at[slot, p], dst, sems.at[3, p])
                    copy.start()
                    copy.wait()

            second = dot_tn(r.act[...], r.db[...])
            store(1, second)
            tick_in(b, 3)
            store(0, dot_tn(r.dpre[...], r.n2[...]))
            tick_in(b, 4)
            return carry

        lax.fori_loop(0, steps, step, 0)
        r.small2[...] = jnp.zeros_like(r.small2)
        r.n2[...] = jnp.zeros_like(r.n2)

        def add(row, value):
            r.small2[row:row + 1, :] += jnp.sum(value, axis=0, keepdims=True)

        def finish(i, carry):
            span = pl.ds(at_image(i), rows)
            up = cot[i].astype(F32)
            mlp = branch[span, :] + r.fc2_bias[...]
            res = r.res[span, :]
            out[i] = (res + r.gamma2[...] * mlp).astype(BF16)
            add(S_GA2, up * mlp)
            add(S_FB2, (up * r.gamma2[...]).astype(BF16).astype(F32))
            n, inv = norm_parts(res)
            dn = r.dn[span, :]
            add(S_LG2, dn * n)
            add(S_LB2, dn)
            dres = up + norm_back(n, inv, dn, r.ln2_gain[...])
            add(S_GA1, dres * (res - hidden_of(i)))
            r.res[span, :] = dres
            dproj = (dres * r.gamma1[...]).astype(BF16)
            r.n2[span, :] = dproj
            add(S_PB, dproj.astype(F32))
            return carry

        lax.fori_loop(0, images, finish, 0)
        r.small2[S_GA1:S_GA1 + 1, :] = r.small2[S_GA1:S_GA1 + 1, :] / r.gamma1[...]
        store_out = pltpu.make_async_copy(out, r.out, sems.at[2, 1])
        store_out.start()
        store_out.wait()

    if direct:
        slots_shape = (2, 2) + r.w1.shape[1:]
    else:
        slots_shape = (2, 2, block, width)
    pl.run_scoped(
        feed_forward, pltpu.VMEM(r.cot.shape, BF16), pltpu.VMEM(r.cot.shape, BF16), pltpu.VMEM((flat, width), F32),
        pltpu.VMEM(slots_shape, BF16), pltpu.SemaphoreType.DMA((4, 2)),
    )
    plan = {}

    def attention_backward(pbuf, dpt, dv_all, g, sems):
        nonlocal plan
        dqkv = (r.act, r.dpre, dv_all)
        pair_of = lambda s: (s % 2) * per + s // 2

        def fetch(s, into):
            src = r.p.at[:, pl.ds(2 * pair_of(s), 2)]
            return pltpu.make_async_copy(src, pbuf.at[into], sems.at[into])

        fetch(0, 0).start()
        if direct:
            ar, lines, gathers = [], [], []
            for m in range(per):
                ar.append(SquareSum(
                    wire,
                    theirs=lambda p, m=m: g.at[m, 1 - head, p],
                    mine=lambda p, yy, xx, m=m: g.at[m, head, p, :, :, every(yy), every(xx)],
                    pair_in=lambda p, m=m: r.ar_pair.at[m, p],
                    square_in=lambda p, m=m: r.ar_square.at[m, p], line_in=lambda p, m=m: r.ar_line.at[m, p],
                ))
                lines.append(ColumnSum(
                    wire, depth, part=lambda p, zz, m=m: g.at[m, head, p, :, zz, y, x],
                    column_in=lambda p, k, m=m: r.ar_column.at[m, p, k - 1],
                ))
                lanes_m = slice(m * LANES, (m + 1) * LANES)
                into = lambda p, zz, yy, xx, lanes_m=lanes_m: r.gathered.at[p, :, zz, yy, xx, :, lanes_m]
                gathers.append(gather_stages(wire, depth, own=lambda p, into=into: into(p, z, y, x), slot=into))

            def third(m):
                ar[m].third()
                for k in range(1, depth):
                    lines[m].send(k)

            def last(m):
                for p in range(2):
                    r.gathered[p, :, z, y, x, :, m * LANES:(m + 1) * LANES] = lines[m].total(p).astype(BF16)
                gathers[m]["begin"]()

            def ff_last():
                for p in range(2):
                    r.gff[p] = column.total(p)

            g0, g1, g2 = gathers
            plan = {
                (0, 1): [squares[3].first, part(close, 2)], (0, 4): [squares[3].second], (1, 3): [part(close, 3)],
                (1, 4): [ar[0].pair], (2, 3): [ar[0].first], (3, 4): [ar[1].pair, ar[0].second],
                (4, 3): [ar[1].first], (4, 4): [part(third, 0)],
                (5, 4): [ar[2].pair, ar[1].second, part(last, 0)],
                (5, 6): [ar[2].first, part(third, 1)], (5, 7): [g0["z1"], g0["z2"], g0["z3"]], (5, 8): [part(last, 1)],
                (5, 9): [ar[2].second, g0["a0"], g0["a1"], g0["a2"], g0["a3"]], (5, 10): [g1["z1"], g1["z2"], g1["z3"]],
                (5, 11): [part(third, 2), g0["b"], g0["c"]], (5, 12): [g1["a0"], g1["a1"], g1["a2"], g1["a3"]], (5, 13): [ff_last],
            }

        for i in range(images):
            at = slice(i * rp, (i + 1) * rp)
            r.db[at, :] = dot_nt(r.n2[at, :], r.wp[...]).astype(BF16)
        dpt[...] = r.n2[...].T
        r.small1[...] = jnp.zeros_like(r.small1)

        def step(s, carry):
            j = pair_of(s)
            now = s % 2
            fetch(s, now).wait()

            @pl.when(s + 1 < pairs)
            def _():
                fetch(s + 1, 1 - now).start()

            tick_in(s, 1)
            lanes = pl.ds(pl.multiple_of(j * LANES, LANES), LANES)
            r.bias[2 * j] = jnp.zeros((rp, keys), F32)
            r.bias[2 * j + 1] = jnp.zeros((rp, keys), F32)

            def image(i, carry):
                at = pl.ds(at_image(i), rp)
                qp = r.q[i, :, lanes]
                kp = r.k[i, :, lanes]
                vp = r.v[i, :, lanes]
                da = r.db[at, lanes]
                lo = low_half((rp, LANES))
                dv, dq, dk = [], [], []
                for n in range(2):
                    das = jnp.where(lo if n == 0 else jnp.logical_not(lo), da, jnp.zeros_like(da))
                    prob = pbuf[now, i, n]
                    dp = dot_nt(das, vp)
                    dsc = prob * (dp - jnp.sum(prob * dp, axis=-1, keepdims=True))
                    dsb = dsc.astype(BF16)
                    r.bias[2 * j + n] += dsb.astype(F32)
                    dv.append(dot_tn(prob.astype(BF16), da))
                    dq.append(dot(dsb, kp))
                    dk.append(dot_tn(dsb, qp))
                lok = low_half((keys, LANES))
                dqkv[0][at, lanes] = (jnp.where(lo, dq[0], dq[1]) * scale).astype(BF16)
                dqkv[1][at, lanes] = (jnp.where(lok, dk[0], dk[1]) * scale)[:rp].astype(BF16)
                dqkv[2][at, lanes] = jnp.where(lok, dv[0], dv[1])[:rp].astype(BF16)
                return carry

            lax.fori_loop(0, images // 2, image, 0)
            tick_in(s, 2)
            lax.fori_loop(images // 2, images, image, 0)
            tick_in(s, 3)

            def store(c, value):
                value = value.astype(BF16)
                if direct:
                    g[s // 2, s % 2, c // 2, c % 2] = value.reshape(g.shape[4:])
                else:
                    g[...] = value
                    copy = pltpu.make_async_copy(g, r.gw.at[j, c], sems.at[2])
                    copy.start()
                    copy.wait()

            for c in range(3):
                store(c, dot(r.nt[...], dqkv[c][:, lanes]))
            store(3, dot(dpt[...], r.att[:, lanes]))
            tick_in(s, 4)
            return carry

        lax.fori_loop(0, pairs, step, 0)
        now = lambda point: run_all(plan.get((pairs - 1, point), ()))

        def total_rows(row, c):
            def add(i, acc):
                return acc + jnp.sum(dqkv[c][pl.ds(at_image(i), rp), :].astype(F32), axis=0, keepdims=True)
            r.small1[row:row + 1, :] = lax.fori_loop(0, images, add, jnp.zeros((1, width), F32))

        total_rows(T_QB, 0)
        total_rows(T_VB, 2)

        def finish(i, carry):
            span = pl.ds(at_image(i), rp)
            dn = dot_nt(dqkv[0][span, :], r.w[0])
            dn += dot_nt(dqkv[1][span, :], r.w[1])
            dn += dot_nt(dqkv[2][span, :], r.w[2])
            dn = dn[:rows]
            ch = r.ch[i]
            n, inv = norm_parts(hidden_of(i))
            dh = r.res[pl.ds(at_image(i), rows), :] + norm_back(n, inv, dn, r.ln1_gain[...])
            r.dn[pl.ds(at_image(i), rows), :] = dh * (1.0 - ch)
            for row, value in ((T_MASK, dh * ch), (T_LG1, dn * n), (T_LB1, dn)):
                r.small1[row:row + 1, :] += jnp.sum(value, axis=0, keepdims=True)
            return carry

        leaving = []
        for i in range(images):
            lax.fori_loop(i, i + 1, finish, 0)
            leaving.append(local.start(lambda i=i: (r.dn.at[pl.ds(i * rp, rows)], r.gx.at[i])))
            now(5 + i)

        a_iota = lax.broadcasted_iota(jnp.int32, (8, keys), 0)
        b_iota = lax.broadcasted_iota(jnp.int32, (LANES, keys), 0)

        def scatter(t, acc):
            at = pl.ds(pl.multiple_of(t * 8, 8), 8)
            idx = r.idx[at, :]
            high, low = idx >> 7, idx & (LANES - 1)
            tiles = [r.bias[h, at, :] for h in range(heads)]
            lefts, rests, ones = [], [], []
            for n in range(8):
                pick = jnp.broadcast_to(high[n:n + 1], (8, keys)) == a_iota
                ones.append((jnp.broadcast_to(low[n:n + 1], (LANES, keys)) == b_iota).astype(F32).astype(BF16))
                left = jnp.concatenate(
                    [jnp.where(pick, jnp.broadcast_to(tile[n:n + 1], (8, keys)), 0.0) for tile in tiles], axis=0)
                top = left.astype(BF16)
                lefts.append(top)
                rests.append((left - top.astype(F32)).astype(BF16))
            one = jnp.concatenate(ones, axis=1)
            return acc + dot_nt(jnp.concatenate(lefts, axis=1), one) + dot_nt(jnp.concatenate(rests, axis=1), one)

        table = jnp.zeros((heads * 8, LANES), F32)
        blocks = rp // 8
        for n in range(5):
            table = lax.fori_loop(n * blocks // 5, (n + 1) * blocks // 5, scatter, table)
            now(9 + n)
        for wait in leaving:
            wait()
        if not direct:
            r.gt[...] = table
            r.small1_out[...] = r.small1[...]
            r.small2_out[...] = r.small2[...]
            r.gb1_out[...] = r.gb1[...]
            return
        wide = width // LANES
        tall = heads * 8 // wide
        r.bufs[0, 0:8] = r.small1[...]
        r.bufs[0, 8:16] = r.small2[...]
        at = 16
        for t in range(wide):
            r.bufs[0, at:at + tall, t * LANES:(t + 1) * LANES] = table[t * tall:(t + 1) * tall]
        at += tall
        r.bufs[0, at:at + steps] = r.gb1[...]
        small.begin()
        last(2)
        small.middle(1)
        run_all([g1["b"], g1["c"]])
        run_all(g2["z%d" % k] for k in range(1, depth))
        small.middle(2)
        run_all(g2["a%d" % k] for k in range(depth))
        small.column()
        run_all([g2["b"], g2["c"]])
        keep = local.start(lambda: (r.gathered, r.full))
        r.small[...] = small.result()
        for m in range(per):
            ar[m].sent()
        wire.sent()
        keep()

    if direct:
        g_shape = (per, 2, 2, 2, depth, 2, 2) + r.gathered.shape[5:6] + (LANES,)
    else:
        g_shape = (width, LANES)
    pl.run_scoped(
        attention_backward, pltpu.VMEM((2, images, 2, rp, keys), F32), pltpu.VMEM((width, flat), BF16),
        pltpu.VMEM((flat, width), BF16), pltpu.VMEM(g_shape, BF16), dma(3),
    )


def layer(direct, given, extra, heads, rp, keys, depth):
    x, kv = given[0], given[2]
    images, rows, width = x.shape
    flat = images * rp
    tall = -(-max(kv.shape[0], images) // 8) * 8
    steps = 4
    ff = extra[-1].size
    outs = [sd(x.shape, BF16), sd(x.shape, F32), sd((images, heads, rp, keys), F32)]
    out_specs = [ANY] * 3
    bf = lambda *shape: pltpu.VMEM(shape, BF16)
    fl = lambda *shape: pltpu.VMEM(shape, F32)
    scratch = [
        pltpu.VMEM((rp, keys), jnp.int32), pltpu.VMEM((tall, keys), jnp.int32), fl(tall, keys), fl(images, rows, 1),
        fl(heads, rp, keys), bf(width, flat), bf(images, rp, width), bf(images, keys, width), bf(images, keys, width),
        bf(flat, width), fl(flat, width), bf(flat, width), bf(flat, width), bf(flat, width), bf(flat, width),
        fl(flat, width), fl(8, width), fl(8, width), fl(steps, ff // steps), dma(24),
    ]
    in_specs = vmem(len(given) - 1) + [ANY]
    params = {}
    if direct:
        mixown, wown, wpown, own1, own2, spot = extra
        per = heads // 4
        share = own1.shape[0]
        own = width // (4 * depth)
        total = 16 + heads * 8 * LANES // width + steps
        big = sd((depth, 2, 2, 2) + own1.shape, BF16)
        outs += [big, big, sd((2, 2, depth, 2, 2, own, per * LANES), BF16), sd((2, share, width), F32), sd((total, width), F32)]
        in_specs += vmem(6)
        out_specs += [ANY] * 3 + vmem(2)
        n = 3 + 2 * (4 * depth + 4) + 2 + depth + 6 * steps + 2 * (depth - 1)
        n += per * (6 + 2 * (depth - 1) + 8 * depth) + 2 + depth
        scratch += [
            bf(3, width, width), bf(width, width), fl(2, *mixown.shape), fl(7, *spot.shape), fl(depth, *spot.shape),
            bf(2, 2, 2, 2, 2, share, width), bf(2, 2, 2, 2, share, width), bf(2, 2, 2, share, width), bf(2, 2, share, width),
            bf(2, depth, share, width), bf(2, depth - 1, share, width),
            bf(per, 2, 2, depth, 2, 2, own, LANES), bf(per, 2, 2, depth, 2, own, LANES), bf(per, 2, 2, depth, own, LANES),
            bf(per, 2, depth - 1, 2, own, LANES), bf(2, 2, depth, 2, 2, own, per * LANES),
            fl(7, total, width), fl(depth, total, width), dma(n), dma(n),
        ]
        params = dict(collective_id=1, has_side_effects=True)
    else:
        part = sd((ff, width), BF16)
        outs += [part, part, sd((heads // 2, 4, width, LANES), BF16), sd((heads * 8, LANES), F32)]
        outs += [sd((8, width), F32), sd((8, width), F32), sd((steps, ff // steps), F32)]
        in_specs += vmem(3) + [ANY, ANY] + vmem(1)
        out_specs += [ANY] * 3 + vmem(4)
    return pl.pallas_call(
        functools.partial(layer_kernel, direct), name="layer",
        out_shape=tuple(outs), in_specs=in_specs, out_specs=out_specs, scratch_shapes=scratch,
        compiler_params=pltpu.CompilerParams(vmem_limit_bytes=63 * 2**20, **params),
    )(*given, *extra)


def shards(
    inputs, masked, key_valid, rel_index, mask_token, ln1_gain, ln1_bias, w_qkv, qv_bias, rel_table,
    w_proj, proj_bias, gamma1, ln2_gain, ln2_bias, w_fc1, fc1_bias, w_fc2, fc2_bias, gamma2, cotangent,
):
    images, rows, width = inputs.shape
    dp, hn = lax.axis_size("dp"), lax.axis_size("head")
    me, head = lax.axis_index("dp"), lax.axis_index("head")
    depth = dp // 4
    share = w_fc2.shape[0]
    ff = share * dp * hn
    entries, heads = rel_table.shape[0], rel_table.shape[1] * hn
    rp, keys = -(-rows // 16) * 16, -(-rows // LANES) * LANES
    direct = hn == 2 and dp == 16 and share % 16 == 0 and width % (16 * dp) == 0

    tab_rows = -(-entries // LANES)
    tab = jnp.pad(rel_table.T, ((0, 0), (0, tab_rows * LANES - entries)))
    mix = jnp.concatenate([tab.reshape(-1, LANES), qv_bias.reshape(-1, LANES)])
    vectors = (mask_token, ln1_gain, ln1_bias, proj_bias, gamma1, ln2_gain, ln2_bias, fc2_bias, gamma2)
    given = (inputs, masked, key_valid, rel_index) + vectors + (cotangent,)
    w3 = jnp.transpose(w_qkv, (1, 0, 2))
    if direct:
        spot_shape = (4, ff // 4)
        owner = (lax.broadcasted_iota(jnp.int32, spot_shape, 0) * (ff // 4) + lax.broadcasted_iota(jnp.int32, spot_shape, 1)) // share
        spot = jnp.where(owner == me * hn + head, jnp.tile(fc1_bias.astype(F32), ff // 4 // share)[None], 0.0)
        extra = (mix, w3, w_proj, w_fc1.T, w_fc2, spot)
        out, gx, _, _, _, full, gff, small = layer(True, given, extra, heads, rp, keys, depth)
        g_fc1, g_fc2 = gff[0], gff[1]
        full = full.reshape(4, width, -1).astype(F32)
        s1, s2 = small[:8], small[8:16]
        wide = width // LANES
        tall = heads * 8 // wide
        table = jnp.transpose(small[16:16 + tall].reshape(tall, wide, LANES), (1, 0, 2)).reshape(heads, -1)
        g_b1 = small[16 + tall:].reshape(-1)
    else:
        w = lax.all_gather(w3, "head", axis=2, tiled=True)
        wp = lax.all_gather(w_proj, "head", axis=0, tiled=True)
        w1 = lax.all_gather(w_fc1.T, ("dp", "head"), axis=0, tiled=True)
        w2 = lax.all_gather(w_fc2, ("dp", "head"), axis=0, tiled=True)
        b1 = lax.all_gather(fc1_bias, ("dp", "head"), axis=0, tiled=True).astype(F32).reshape(4, -1)
        extra = (lax.all_gather(mix, "head", axis=0), w, wp, w1, w2, b1)
        out, gx, _, ga, gb, gw, gt, s1, s2, gb1 = layer(False, given, extra, heads, rp, keys, depth)
        g_fc1 = lax.psum_scatter(ga.astype(F32), ("dp", "head"), scatter_dimension=0, tiled=True)
        g_fc2 = lax.psum_scatter(gb.astype(F32), ("dp", "head"), scatter_dimension=0, tiled=True)
        full = lax.psum(lax.psum_scatter(gw.astype(F32), "head", scatter_dimension=0, tiled=True), "dp")
        full = jnp.transpose(full, (1, 2, 0, 3)).reshape(4, width, -1)
        s1, s2, table, g_b1 = lax.psum((s1, s2, gt.reshape(heads, -1), gb1.reshape(-1)), ("dp", "head"))
    g_qkv, g_proj = full[:3], full[3].T
    g_table = lax.dynamic_slice_in_dim(table, head * (heads // hn), heads // hn, 0)[:, :entries].T
    g_b1 = lax.dynamic_slice_in_dim(g_b1, (me * hn + head) * share, share)
    g_qvb = lax.dynamic_slice_in_dim(s1[T_QB:T_VB + 1], head * (width // hn), width // hn, 1)
    return (
        out, gx, s1[T_MASK], s1[T_LG1], s1[T_LB1], jnp.transpose(g_qkv, (1, 0, 2)), g_qvb, g_table, g_proj,
        s2[S_PB], s2[S_GA1], s2[S_LG2], s2[S_LB2], g_fc1.T, g_b1, g_fc2, s2[S_FB2], s2[S_GA2],
    )


def solution(mesh):
    in_specs = (
        P(("dp", "head"), None, None),
        P(("dp", "head"), None),
        P("dp", None),
        P(),
        P(),
        P(),
        P(),
        P(None, None, "head"),
        P(None, "head"),
        P(None, "head"),
        P("head", None),
        P(),
        P(),
        P(),
        P(),
        P(None, ("dp", "head")),
        P(("dp", "head")),
        P(("dp", "head"), None),
        P(),
        P(),
        P(("dp", "head"), None, None),
    )
    out_specs = (
        P(("dp", "head"), None, None),
        P(("dp", "head"), None, None),
        P(),
        P(),
        P(),
        P(None, None, "head"),
        P(None, "head"),
        P(None, "head"),
        P("head", None),
        P(),
        P(),
        P(),
        P(),
        P(None, ("dp", "head")),
        P(("dp", "head")),
        P(("dp", "head"), None),
        P(),
        P(),
    )
    return jax.shard_map(shards, mesh=mesh, in_specs=in_specs, out_specs=out_specs, check_vma=False)
```

```python
import functools
import types
import jax
import jax.numpy as jnp
from jax import lax
from jax.experimental import pallas as pl
from jax.experimental.pallas import tpu as pltpu
from jax.sharding import PartitionSpec as P

F32 = jnp.float32
BF16 = jnp.bfloat16
EPS = 1e-06
LANES = 128
S_GA2, S_FB2, S_LG2, S_LB2, S_GA1, S_PB = range(6)
T_MASK, T_LG1, T_LB1, T_QB, T_VB = range(5)


def dot(a, b):
    return jnp.dot(a, b, preferred_element_type=F32)


def dot_nt(a, b):
    return lax.dot_general(a, b, (((1,), (1,)), ((), ())), preferred_element_type=F32)


def dot_tn(a, b):
    return lax.dot_general(a, b, (((0,), (0,)), ((), ())), preferred_element_type=F32)


def norm_parts(v):
    c = v - jnp.mean(v, axis=-1, keepdims=True)
    r = lax.rsqrt(jnp.mean(c * c, axis=-1, keepdims=True) + EPS)
    return c * r, r


def norm_back(n, r, y, gain):
    yg = y * gain
    return r * (
        yg - jnp.mean(yg, axis=-1, keepdims=True) - n * jnp.mean(yg * n, axis=-1, keepdims=True)
    )


def low_half(shape):
    return lax.broadcasted_iota(jnp.int32, shape, 1) < (LANES // 2)

MESHID = pl.DeviceIdType.MESH


def here():
    dp = lax.axis_index("dp")
    return dp // 4, (dp // 2) % 2, dp % 2, lax.axis_index("head")


def at_dp(z, y, x):
    return {"dp": (z * 2 + y) * 2 + x}


def greet(depth):
    z, y, x, head = here()
    found = [at_dp(z, y, 1 - x), at_dp(z, 1 - y, x), {"head": 1 - head}]
    found += [at_dp((z + k) % depth, y, x) for k in range(1, depth)]
    barrier = pltpu.get_barrier_semaphore()
    for dev in found:
        pl.semaphore_signal(barrier, inc=1, device_id=dev, device_id_type=MESHID)
    pl.semaphore_wait(barrier, len(found))


class Wire:
    def __init__(self, send, recv):
        self.send, self.recv, self.next, self.open = send, recv, 0, []

    def slot(self):
        self.next += 1
        return self.next - 1

    def copy(self, i, src, dst, dev):
        return pltpu.make_async_remote_copy(
            src_ref=src, dst_ref=dst, send_sem=self.send.at[i], recv_sem=self.recv.at[i],
            device_id=dev, device_id_type=MESHID,
        )

    def start(self, i, make):
        self.copy(i, *make()).start()
        self.open.append((i, make))

    def arrived(self, i, ref, dev):
        self.copy(i, ref, ref, dev).wait_recv()

    def sent(self):
        for i, make in self.open:
            self.copy(i, *make()).wait_send()
        self.open = []


class Local:
    def __init__(self, sems):
        self.sems, self.next, self.open = sems, 0, []

    def start(self, make):
        i = self.next
        self.next += 1
        pltpu.make_async_copy(*make(), self.sems.at[i]).start()
        wait = lambda: pltpu.make_async_copy(*make(), self.sems.at[i]).wait()
        self.open.append(wait)
        return wait


def hops(p, y, x):
    ey, ex = (1 - y, x), (y, 1 - x)
    return (ey, ex) if p == 0 else (ex, ey)


def gather_stages(wire, depth, own, slot, plane=None):
    z, y, x, head = here()
    ids = {}
    for p in range(2):
        for k in range(depth):
            for kind in "zabc" + ("" if plane is None else "s"):
                ids[p, kind, k] = wire.slot()
    up = lambda k: (z + k) % depth
    down = lambda k: (z + depth - k) % depth

    def columns(p):
        (ay, ax), (by, bx) = hops(p, y, x)
        return (y, x), (ay, ax), (by, bx), (1 - y, 1 - x)

    def send_up(k):
        for p in range(2):
            wire.start(ids[p, "z", k], lambda p=p: (own(p), slot(p, z, y, x), at_dp(up(k), y, x)))

    def send_square(p, k, kind, col, to, first=False):
        def make():
            cs = columns(p)
            dst = slot(p, down(k), *cs[col])
            return own(p) if first else dst, dst, at_dp(z, *cs[to])
        wire.start(ids[p, kind, k], make)

    def wait(p, k, kind, col, frm):
        cs = columns(p)
        dev = at_dp(down(k), y, x) if frm is None else at_dp(z, *cs[frm])
        wire.arrived(ids[p, kind, k], slot(p, down(k), *cs[col]), dev)

    def begin():
        send_up(1)
        for p in range(2):
            send_square(p, 0, "a", 0, 1, True)
            send_square(p, 0, "b", 0, 2, True)
        for k in range(2, depth if plane is None else 2):
            send_up(k)

    def from_column(k):
        for p in range(2):
            wait(p, k, "z", 0, None)
            send_square(p, k, "a", 0, 1)
        for p in range(2):
            send_square(p, k, "b", 0, 2)
        if plane is not None and k + 1 < depth:
            send_up(k + 1)

    def from_first(k):
        for p in range(2):
            wait(p, k, "a", 1, 1)
            send_square(p, k, "c", 1, 2)

    def from_second(k):
        for p in range(2):
            wait(p, k, "b", 2, 2)
            wait(p, k, "c", 3, 2)

    def across(k):
        from_second(k)
        for p in range(2):
            def make(p=p):
                block = plane(p, down(k), head)
                return block, block, {"head": 1 - head}
            wire.start(ids[p, "s", k], make)

    def crossed(k):
        for p in range(2):
            wire.arrived(ids[p, "s", k], plane(p, down(k), 1 - head), {"head": 1 - head})

    part = functools.partial
    stages = {"begin": begin}
    for k in range(depth):
        for name, stage in (("z", from_column), ("a", from_first), ("d", from_second), ("s", across), ("x", crossed)):
            stages[name + str(k)] = part(stage, k)
    return stages


def add_into(dst, src):
    dst[...] = (dst[...].astype(F32) + src[...].astype(F32)).astype(dst.dtype)


class SquareSum:
    def __init__(self, wire, theirs, mine, pair_in, square_in, line_in):
        self.wire, self.theirs, self.mine = wire, theirs, mine
        self.pair_in, self.square_in, self.line_in = pair_in, square_in, line_in
        self.ids = {(p, kind): wire.slot() for p in range(2) for kind in "hab"}
        self.place = here()

    def devices(self, p):
        z, y, x, head = self.place
        ex, ey = at_dp(z, y, 1 - x), at_dp(z, 1 - y, x)
        return (ex, ey) if p == 0 else (ey, ex)

    def copy(self, p, kind):
        z, y, x, head = self.place
        if kind == "h":
            src, dst, dev = self.theirs(p), self.pair_in(p), {"head": 1 - head}
        elif kind == "a":
            src = self.mine(p, None, 1 - x) if p == 0 else self.mine(p, 1 - y, None)
            dst, dev = self.square_in(p), self.devices(p)[0]
        else:
            src = self.mine(p, 1 - y, x) if p == 0 else self.mine(p, y, 1 - x)
            dst, dev = self.line_in(p), self.devices(p)[1]
        return self.wire.copy(self.ids[p, kind], src, dst, dev)

    def pair(self):
        for p in range(2):
            self.copy(p, "h").start()

    def first(self):
        for p in range(2):
            self.wire.arrived(self.ids[p, "h"], self.pair_in(p), {"head": 1 - self.place[3]})
            add_into(self.mine(p, None, None), self.pair_in(p))
            self.copy(p, "a").start()

    def second(self):
        z, y, x, head = self.place
        for p in range(2):
            self.wire.arrived(self.ids[p, "a"], self.square_in(p), self.devices(p)[0])
            add_into(self.mine(p, None, x) if p == 0 else self.mine(p, y, None), self.square_in(p))
            self.copy(p, "b").start()

    def third(self):
        z, y, x, head = self.place
        for p in range(2):
            self.wire.arrived(self.ids[p, "b"], self.line_in(p), self.devices(p)[1])
            add_into(self.mine(p, y, x), self.line_in(p))

    def sent(self):
        for p in range(2):
            for kind in "hab":
                self.copy(p, kind).wait_send()


class ColumnSum:
    def __init__(self, wire, depth, part, column_in):
        self.wire, self.depth, self.part, self.column_in = wire, depth, part, column_in
        self.ids = {(p, k): wire.slot() for p in range(2) for k in range(1, depth)}
        self.place = here()

    def send(self, k):
        def make(p):
            z, y, x, head = self.place
            to = (z + self.depth - k) % self.depth
            return self.part(p, to), self.column_in(p, k), at_dp(to, y, x)

        for p in range(2):
            self.wire.start(self.ids[p, k], functools.partial(make, p))

    def total(self, p):
        z, y, x, head = self.place
        acc = self.part(p, z)[...].astype(F32)
        for k in range(1, self.depth):
            back = at_dp((z + k) % self.depth, y, x)
            self.wire.arrived(self.ids[p, k], self.column_in(p, k), back)
            acc = acc + self.column_in(p, k)[...].astype(F32)
        return acc


class SmallSum:
    def __init__(self, wire, depth, bufs, line):
        self.wire, self.depth, self.bufs, self.line = wire, depth, bufs, line
        self.ids = [wire.slot() for _ in range(2 + depth)]
        self.place = here()

    def devices(self):
        z, y, x, head = self.place
        return [{"head": 1 - head}, at_dp(z, y, 1 - x), at_dp(z, 1 - y, x)]

    def send(self, n):
        self.wire.start(self.ids[n], lambda: (self.bufs.at[2 * n], self.bufs.at[2 * n + 1], self.devices()[n]))

    def take(self, n):
        self.wire.arrived(self.ids[n], self.bufs.at[2 * n + 1], self.devices()[n])
        self.bufs[2 * n + 2] = self.bufs[2 * n] + self.bufs[2 * n + 1]

    def begin(self):
        self.send(0)

    def middle(self, n):
        self.take(n - 1)
        self.send(n)

    def column(self):
        z, y, x, head = self.place
        self.take(2)
        self.line[z] = self.bufs[6]
        for k in range(1, self.depth):
            self.wire.start(
                self.ids[2 + k],
                lambda k=k: (self.bufs.at[6], self.line.at[z], at_dp((z + k) % self.depth, y, x)),
            )

    def result(self):
        z, y, x, head = self.place
        for k in range(1, self.depth):
            back = (z + self.depth - k) % self.depth
            self.wire.arrived(self.ids[2 + k], self.line.at[back], at_dp(back, y, x))
        total = self.line[0]
        for n in range(1, self.depth):
            total = total + self.line[n]
        return total


def bind(names, refs):
    assert len(names) == len(refs)
    return types.SimpleNamespace(**dict(zip(names, refs)))


def spread_mask(masked, tmp, ch):
    images, rows = masked.shape
    tmp[...] = jnp.zeros_like(tmp)
    tmp[0:images, 0:rows] = masked[...].astype(F32)
    turned = tmp[...].T
    for i in range(images):
        ch[i] = turned[0:rows, i:i + 1]


def pad_index(raw, idx):
    idx[...] = jnp.zeros_like(idx)
    idx[0:raw.shape[0], 0:raw.shape[1]] = raw[...]


def run_all(stages):
    for stage in stages:
        stage()


def vmem(n):
    return [pl.BlockSpec(memory_space=pltpu.VMEM)] * n

ANY = pl.BlockSpec(memory_space=pl.ANY)
sd = jax.ShapeDtypeStruct
dma = lambda n: pltpu.SemaphoreType.DMA((n,))
VECTORS = ("mask_token", "ln1_gain", "ln1_bias", "proj_bias", "gamma1", "ln2_gain", "ln2_bias", "fc2_bias", "gamma2")
GIVEN = ("x", "masked", "kv", "raw") + VECTORS + ("cot",)
KEPT = (
    "idx", "valid", "tmp", "ch", "bias", "nt", "q", "k", "v", "att", "res", "n2", "db", "act", "dpre", "dn",
    "small1", "small2", "gb1", "lsem",
)
SHARED = (
    "w", "wp", "mix", "b1", "b1line", "g", "pair_in", "square_in", "line_in", "column", "column_in",
    "ar_pair", "ar_square", "ar_line", "ar_column", "gathered", "bufs", "line", "tbufs", "tline", "lbufs", "lline", "send", "recv",
)


class Row:
    def __init__(self, ref):
        self.ref = ref

    def __getitem__(self, at):
        return self.ref[...].reshape(1, -1)


def layer_kernel(direct, *refs):
    if direct:
        names = GIVEN + ("mixown", "wown", "wpown", "own1", "own2", "spot")
        names += ("out", "gx", "p", "w1", "w2", "full", "gff", "small", "table", "late") + KEPT + SHARED
    else:
        names = GIVEN + ("mix", "w", "wp", "w1", "w2", "b1")
        names += ("out", "gx", "p", "g1", "g2", "gw", "gt", "small1_out", "small2_out", "gb1_out") + KEPT
    r = bind(names, refs)
    for name in VECTORS:
        setattr(r, name, Row(getattr(r, name)))
    images, rows, width = r.x.shape
    heads, rp, keys = r.bias.shape
    flat = images * rp
    scale = (width // heads) ** -0.5
    pairs, per = heads // 2, heads // 4
    steps, block = r.b1.shape[-2:]
    own_heads = heads // r.mix.shape[0]
    own_tiles = width // r.mix.shape[0] // LANES
    chunks = (r.mix.shape[1] - 2 * own_tiles) // own_heads
    local = Local(r.lsem)
    z, y, x, head = here()
    plan = {}
    part = functools.partial
    every = lambda v: slice(None) if v is None else v
    level = lambda b: (z + 2 * steps - b) % steps
    at_image = lambda i: pl.multiple_of(i * rp, 16)

    if direct:
        depth = r.w1.shape[0]
        half = r.wown.shape[2]
        lanes_of = lambda hd: pl.ds(pl.multiple_of(hd * half, LANES), half)
        full = (r.w1, r.w2)
        wire = Wire(r.send, r.recv)
        greet(depth)
        other = {"head": 1 - head}
        swaps = [
            (r.mixown, lambda hd: r.mix.at[hd]),
            (r.wown, lambda hd: r.w.at[:, :, lanes_of(hd)]),
            (r.wpown, lambda hd: r.wp.at[lanes_of(hd)]),
        ]
        swap_ids = [wire.slot() for _ in swaps]
        bias_id = wire.slot()
        bias_of = lambda hd: r.bias.at[pl.ds(hd * own_heads, own_heads)]
        for i, (src, place) in zip(swap_ids, swaps):
            wire.start(i, lambda src=src, place=place: (src, place(head), other))
        for src, place in swaps:
            local.start(lambda src=src, place=place: (src, place(head)))
        slot = lambda p, zz, yy, xx: full[p].at[zz, yy, xx, head]
        own = (r.own1, r.own2)
        for p in range(2):
            local.start(lambda p=p: (own[p], slot(p, z, y, x)))
        r.b1[0] = r.spot[...]
        bias_sum = SmallSum(wire, depth, r.b1, r.b1line)
        ag = gather_stages(
            wire, depth, own=lambda p: own[p], slot=slot,
            plane=lambda p, zz, hd: full[p].at[zz, :, :, hd],
        )
        ag["begin"]()
        bias_sum.begin()
        squares = [
            SquareSum(
                wire,
                theirs=lambda p, b=b: r.g.at[b % 3, p, :, :, 1 - head],
                mine=lambda p, yy, xx, b=b: r.g.at[b % 3, p, every(yy), every(xx), head],
                pair_in=lambda p, b=b: r.pair_in.at[b % 2, p],
                square_in=lambda p, b=b: r.square_in.at[b % 2, p],
                line_in=lambda p, b=b: r.line_in.at[b % 2, p],
            )
            for b in range(steps)
        ]
        column = ColumnSum(wire, depth, part=lambda p, zz: r.column.at[p, zz], column_in=lambda p, k: r.column_in.at[p, k - 1])

        def close(b):
            squares[b].third()
            for p in range(2):
                r.column[p, level(b)] = r.g[b % 3, p, y, x, head]
            if b:
                column.send(b)
            squares[b].sent()

        early = SmallSum(wire, depth, r.bufs, r.line)
        tables = SmallSum(wire, depth, r.tbufs, r.tline)
        late = SmallSum(wire, depth, r.lbufs, r.lline)
        plan = {
            "p0": [ag["z1"], ag["a0"]], "p1": [part(bias_sum.middle, 1)],
            "t0": [ag["s0"], ag["a1"], part(bias_sum.middle, 2)],
            "t3": [ag["z2"], ag["s1"], bias_sum.column], "t5": [ag["a2"]],
            "t7": [ag["z3"], ag["s2"]],
        }

    def tick(point):
        run_all(plan.get(point, ()))

    def tick_in(step, point):
        for key, stages in plan.items():
            if isinstance(key, tuple) and key[1] == point:
                pl.when(step == key[0])(part(run_all, stages))

    spread_mask(r.masked, r.tmp, r.ch)
    pad_index(r.raw, r.idx)
    r.valid[...] = jnp.zeros_like(r.valid)
    r.valid[0:r.kv.shape[0], 0:rows] = r.kv[...]

    def hidden_of(i):
        ch = r.ch[i]
        return r.x[i].astype(F32) * (1.0 - ch) + ch * r.mask_token[...]

    def attention_forward(normed, pring):
        normed[...] = jnp.zeros_like(normed)
        r.n2[...] = jnp.zeros_like(r.n2)
        r.res[...] = jnp.zeros_like(r.res)

        def first_norm(i, carry):
            n, _ = norm_parts(hidden_of(i))
            normed[pl.ds(at_image(i), rows), :] = (n * r.ln1_gain[...] + r.ln1_bias[...]).astype(BF16)
            return carry

        lax.fori_loop(0, images, first_norm, 0)
        if direct:
            for wait in local.open:
                wait()
            local.open = []

        def gather_head(h, carry):
            for side in range(keys // LANES):
                idx = r.idx[:, side * LANES:(side + 1) * LANES]
                low = idx & (LANES - 1)
                high = idx >> 7
                acc = jnp.zeros(idx.shape, F32)
                for c in range(chunks):
                    if direct:
                        row = r.mixown[pl.ds(h * chunks + c, 1), :]
                    else:
                        row = r.mix[h // own_heads, pl.ds((h % own_heads) * chunks + c, 1), :]
                    got = jnp.take_along_axis(jnp.broadcast_to(row, idx.shape), low, axis=1)
                    acc = jnp.where(high == c, got, acc)
                r.bias[head * own_heads + h if direct else h, :, side * LANES:(side + 1) * LANES] = acc
            return carry

        some = own_heads if direct else heads
        for n in range(3):
            lax.fori_loop(n * some // 3, (n + 1) * some // 3, gather_head, 0)
            tick("g%d" % n)
        if direct:
            wire.copy(bias_id, bias_of(head), bias_of(head), other).start()
            for n in range(3):
                wire.arrived(swap_ids[n], swaps[n][1](1 - head), other)
        zeros_tail = jnp.zeros((images, keys - rp, width), BF16)
        r.k[:, rp:, :] = zeros_tail
        r.v[:, rp:, :] = zeros_tail

        def bias_row(kind, nb):
            tiles = []
            for t in (2 * nb, 2 * nb + 1):
                at = own_heads * chunks + kind * own_tiles + t % own_tiles
                tiles.append(r.mix[t // own_tiles, at:at + 1, :])
            return jnp.concatenate(tiles, axis=1)

        for c, (dst, kind) in enumerate(((r.q, 0), (r.k, None), (r.v, 1))):
            for nb in range(width // 256):
                cols = slice(nb * 256, (nb + 1) * 256)
                acc = dot(normed[...], r.w[c, :, cols])
                if kind is not None:
                    acc = acc + bias_row(kind, nb)
                acc = acc.astype(BF16)
                if kind == 0:
                    acc = acc * scale
                for i in range(images):
                    dst[i, :rp, cols] = acc[i * rp:(i + 1) * rp]
            tick("p%d" % c)
        r.nt[...] = normed[...].T
        if direct:
            wire.arrived(bias_id, bias_of(1 - head), other)

        def attend(t, carry):
            i = t // pairs
            j = t % pairs
            lanes = pl.ds(pl.multiple_of(j * LANES, LANES), LANES)
            qp = r.q[i, :, lanes]
            kp = r.k[i, :, lanes]
            vp = r.v[i, :, lanes]
            lo = low_half((rp, LANES))
            ok = r.valid[pl.ds(head * images + i, 1), :] > 0
            outs = []
            for s in range(2):
                qs = jnp.where(lo if s == 0 else jnp.logical_not(lo), qp, jnp.zeros_like(qp))
                sc = dot_nt(qs, kp) + r.bias[2 * j + s]
                sc = jnp.where(ok, sc, -1e30)
                e = jnp.exp(sc - jnp.max(sc, axis=-1, keepdims=True))
                prob = e * (1.0 / jnp.sum(e, axis=-1, keepdims=True))
                pring[i % 2, 2 * j + s] = prob
                outs.append(dot(prob.astype(BF16), vp))
            r.att[pl.ds(at_image(i), rp), lanes] = jnp.where(lo, outs[0], outs[1]).astype(BF16)
            return carry

        stored = {}
        for n in range(2 * images):
            i = n // 2
            if n % 2 == 0 and i >= 2:
                stored[i - 2]()
            lax.fori_loop(n * pairs // 2, (n + 1) * pairs // 2, attend, 0)
            if n % 2:
                stored[i] = local.start(lambda i=i: (pring.at[i % 2], r.p.at[i]))
            tick("t%d" % n)

        def finish(t, carry):
            both = dot(r.att[pl.ds(at_image(2 * t), 2 * rp), :], r.wp[...]) + r.proj_bias[...]
            for side in range(2):
                i = 2 * t + side
                res = hidden_of(i) + r.gamma1[...] * both[side * rp:side * rp + rows]
                r.res[pl.ds(at_image(i), rows), :] = res
                n, _ = norm_parts(res)
                r.n2[pl.ds(at_image(i), rows), :] = (n * r.ln2_gain[...] + r.ln2_bias[...]).astype(BF16)
            return carry

        lax.fori_loop(0, images // 2, finish, 0)
        stored[images - 2]()
        stored[images - 1]()

    pl.run_scoped(attention_forward, pltpu.VMEM((flat, width), BF16), pltpu.VMEM((2, heads, rp, keys), F32))

    if direct:
        wire.copy(bias_id, bias_of(head), bias_of(head), other).wait_send()
        ag["x0"]()
        r.b1[1] = bias_sum.result()
        plan = {
            (0, 0): [ag["x1"]], (0, 1): [ag["a3"]], (0, 4): [ag["s3"], squares[0].pair],
            (1, 0): [ag["x2"]], (1, 1): [squares[0].first], (1, 4): [squares[1].pair],
            (2, 0): [ag["x3"]], (2, 1): [squares[0].second, squares[1].first], (2, 4): [squares[2].pair],
            (3, 1): [part(close, 0), squares[1].second, squares[2].first], (3, 4): [squares[3].pair],
        }

    def feed_forward(cot, branch, slots, sems):
        def weights(b, into):
            copies = []
            for p, src in enumerate((r.w1, r.w2)):
                if direct:
                    view = src.at[level(b)]
                else:
                    view = src.at[pl.ds(pl.multiple_of(level(b) * block, 16), block)]
                copies.append(pltpu.make_async_copy(view, slots.at[into, p], sems.at[into, p]))
            return copies

        for copy in weights(0, 0):
            copy.start()
        fetch = pltpu.make_async_copy(r.cot, cot, sems.at[2, 0])
        fetch.start()
        r.db[...] = jnp.zeros_like(r.db)
        branch[...] = jnp.zeros_like(branch)
        r.dn[...] = jnp.zeros_like(r.dn)
        fetch.wait()

        def fill(i, carry):
            r.db[pl.ds(at_image(i), rows), :] = (cot[i].astype(F32) * r.gamma2[...]).astype(BF16)
            return carry

        lax.fori_loop(0, images, fill, 0)

        def step(b, carry):
            slot = b % 2
            t = level(b)
            for copy in weights(b, slot):
                copy.wait()
            tick_in(b, 0)

            @pl.when(b + 1 < steps)
            def _():
                for copy in weights(b + 1, 1 - slot):
                    copy.start()

            w1 = lambda: slots[slot, 0].reshape(block, width)
            w2 = lambda: slots[slot, 1].reshape(block, width)
            b1 = r.b1[1, pl.ds(t, 1), :] if direct else r.b1[pl.ds(t, 1), :]

            def tile(i, gb1):
                at = pl.ds(pl.multiple_of(i * 2 * rp, 16), 2 * rp)
                pre = dot_nt(r.n2[at, :], w1()) + b1
                cdf = 0.5 * (1.0 + lax.erf(pre * 0.7071067811865476))
                slope = cdf + pre * (0.3989422804014327 * jnp.exp(-0.5 * pre * pre))
                act = (pre * cdf).astype(BF16)
                r.act[at, :] = act
                dpre = (dot_nt(r.db[at, :], w2()) * slope).astype(BF16)
                r.dpre[at, :] = dpre
                branch[at, :] += dot(act, w2())
                r.dn[at, :] += dot(dpre, w1())
                return gb1 + jnp.sum(dpre.astype(F32), axis=0, keepdims=True)

            gb1 = lax.fori_loop(0, images // 4, tile, jnp.zeros((1, block), F32))
            tick_in(b, 1)
            r.gb1[pl.ds(t, 1), :] = lax.fori_loop(images // 4, images // 2, tile, gb1)
            tick_in(b, 2)

            def store(p, value):
                value = value.astype(BF16)
                if direct:
                    r.g[b % 3, p] = value.reshape(r.g.shape[2:])
                else:
                    slots[slot, p] = value
                    dst = (r.g1, r.g2)[p].at[pl.ds(pl.multiple_of(t * block, 16), block)]
                    copy = pltpu.make_async_copy(slots.at[slot, p], dst, sems.at[3, p])
                    copy.start()
                    copy.wait()

            second = dot_tn(r.act[...], r.db[...])
            store(1, second)
            tick_in(b, 3)
            store(0, dot_tn(r.dpre[...], r.n2[...]))
            tick_in(b, 4)
            return carry

        lax.fori_loop(0, steps, step, 0)
        r.small2[...] = jnp.zeros_like(r.small2)
        r.n2[...] = jnp.zeros_like(r.n2)

        def add(row, value):
            r.small2[row:row + 1, :] += jnp.sum(value, axis=0, keepdims=True)

        def finish(i, carry):
            span = pl.ds(at_image(i), rows)
            up = cot[i].astype(F32)
            mlp = branch[span, :] + r.fc2_bias[...]
            res = r.res[span, :]
            cot[i] = (res + r.gamma2[...] * mlp).astype(BF16)
            add(S_GA2, up * mlp)
            add(S_FB2, (up * r.gamma2[...]).astype(BF16).astype(F32))
            n, inv = norm_parts(res)
            dn = r.dn[span, :]
            add(S_LG2, dn * n)
            add(S_LB2, dn)
            dres = up + norm_back(n, inv, dn, r.ln2_gain[...])
            add(S_GA1, dres * (res - hidden_of(i)))
            r.res[span, :] = dres
            dproj = (dres * r.gamma1[...]).astype(BF16)
            r.n2[span, :] = dproj
            add(S_PB, dproj.astype(F32))
            return carry

        lax.fori_loop(0, images, finish, 0)
        r.small2[S_GA1:S_GA1 + 1, :] = r.small2[S_GA1:S_GA1 + 1, :] / r.gamma1[...]
        store_out = pltpu.make_async_copy(cot, r.out, sems.at[2, 1])
        store_out.start()
        store_out.wait()

    if direct:
        slots_shape = (2, 2) + r.w1.shape[1:]
    else:
        slots_shape = (2, 2, block, width)
    pl.run_scoped(
        feed_forward, pltpu.VMEM(r.cot.shape, BF16), pltpu.VMEM((flat, width), F32),
        pltpu.VMEM(slots_shape, BF16), pltpu.SemaphoreType.DMA((4, 2)),
    )
    plan = {}

    def attention_backward(pbuf, dpt, g, sems):
        nonlocal plan
        dqkv = (r.act, r.dpre, r.n2)
        pair_of = lambda s: (s % 2) * per + s // 2

        def fetch(t):
            src = r.p.at[t % images, pl.ds(2 * pair_of(t // images), 2)]
            return pltpu.make_async_copy(src, pbuf.at[t % 3], sems.at[t % 3])

        for t in range(2):
            fetch(t).start()
        if direct:
            ar, lines, gathers = [], [], []
            for m in range(per):
                ar.append(SquareSum(
                    wire,
                    theirs=lambda p, m=m: g.at[m, 1 - head, p],
                    mine=lambda p, yy, xx, m=m: g.at[m, head, p, :, :, every(yy), every(xx)],
                    pair_in=lambda p, m=m: r.ar_pair.at[m, p],
                    square_in=lambda p, m=m: r.ar_square.at[m, p], line_in=lambda p, m=m: r.ar_line.at[m, p],
                ))
                lines.append(ColumnSum(
                    wire, depth, part=lambda p, zz, m=m: g.at[m, head, p, :, zz, y, x],
                    column_in=lambda p, k, m=m: r.ar_column.at[m, p, k - 1],
                ))
                lanes_m = slice(m * LANES, (m + 1) * LANES)
                into = lambda p, zz, yy, xx, lanes_m=lanes_m: r.gathered.at[p, :, zz, yy, xx, :, lanes_m]
                gathers.append(gather_stages(wire, depth, own=lambda p, into=into: into(p, z, y, x), slot=into))

            def third(m):
                ar[m].third()
                for k in range(1, depth):
                    lines[m].send(k)

            def last(m):
                for p in range(2):
                    r.gathered[p, :, z, y, x, :, m * LANES:(m + 1) * LANES] = lines[m].total(p).astype(BF16)
                gathers[m]["begin"]()

            def ff_last():
                for p in range(2):
                    r.gff[p] = column.total(p)

            def early_begin():
                r.bufs[0] = jnp.zeros(r.bufs.shape[1:], F32)
                r.bufs[0, 0:8] = r.small2[...]
                r.bufs[0, 8:8 + steps] = r.gb1[...]
                early.begin()

            g0, g1, g2 = gathers
            plan = {
                "start": [part(close, 1), squares[2].second, squares[3].first, early_begin],
                (0, 4): [part(close, 2), part(early.middle, 1)], (1, 1): [squares[3].second], (1, 4): [ar[0].pair, part(early.middle, 2)],
                (2, 2): [ar[0].first], (2, 3): [part(close, 3)], (2, 4): [early.column],
                (3, 2): [ar[0].second], (3, 4): [ar[1].pair], (4, 1): [part(third, 0)], (4, 2): [ar[1].first],
                (5, 1): [part(last, 0)], (5, 2): [ar[1].second], (5, 4): [ar[2].pair, g0["z1"], g0["z2"], g0["z3"]],
                (5, 5): [ar[2].first, part(third, 1)], (5, 6): [g0["a0"], g0["a1"], g0["a2"], g0["a3"]],
                (5, 7): [part(last, 1)], (5, 8): [ar[2].second], (5, 9): [g1["z1"], g1["z2"], g1["z3"]],
                (5, 10): [part(third, 2), part(tables.middle, 1)], (5, 11): [g0["d0"], g0["d1"], g0["d2"], g0["d3"]],
                (5, 12): [part(last, 2), part(tables.middle, 2), g1["a0"], g1["a1"], g1["a2"], g1["a3"]],
                (5, 13): [tables.column],
            }

        tick("start")
        for t in range(images // 2):
            at = slice(2 * t * rp, 2 * (t + 1) * rp)
            r.db[at, :] = dot_nt(r.n2[at, :], r.wp[...]).astype(BF16)
        dpt[...] = r.n2[...].T
        r.small1[...] = jnp.zeros_like(r.small1)

        def step(s, carry):
            j = pair_of(s)
            tick_in(s, 1)
            lanes = pl.ds(pl.multiple_of(j * LANES, LANES), LANES)
            r.bias[2 * j] = jnp.zeros((rp, keys), F32)
            r.bias[2 * j + 1] = jnp.zeros((rp, keys), F32)

            def image(i, carry):
                t = s * images + i
                fetch(t).wait()

                @pl.when(t + 2 < pairs * images)
                def _():
                    fetch(t + 2).start()

                at = pl.ds(at_image(i), rp)
                qp = r.q[i, :, lanes]
                kp = r.k[i, :, lanes]
                vp = r.v[i, :, lanes]
                da = r.db[at, lanes]
                lo = low_half((rp, LANES))
                dv, dq, dk = [], [], []
                for n in range(2):
                    das = jnp.where(lo if n == 0 else jnp.logical_not(lo), da, jnp.zeros_like(da))
                    prob = pbuf[t % 3, n]
                    dp = dot_nt(das, vp)
                    dsc = prob * (dp - jnp.sum(prob * dp, axis=-1, keepdims=True))
                    dsb = dsc.astype(BF16)
                    r.bias[2 * j + n] += dsb.astype(F32)
                    dv.append(dot_tn(prob.astype(BF16), da))
                    dq.append(dot(dsb, kp))
                    dk.append(dot_tn(dsb, qp))
                lok = low_half((keys, LANES))
                dqkv[0][at, lanes] = (jnp.where(lo, dq[0], dq[1]) * scale).astype(BF16)
                dqkv[1][at, lanes] = jnp.where(lok, dk[0], dk[1])[:rp].astype(BF16)
                dqkv[2][at, lanes] = jnp.where(lok, dv[0], dv[1])[:rp].astype(BF16)
                return carry

            lax.fori_loop(0, images // 2, image, 0)
            tick_in(s, 2)
            lax.fori_loop(images // 2, images, image, 0)
            tick_in(s, 3)

            def store(c, value):
                value = value.astype(BF16)
                if direct:
                    g[s // 2, s % 2, c // 2, c % 2] = value.reshape(g.shape[4:])
                else:
                    g[...] = value
                    copy = pltpu.make_async_copy(g, r.gw.at[j, c], sems.at[3])
                    copy.start()
                    copy.wait()

            three = dot(r.nt[...], jnp.concatenate([dqkv[c][:, lanes] for c in range(3)], axis=1))
            for c in range(3):
                store(c, three[:, c * LANES:(c + 1) * LANES])
            store(3, dot(dpt[...], r.att[:, lanes]))
            tick_in(s, 4)
            return carry

        lax.fori_loop(0, pairs, step, 0)
        now = lambda point: run_all(plan.get((pairs - 1, point), ()))

        def total_rows(row, c):
            def add(i, acc):
                return acc + jnp.sum(dqkv[c][pl.ds(at_image(i), rp), :].astype(F32), axis=0, keepdims=True)
            r.small1[row:row + 1, :] = lax.fori_loop(0, images, add, jnp.zeros((1, width), F32))

        total_rows(T_QB, 0)
        total_rows(T_VB, 2)

        a_iota = lax.broadcasted_iota(jnp.int32, (8, keys), 0)
        b_iota = lax.broadcasted_iota(jnp.int32, (LANES, keys), 0)

        def scatter(t, acc):
            at = pl.ds(pl.multiple_of(t * 8, 8), 8)
            idx = r.idx[at, :]
            high, low = idx >> 7, idx & (LANES - 1)
            tiles = [r.bias[h, at, :] for h in range(heads)]
            lefts, rests, ones = [], [], []
            for n in range(8):
                pick = jnp.broadcast_to(high[n:n + 1], (8, keys)) == a_iota
                ones.append((jnp.broadcast_to(low[n:n + 1], (LANES, keys)) == b_iota).astype(F32).astype(BF16))
                left = jnp.concatenate(
                    [jnp.where(pick, jnp.broadcast_to(tile[n:n + 1], (8, keys)), 0.0) for tile in tiles], axis=0)
                top = left.astype(BF16)
                lefts.append(top)
                rests.append((left - top.astype(F32)).astype(BF16))
            one = jnp.concatenate(ones, axis=1)
            return acc + dot_nt(jnp.concatenate(lefts, axis=1), one) + dot_nt(jnp.concatenate(rests, axis=1), one)

        table = jnp.zeros((heads * 8, LANES), F32)
        blocks = rp // 8
        for n in range(5):
            table = lax.fori_loop(n * blocks // 5, (n + 1) * blocks // 5, scatter, table)
            now(5 + n)
        wide = width // LANES
        tall = heads * 8 // wide
        if direct:
            for t in range(wide):
                r.tbufs[0, :, t * LANES:(t + 1) * LANES] = table[t * tall:(t + 1) * tall]
            tables.begin()
        def finish(i, carry):
            span = pl.ds(at_image(i), rp)
            dn = dot_nt(dqkv[0][span, :], r.w[0])
            dn += dot_nt(dqkv[1][span, :], r.w[1])
            dn += dot_nt(dqkv[2][span, :], r.w[2])
            dn = dn[:rows]
            ch = r.ch[i]
            n, inv = norm_parts(hidden_of(i))
            dh = r.res[pl.ds(at_image(i), rows), :] + norm_back(n, inv, dn, r.ln1_gain[...])
            r.dn[pl.ds(at_image(i), rows), :] = dh * (1.0 - ch)
            for row, value in ((T_MASK, dh * ch), (T_LG1, dn * n), (T_LB1, dn)):
                r.small1[row:row + 1, :] += jnp.sum(value, axis=0, keepdims=True)
            return carry

        leaving = []
        for i in range(images):
            lax.fori_loop(i, i + 1, finish, 0)
            leaving.append(local.start(lambda i=i: (r.dn.at[pl.ds(i * rp, rows)], r.gx.at[i])))
            now(10 + i)

        for wait in leaving:
            wait()
        if not direct:
            r.gt[...] = table
            r.small1_out[...] = r.small1[...]
            r.small2_out[...] = r.small2[...]
            r.gb1_out[...] = r.gb1[...]
            return
        r.lbufs[0] = r.small1[...]
        late.begin()
        r.small[...] = early.result()
        late.middle(1)
        run_all(g2["z%d" % k] for k in range(1, depth))
        late.middle(2)
        run_all(g1["d%d" % k] for k in range(depth))
        run_all(g2["a%d" % k] for k in range(depth))
        late.column()
        ff_last()
        r.table[...] = tables.result()
        run_all(g2["d%d" % k] for k in range(depth))
        keep = local.start(lambda: (r.gathered, r.full))
        r.late[...] = late.result()
        for m in range(per):
            ar[m].sent()
        wire.sent()
        keep()

    if direct:
        g_shape = (per, 2, 2, 2, depth, 2, 2) + r.gathered.shape[5:6] + (LANES,)
    else:
        g_shape = (width, LANES)
    pl.run_scoped(
        attention_backward, pltpu.VMEM((3, 2, rp, keys), F32), pltpu.VMEM((width, flat), BF16),
        pltpu.VMEM(g_shape, BF16), dma(4),
    )


def layer(direct, given, extra, heads, rp, keys, depth):
    x, kv = given[0], given[2]
    images, rows, width = x.shape
    flat = images * rp
    tall = -(-max(kv.shape[0], images) // 8) * 8
    steps = 4
    ff = extra[-1].size
    outs = [sd(x.shape, BF16), sd(x.shape, F32), sd((images, heads, rp, keys), F32)]
    out_specs = [ANY] * 3
    bf = lambda *shape: pltpu.VMEM(shape, BF16)
    fl = lambda *shape: pltpu.VMEM(shape, F32)
    scratch = [
        pltpu.VMEM((rp, keys), jnp.int32), pltpu.VMEM((tall, keys), jnp.int32), fl(tall, keys), fl(images, rows, 1),
        fl(heads, rp, keys), bf(width, flat), bf(images, rp, width), bf(images, keys, width), bf(images, keys, width),
        bf(flat, width), fl(flat, width), bf(flat, width), bf(flat, width), bf(flat, width), bf(flat, width),
        fl(flat, width), fl(8, width), fl(8, width), fl(steps, ff // steps), dma(24),
    ]
    in_specs = vmem(len(given) - 1) + [ANY]
    params = {}
    if direct:
        mixown, wown, wpown, own1, own2, spot = extra
        per = heads // 4
        share = own1.shape[0]
        own = width // (4 * depth)
        total = 8 + 8
        tall_t = heads * 8 * LANES // width
        big = sd((depth, 2, 2, 2) + own1.shape, BF16)
        outs += [big, big, sd((2, 2, depth, 2, 2, own, per * LANES), BF16), sd((2, share, width), F32)]
        outs += [sd((total, width), F32), sd((tall_t, width), F32), sd((8, width), F32)]
        in_specs += vmem(6)
        out_specs += [ANY] * 3 + vmem(4)
        n = 4 + 2 * (4 * depth + 4) + 2 + depth + 6 * steps + 2 * (depth - 1)
        n += per * (6 + 2 * (depth - 1) + 8 * depth) + 3 * (2 + depth)
        scratch += [
            bf(3, width, width), bf(width, width), fl(2, *mixown.shape), fl(7, *spot.shape), fl(depth, *spot.shape),
            bf(3, 2, 2, 2, 2, share, width), bf(2, 2, 2, 2, share, width), bf(2, 2, 2, share, width), bf(2, 2, share, width),
            bf(2, depth, share, width), bf(2, depth - 1, share, width),
            bf(per, 2, 2, depth, 2, 2, own, LANES), bf(per, 2, 2, depth, 2, own, LANES), bf(per, 2, 2, depth, own, LANES),
            bf(per, 2, depth - 1, 2, own, LANES), bf(2, 2, depth, 2, 2, own, per * LANES),
            fl(7, total, width), fl(depth, total, width), fl(7, tall_t, width), fl(depth, tall_t, width), fl(7, 8, width), fl(depth, 8, width), dma(n), dma(n),
        ]
        params = dict(collective_id=1, has_side_effects=True)
    else:
        part = sd((ff, width), BF16)
        outs += [part, part, sd((heads // 2, 4, width, LANES), BF16), sd((heads * 8, LANES), F32)]
        outs += [sd((8, width), F32), sd((8, width), F32), sd((steps, ff // steps), F32)]
        in_specs += vmem(3) + [ANY, ANY] + vmem(1)
        out_specs += [ANY] * 3 + vmem(4)
    return pl.pallas_call(
        functools.partial(layer_kernel, direct), name="layer",
        out_shape=tuple(outs), in_specs=in_specs, out_specs=out_specs, scratch_shapes=scratch,
        compiler_params=pltpu.CompilerParams(vmem_limit_bytes=63 * 2**20, **params),
    )(*given, *extra)


def shards(
    inputs, masked, key_valid, rel_index, mask_token, ln1_gain, ln1_bias, w_qkv, qv_bias, rel_table,
    w_proj, proj_bias, gamma1, ln2_gain, ln2_bias, w_fc1, fc1_bias, w_fc2, fc2_bias, gamma2, cotangent,
):
    images, rows, width = inputs.shape
    dp, hn = lax.axis_size("dp"), lax.axis_size("head")
    me, head = lax.axis_index("dp"), lax.axis_index("head")
    depth = dp // 4
    share = w_fc2.shape[0]
    ff = share * dp * hn
    entries, heads = rel_table.shape[0], rel_table.shape[1] * hn
    rp, keys = -(-rows // 16) * 16, -(-rows // LANES) * LANES
    direct = hn == 2 and dp == 16 and share % 16 == 0 and width % (16 * dp) == 0

    tab_rows = -(-entries // LANES)
    tab = jnp.pad(rel_table.T, ((0, 0), (0, tab_rows * LANES - entries)))
    mix = jnp.concatenate([tab.reshape(-1, LANES), qv_bias.reshape(-1, LANES)])
    vectors = (mask_token, ln1_gain, ln1_bias, proj_bias, gamma1, ln2_gain, ln2_bias, fc2_bias, gamma2)
    given = (inputs, masked, key_valid, rel_index) + vectors + (cotangent,)
    w3 = jnp.transpose(w_qkv, (1, 0, 2))
    if direct:
        spot_shape = (4, ff // 4)
        owner = (lax.broadcasted_iota(jnp.int32, spot_shape, 0) * (ff // 4) + lax.broadcasted_iota(jnp.int32, spot_shape, 1)) // share
        spot = jnp.where(owner == me * hn + head, jnp.tile(fc1_bias.astype(F32), ff // 4 // share)[None], 0.0)
        extra = (mix, w3, w_proj, w_fc1.T, w_fc2, spot)
        out, gx, _, _, _, full, gff, small, table, late = layer(True, given, extra, heads, rp, keys, depth)
        g_fc1, g_fc2 = gff[0], gff[1]
        full = full.reshape(4, width, -1).astype(F32)
        s1, s2 = late, small[:8]
        wide = width // LANES
        tall = heads * 8 // wide
        table = jnp.transpose(table.reshape(tall, wide, LANES), (1, 0, 2)).reshape(heads, -1)
        g_b1 = small[8:12].reshape(-1)
    else:
        w = lax.all_gather(w3, "head", axis=2, tiled=True)
        wp = lax.all_gather(w_proj, "head", axis=0, tiled=True)
        w1 = lax.all_gather(w_fc1.T, ("dp", "head"), axis=0, tiled=True)
        w2 = lax.all_gather(w_fc2, ("dp", "head"), axis=0, tiled=True)
        b1 = lax.all_gather(fc1_bias, ("dp", "head"), axis=0, tiled=True).astype(F32).reshape(4, -1)
        extra = (lax.all_gather(mix, "head", axis=0), w, wp, w1, w2, b1)
        out, gx, _, ga, gb, gw, gt, s1, s2, gb1 = layer(False, given, extra, heads, rp, keys, depth)
        g_fc1 = lax.psum_scatter(ga.astype(F32), ("dp", "head"), scatter_dimension=0, tiled=True)
        g_fc2 = lax.psum_scatter(gb.astype(F32), ("dp", "head"), scatter_dimension=0, tiled=True)
        full = lax.psum(lax.psum_scatter(gw.astype(F32), "head", scatter_dimension=0, tiled=True), "dp")
        full = jnp.transpose(full, (1, 2, 0, 3)).reshape(4, width, -1)
        s1, s2, table, g_b1 = lax.psum((s1, s2, gt.reshape(heads, -1), gb1.reshape(-1)), ("dp", "head"))
    g_qkv, g_proj = full[:3], full[3].T
    g_table = lax.dynamic_slice_in_dim(table, head * (heads // hn), heads // hn, 0)[:, :entries].T
    g_b1 = lax.dynamic_slice_in_dim(g_b1, (me * hn + head) * share, share)
    g_qvb = lax.dynamic_slice_in_dim(s1[T_QB:T_VB + 1], head * (width // hn), width // hn, 1)
    return (
        out, gx, s1[T_MASK], s1[T_LG1], s1[T_LB1], jnp.transpose(g_qkv, (1, 0, 2)), g_qvb, g_table, g_proj,
        s2[S_PB], s2[S_GA1], s2[S_LG2], s2[S_LB2], g_fc1.T, g_b1, g_fc2, s2[S_FB2], s2[S_GA2],
    )


def solution(mesh):
    in_specs = (
        P(("dp", "head"), None, None),
        P(("dp", "head"), None),
        P("dp", None),
        P(),
        P(),
        P(),
        P(),
        P(None, None, "head"),
        P(None, "head"),
        P(None, "head"),
        P("head", None),
        P(),
        P(),
        P(),
        P(),
        P(None, ("dp", "head")),
        P(("dp", "head")),
        P(("dp", "head"), None),
        P(),
        P(),
        P(("dp", "head"), None, None),
    )
    out_specs = (
        P(("dp", "head"), None, None),
        P(("dp", "head"), None, None),
        P(),
        P(),
        P(),
        P(None, None, "head"),
        P(None, "head"),
        P(None, "head"),
        P("head", None),
        P(),
        P(),
        P(),
        P(),
        P(None, ("dp", "head")),
        P(("dp", "head")),
        P(("dp", "head"), None),
        P(),
        P(),
    )
    return jax.shard_map(shards, mesh=mesh, in_specs=in_specs, out_specs=out_specs, check_vma=False)
```

```python
import functools
import types
import jax
import jax.numpy as jnp
from jax import lax
from jax.experimental import pallas as pl
from jax.experimental.pallas import tpu as pltpu
from jax.sharding import PartitionSpec as P

F32 = jnp.float32
BF16 = jnp.bfloat16
EPS = 1e-06
LANES = 128
S_GA2, S_FB2, S_LG2, S_LB2, S_GA1, S_PB = range(6)
T_MASK, T_LG1, T_LB1, T_QB, T_VB = range(5)


def dot(a, b):
    return jnp.dot(a, b, preferred_element_type=F32)


def dot_nt(a, b):
    return lax.dot_general(a, b, (((1,), (1,)), ((), ())), preferred_element_type=F32)


def dot_tn(a, b):
    return lax.dot_general(a, b, (((0,), (0,)), ((), ())), preferred_element_type=F32)


def norm_parts(v):
    c = v - jnp.mean(v, axis=-1, keepdims=True)
    r = lax.rsqrt(jnp.mean(c * c, axis=-1, keepdims=True) + EPS)
    return c * r, r


def norm_back(n, r, y, gain):
    yg = y * gain
    return r * (
        yg - jnp.mean(yg, axis=-1, keepdims=True) - n * jnp.mean(yg * n, axis=-1, keepdims=True)
    )


def low_half(shape):
    return lax.broadcasted_iota(jnp.int32, shape, 1) < (LANES // 2)

MESHID = pl.DeviceIdType.MESH


def here():
    dp = lax.axis_index("dp")
    return dp // 4, (dp // 2) % 2, dp % 2, lax.axis_index("head")


def at_dp(z, y, x):
    return {"dp": (z * 2 + y) * 2 + x}


FLIPS = ((0, 0, 1), (0, 1, 0), (1, 0, 0), (0, 1, 1), (1, 0, 1), (1, 1, 0), (1, 1, 1))


def flipped(place, flip):
    z, y, x, head = place
    turn = lambda v, f: 1 - v if f else v
    fh, fy, fx = turn(head, flip[0]), turn(y, flip[1]), turn(x, flip[2])
    return dict(at_dp(z, fy, fx), head=fh), (fh, fy, fx)


def greet(depth):
    place = z, y, x, head = here()
    found = [flipped(place, flip)[0] for flip in FLIPS]
    found += [at_dp((z + k) % depth, y, x) for k in range(1, depth)]
    barrier = pltpu.get_barrier_semaphore()
    for dev in found:
        pl.semaphore_signal(barrier, inc=1, device_id=dev, device_id_type=MESHID)
    pl.semaphore_wait(barrier, len(found))


class Wire:
    def __init__(self, send, recv):
        self.send, self.recv, self.next, self.open = send, recv, 0, []

    def slot(self):
        self.next += 1
        return self.next - 1

    def copy(self, i, src, dst, dev):
        return pltpu.make_async_remote_copy(
            src_ref=src, dst_ref=dst, send_sem=self.send.at[i], recv_sem=self.recv.at[i],
            device_id=dev, device_id_type=MESHID,
        )

    def start(self, i, make):
        self.copy(i, *make()).start()
        self.open.append((i, make))

    def arrived(self, i, ref, dev):
        self.copy(i, ref, ref, dev).wait_recv()

    def sent(self):
        for i, make in self.open:
            self.copy(i, *make()).wait_send()
        self.open = []


class Local:
    def __init__(self, sems):
        self.sems, self.next, self.open = sems, 0, []

    def start(self, make):
        i = self.next
        self.next += 1
        pltpu.make_async_copy(*make(), self.sems.at[i]).start()
        wait = lambda: pltpu.make_async_copy(*make(), self.sems.at[i]).wait()
        self.open.append(wait)
        return wait


def hops(p, y, x):
    ey, ex = (1 - y, x), (y, 1 - x)
    return (ey, ex) if p == 0 else (ex, ey)


def gather_stages(wire, depth, own, slot, plane=None):
    z, y, x, head = here()
    ids = {}
    for p in range(2):
        for k in range(depth):
            for kind in "zabc" + ("" if plane is None else "s"):
                ids[p, kind, k] = wire.slot()
    up = lambda k: (z + k) % depth
    down = lambda k: (z + depth - k) % depth

    def columns(p):
        (ay, ax), (by, bx) = hops(p, y, x)
        return (y, x), (ay, ax), (by, bx), (1 - y, 1 - x)

    def send_up(k):
        for p in range(2):
            wire.start(ids[p, "z", k], lambda p=p: (own(p), slot(p, z, y, x), at_dp(up(k), y, x)))

    def send_square(p, k, kind, col, to, first=False):
        def make():
            cs = columns(p)
            dst = slot(p, down(k), *cs[col])
            return own(p) if first else dst, dst, at_dp(z, *cs[to])
        wire.start(ids[p, kind, k], make)

    def wait(p, k, kind, col, frm):
        cs = columns(p)
        dev = at_dp(down(k), y, x) if frm is None else at_dp(z, *cs[frm])
        wire.arrived(ids[p, kind, k], slot(p, down(k), *cs[col]), dev)

    def begin():
        send_up(1)
        for p in range(2):
            send_square(p, 0, "a", 0, 1, True)
            send_square(p, 0, "b", 0, 2, True)
        for k in range(2, depth if plane is None else 2):
            send_up(k)

    def from_column(k):
        for p in range(2):
            wait(p, k, "z", 0, None)
            send_square(p, k, "a", 0, 1)
        for p in range(2):
            send_square(p, k, "b", 0, 2)
        if plane is not None and k + 1 < depth:
            send_up(k + 1)

    def from_first(k):
        for p in range(2):
            wait(p, k, "a", 1, 1)
            send_square(p, k, "c", 1, 2)

    def from_second(k):
        for p in range(2):
            wait(p, k, "b", 2, 2)
            wait(p, k, "c", 3, 2)

    def across(k):
        from_second(k)
        for p in range(2):
            def make(p=p):
                block = plane(p, down(k), head)
                return block, block, {"head": 1 - head}
            wire.start(ids[p, "s", k], make)

    def crossed(k):
        for p in range(2):
            wire.arrived(ids[p, "s", k], plane(p, down(k), 1 - head), {"head": 1 - head})

    part = functools.partial
    stages = {"begin": begin}
    for k in range(depth):
        for name, stage in (("z", from_column), ("a", from_first), ("d", from_second), ("s", across), ("x", crossed)):
            stages[name + str(k)] = part(stage, k)
    return stages


def add_into(dst, src):
    dst[...] = (dst[...].astype(F32) + src[...].astype(F32)).astype(dst.dtype)


class SquareSum:
    def __init__(self, wire, theirs, mine, pair_in, square_in, line_in):
        self.wire, self.theirs, self.mine = wire, theirs, mine
        self.pair_in, self.square_in, self.line_in = pair_in, square_in, line_in
        self.ids = {(p, kind): wire.slot() for p in range(2) for kind in "hab"}
        self.place = here()

    def devices(self, p):
        z, y, x, head = self.place
        ex, ey = at_dp(z, y, 1 - x), at_dp(z, 1 - y, x)
        return (ex, ey) if p == 0 else (ey, ex)

    def copy(self, p, kind):
        z, y, x, head = self.place
        if kind == "h":
            src, dst, dev = self.theirs(p), self.pair_in(p), {"head": 1 - head}
        elif kind == "a":
            src = self.mine(p, None, 1 - x) if p == 0 else self.mine(p, 1 - y, None)
            dst, dev = self.square_in(p), self.devices(p)[0]
        else:
            src = self.mine(p, 1 - y, x) if p == 0 else self.mine(p, y, 1 - x)
            dst, dev = self.line_in(p), self.devices(p)[1]
        return self.wire.copy(self.ids[p, kind], src, dst, dev)

    def pair(self):
        for p in range(2):
            self.copy(p, "h").start()

    def first(self):
        for p in range(2):
            self.wire.arrived(self.ids[p, "h"], self.pair_in(p), {"head": 1 - self.place[3]})
            add_into(self.mine(p, None, None), self.pair_in(p))
            self.copy(p, "a").start()

    def second(self):
        z, y, x, head = self.place
        for p in range(2):
            self.wire.arrived(self.ids[p, "a"], self.square_in(p), self.devices(p)[0])
            add_into(self.mine(p, None, x) if p == 0 else self.mine(p, y, None), self.square_in(p))
            self.copy(p, "b").start()

    def third(self):
        z, y, x, head = self.place
        for p in range(2):
            self.wire.arrived(self.ids[p, "b"], self.line_in(p), self.devices(p)[1])
            add_into(self.mine(p, y, x), self.line_in(p))

    def sent(self):
        for p in range(2):
            for kind in "hab":
                self.copy(p, kind).wait_send()


class ColumnSum:
    def __init__(self, wire, depth, part, column_in):
        self.wire, self.depth, self.part, self.column_in = wire, depth, part, column_in
        self.ids = {(p, k): wire.slot() for p in range(2) for k in range(1, depth)}
        self.place = here()

    def send(self, k):
        def make(p):
            z, y, x, head = self.place
            to = (z + self.depth - k) % self.depth
            return self.part(p, to), self.column_in(p, k), at_dp(to, y, x)

        for p in range(2):
            self.wire.start(self.ids[p, k], functools.partial(make, p))

    def total(self, p):
        z, y, x, head = self.place
        acc = self.part(p, z)[...].astype(F32)
        for k in range(1, self.depth):
            back = at_dp((z + k) % self.depth, y, x)
            self.wire.arrived(self.ids[p, k], self.column_in(p, k), back)
            acc = acc + self.column_in(p, k)[...].astype(F32)
        return acc


class SmallSum:
    def __init__(self, wire, depth, level, line):
        self.wire, self.depth, self.level, self.line = wire, depth, level, line
        self.ids = {flip: wire.slot() for flip in FLIPS}
        self.ups = [wire.slot() for _ in range(depth)]
        self.place = here()

    def begin(self, fill):
        z, y, x, head = self.place
        fill(self.level.at[head, y, x])
        for flip in FLIPS:
            def make(flip=flip):
                own = self.level.at[head, y, x]
                return own, own, flipped(self.place, flip)[0]
            self.wire.start(self.ids[flip], make)

    def meet(self):
        z, y, x, head = self.place
        for flip in FLIPS:
            dev, spot = flipped(self.place, flip)
            self.wire.arrived(self.ids[flip], self.level.at[spot], dev)
        total = self.level[0, 0, 0]
        for n in range(1, 8):
            total = total + self.level[n // 4, n // 2 % 2, n % 2]
        self.line[z] = total
        for k in range(1, self.depth):
            self.wire.start(
                self.ups[k],
                lambda k=k: (self.line.at[z], self.line.at[z], at_dp((z + k) % self.depth, y, x)),
            )

    def result(self):
        z, y, x, head = self.place
        for k in range(1, self.depth):
            back = (z + self.depth - k) % self.depth
            self.wire.arrived(self.ups[k], self.line.at[back], at_dp(back, y, x))
        total = self.line[0]
        for n in range(1, self.depth):
            total = total + self.line[n]
        return total


def bind(names, refs):
    assert len(names) == len(refs)
    return types.SimpleNamespace(**dict(zip(names, refs)))


def spread_mask(masked, tmp, ch):
    images, rows = masked.shape
    tmp[...] = jnp.zeros_like(tmp)
    tmp[0:images, 0:rows] = masked[...].astype(F32)
    turned = tmp[...].T
    for i in range(images):
        ch[i] = turned[0:rows, i:i + 1]


def pad_index(raw, idx):
    idx[...] = jnp.zeros_like(idx)
    idx[0:raw.shape[0], 0:raw.shape[1]] = raw[...]


def run_all(stages):
    for stage in stages:
        stage()


def vmem(n):
    return [pl.BlockSpec(memory_space=pltpu.VMEM)] * n

ANY = pl.BlockSpec(memory_space=pl.ANY)
sd = jax.ShapeDtypeStruct
dma = lambda n: pltpu.SemaphoreType.DMA((n,))
VECTORS = ("mask_token", "ln1_gain", "ln1_bias", "proj_bias", "gamma1", "ln2_gain", "ln2_bias", "fc2_bias", "gamma2")
GIVEN = ("x", "masked", "kv", "raw") + VECTORS + ("cot",)
KEPT = (
    "idx", "valid", "tmp", "ch", "bias", "nt", "q", "k", "v", "att", "res", "n2", "db", "act", "dpre", "dn",
    "small1", "small2", "gb1", "lsem",
)
SHARED = (
    "w", "wp", "mix", "b1", "b1line", "b1row", "g", "pair_in", "square_in", "line_in", "column", "column_in",
    "ar_pair", "ar_square", "ar_line", "ar_column", "gathered", "bufs", "line", "tbufs", "tline", "lbufs", "lline", "send", "recv",
)


class Row:
    def __init__(self, ref):
        self.ref = ref

    def __getitem__(self, at):
        return self.ref[...].reshape(1, -1)


def layer_kernel(direct, *refs):
    if direct:
        names = GIVEN + ("mixown", "wown", "wpown", "own1", "own2", "spot")
        names += ("out", "gx", "p", "w1", "w2", "full", "proj", "gff1", "gff2", "small", "table", "late") + KEPT + SHARED
    else:
        names = GIVEN + ("mix", "w", "wp", "w1", "w2", "b1")
        names += ("out", "gx", "p", "g1", "g2", "gw", "gt", "small1_out", "small2_out", "gb1_out") + KEPT
    r = bind(names, refs)
    for name in VECTORS:
        setattr(r, name, Row(getattr(r, name)))
    images, rows, width = r.x.shape
    heads, rp, keys = r.bias.shape
    flat = images * rp
    scale = (width // heads) ** -0.5
    pairs, per = heads // 2, heads // 4
    steps, block = r.b1.shape[-2:]
    own_heads = heads // r.mix.shape[0]
    own_tiles = width // r.mix.shape[0] // LANES
    chunks = (r.mix.shape[1] - 2 * own_tiles) // own_heads
    local = Local(r.lsem)
    z, y, x, head = here()
    plan = {}
    part = functools.partial
    every = lambda v: slice(None) if v is None else v
    level = lambda b: (z + 2 * steps - b) % steps
    at_image = lambda i: pl.multiple_of(i * rp, 16)

    if direct:
        depth = r.w1.shape[0]
        half = r.wown.shape[2]
        lanes_of = lambda hd: pl.ds(pl.multiple_of(hd * half, LANES), half)
        full = (r.w1, r.w2)
        wire = Wire(r.send, r.recv)
        greet(depth)
        other = {"head": 1 - head}
        swaps = [
            (r.mixown, lambda hd: r.mix.at[hd]),
            (r.wown, lambda hd: r.w.at[:, :, lanes_of(hd)]),
            (r.wpown, lambda hd: r.wp.at[lanes_of(hd)]),
        ]
        swap_ids = [wire.slot() for _ in swaps]
        bias_id = wire.slot()
        bias_of = lambda hd: r.bias.at[pl.ds(hd * own_heads, own_heads)]
        for i, (src, place) in zip(swap_ids, swaps):
            wire.start(i, lambda src=src, place=place: (src, place(head), other))
        for src, place in swaps:
            local.start(lambda src=src, place=place: (src, place(head)))
        slot = lambda p, zz, yy, xx: full[p].at[zz, yy, xx, head]
        own = (r.own1, r.own2)
        for p in range(2):
            local.start(lambda p=p: (own[p], slot(p, z, y, x)))
        bias_sum = SmallSum(wire, depth, r.b1, r.b1line)
        ag = gather_stages(
            wire, depth, own=lambda p: own[p], slot=slot,
            plane=lambda p, zz, hd: full[p].at[zz, :, :, hd],
        )
        ag["begin"]()

        def fill_bias(ref):
            ref[...] = r.spot[...]

        bias_sum.begin(fill_bias)
        squares = [
            SquareSum(
                wire,
                theirs=lambda p, b=b: r.g.at[b % 3, p, :, :, 1 - head],
                mine=lambda p, yy, xx, b=b: r.g.at[b % 3, p, every(yy), every(xx), head],
                pair_in=lambda p, b=b: r.pair_in.at[b % 2, p],
                square_in=lambda p, b=b: r.square_in.at[b % 2, p],
                line_in=lambda p, b=b: r.line_in.at[b % 2, p],
            )
            for b in range(steps)
        ]
        column = ColumnSum(wire, depth, part=lambda p, zz: r.column.at[p, zz], column_in=lambda p, k: r.column_in.at[p, k - 1])

        def close(b):
            squares[b].third()
            for p in range(2):
                r.column[p, level(b)] = r.g[b % 3, p, y, x, head]
            if b:
                column.send(b)
            squares[b].sent()

        early = SmallSum(wire, depth, r.bufs, r.line)
        tables = SmallSum(wire, depth, r.tbufs, r.tline)
        late = SmallSum(wire, depth, r.lbufs, r.lline)
        plan = {
            "p2": [ag["z1"], ag["a0"]], "t0": [bias_sum.meet],
            "t2": [ag["s0"], ag["a1"]], "t5": [ag["z2"], ag["s1"]], "t7": [ag["a2"]],
        }

    def tick(point):
        run_all(plan.get(point, ()))

    def tick_in(step, point):
        for key, stages in plan.items():
            if isinstance(key, tuple) and key[1] == point:
                pl.when(step == key[0])(part(run_all, stages))

    spread_mask(r.masked, r.tmp, r.ch)
    pad_index(r.raw, r.idx)
    r.valid[...] = jnp.zeros_like(r.valid)
    r.valid[0:r.kv.shape[0], 0:rows] = r.kv[...]

    def hidden_of(i):
        ch = r.ch[i]
        return r.x[i].astype(F32) * (1.0 - ch) + ch * r.mask_token[...]

    def attention_forward(normed, pring):
        normed[...] = jnp.zeros_like(normed)
        r.n2[...] = jnp.zeros_like(r.n2)
        r.res[...] = jnp.zeros_like(r.res)

        def first_norm(i, carry):
            n, _ = norm_parts(hidden_of(i))
            normed[pl.ds(at_image(i), rows), :] = (n * r.ln1_gain[...] + r.ln1_bias[...]).astype(BF16)
            return carry

        lax.fori_loop(0, images, first_norm, 0)
        if direct:
            for wait in local.open:
                wait()
            local.open = []

        def gather_head(h, carry):
            for side in range(keys // LANES):
                idx = r.idx[:, side * LANES:(side + 1) * LANES]
                low = idx & (LANES - 1)
                high = idx >> 7
                acc = jnp.zeros(idx.shape, F32)
                for c in range(chunks):
                    if direct:
                        row = r.mixown[pl.ds(h * chunks + c, 1), :]
                    else:
                        row = r.mix[h // own_heads, pl.ds((h % own_heads) * chunks + c, 1), :]
                    got = jnp.take_along_axis(jnp.broadcast_to(row, idx.shape), low, axis=1)
                    acc = jnp.where(high == c, got, acc)
                r.bias[head * own_heads + h if direct else h, :, side * LANES:(side + 1) * LANES] = acc
            return carry

        some = own_heads if direct else heads
        for n in range(3):
            lax.fori_loop(n * some // 3, (n + 1) * some // 3, gather_head, 0)
            tick("g%d" % n)
        if direct:
            wire.copy(bias_id, bias_of(head), bias_of(head), other).start()
            for n in range(3):
                wire.arrived(swap_ids[n], swaps[n][1](1 - head), other)
        zeros_tail = jnp.zeros((images, keys - rp, width), BF16)
        r.k[:, rp:, :] = zeros_tail
        r.v[:, rp:, :] = zeros_tail

        def bias_row(kind, nb):
            tiles = []
            for t in (2 * nb, 2 * nb + 1):
                at = own_heads * chunks + kind * own_tiles + t % own_tiles
                tiles.append(r.mix[t // own_tiles, at:at + 1, :])
            return jnp.concatenate(tiles, axis=1)

        for c, (dst, kind) in enumerate(((r.q, 0), (r.k, None), (r.v, 1))):
            for nb in range(width // 256):
                cols = slice(nb * 256, (nb + 1) * 256)
                acc = dot(normed[...], r.w[c, :, cols])
                if kind is not None:
                    acc = acc + bias_row(kind, nb)
                acc = acc.astype(BF16)
                if kind == 0:
                    acc = acc * scale
                for i in range(images):
                    dst[i, :rp, cols] = acc[i * rp:(i + 1) * rp]
            tick("p%d" % c)
        r.nt[...] = normed[...].T
        if direct:
            wire.arrived(bias_id, bias_of(1 - head), other)

        def attend(t, carry):
            i = t // pairs
            j = t % pairs
            lanes = pl.ds(pl.multiple_of(j * LANES, LANES), LANES)
            qp = r.q[i, :, lanes]
            kp = r.k[i, :, lanes]
            vp = r.v[i, :, lanes]
            lo = low_half((rp, LANES))
            ok = r.valid[pl.ds(head * images + i, 1), :] > 0
            outs = []
            for s in range(2):
                qs = jnp.where(lo if s == 0 else jnp.logical_not(lo), qp, jnp.zeros_like(qp))
                sc = dot_nt(qs, kp) + r.bias[2 * j + s]
                sc = jnp.where(ok, sc, -1e30)
                e = jnp.exp(sc - jnp.max(sc, axis=-1, keepdims=True))
                prob = e * (1.0 / jnp.sum(e, axis=-1, keepdims=True))
                pring[i % 2, 2 * j + s] = prob
                outs.append(dot(prob.astype(BF16), vp))
            r.att[pl.ds(at_image(i), rp), lanes] = jnp.where(lo, outs[0], outs[1]).astype(BF16)
            return carry

        stored = {}
        for n in range(2 * images):
            i = n // 2
            if n % 2 == 0 and i >= 2:
                stored[i - 2]()
            lax.fori_loop(n * pairs // 2, (n + 1) * pairs // 2, attend, 0)
            if n % 2:
                stored[i] = local.start(lambda i=i: (pring.at[i % 2], r.p.at[i]))
            tick("t%d" % n)

        def finish(t, carry):
            both = dot(r.att[pl.ds(at_image(2 * t), 2 * rp), :], r.wp[...]) + r.proj_bias[...]
            for side in range(2):
                i = 2 * t + side
                res = hidden_of(i) + r.gamma1[...] * both[side * rp:side * rp + rows]
                r.res[pl.ds(at_image(i), rows), :] = res
                n, _ = norm_parts(res)
                r.n2[pl.ds(at_image(i), rows), :] = (n * r.ln2_gain[...] + r.ln2_bias[...]).astype(BF16)
            return carry

        lax.fori_loop(0, images // 2, finish, 0)
        stored[images - 2]()
        stored[images - 1]()

    pl.run_scoped(attention_forward, pltpu.VMEM((flat, width), BF16), pltpu.VMEM((2, heads, rp, keys), F32))

    if direct:
        wire.copy(bias_id, bias_of(head), bias_of(head), other).wait_send()
        ag["x0"]()
        r.b1row[...] = bias_sum.result()
        plan = {
            (0, 0): [ag["x1"]], (0, 1): [ag["z3"]], (0, 2): [ag["s2"]], (0, 4): [ag["a3"], squares[0].pair],
            (1, 0): [ag["x2"]], (1, 1): [squares[0].first, ag["s3"]], (1, 4): [squares[1].pair],
            (2, 0): [ag["x3"]], (2, 1): [squares[0].second, squares[1].first], (2, 4): [squares[2].pair],
            (3, 1): [part(close, 0), squares[1].second, squares[2].first], (3, 4): [squares[3].pair],
        }

    def feed_forward(cot, branch, slots, sems):
        def weights(b, into):
            copies = []
            for p, src in enumerate((r.w1, r.w2)):
                if direct:
                    view = src.at[level(b)]
                else:
                    view = src.at[pl.ds(pl.multiple_of(level(b) * block, 16), block)]
                copies.append(pltpu.make_async_copy(view, slots.at[into, p], sems.at[into, p]))
            return copies

        for copy in weights(0, 0):
            copy.start()
        fetch = pltpu.make_async_copy(r.cot, cot, sems.at[2, 0])
        fetch.start()
        r.db[...] = jnp.zeros_like(r.db)
        branch[...] = jnp.zeros_like(branch)
        r.dn[...] = jnp.zeros_like(r.dn)
        fetch.wait()

        def fill(i, carry):
            r.db[pl.ds(at_image(i), rows), :] = (cot[i].astype(F32) * r.gamma2[...]).astype(BF16)
            return carry

        lax.fori_loop(0, images, fill, 0)

        def step(b, carry):
            slot = b % 2
            t = level(b)
            for copy in weights(b, slot):
                copy.wait()
            tick_in(b, 0)

            @pl.when(b + 1 < steps)
            def _():
                for copy in weights(b + 1, 1 - slot):
                    copy.start()

            w1 = lambda: slots[slot, 0].reshape(block, width)
            w2 = lambda: slots[slot, 1].reshape(block, width)
            b1 = (r.b1row if direct else r.b1)[pl.ds(t, 1), :]

            def tile(i, gb1):
                at = pl.ds(pl.multiple_of(i * 2 * rp, 16), 2 * rp)
                pre = dot_nt(r.n2[at, :], w1()) + b1
                cdf = 0.5 * (1.0 + lax.erf(pre * 0.7071067811865476))
                slope = cdf + pre * (0.3989422804014327 * jnp.exp(-0.5 * pre * pre))
                act = (pre * cdf).astype(BF16)
                r.act[at, :] = act
                dpre = (dot_nt(r.db[at, :], w2()) * slope).astype(BF16)
                r.dpre[at, :] = dpre
                branch[at, :] += dot(act, w2())
                r.dn[at, :] += dot(dpre, w1())
                return gb1 + jnp.sum(dpre.astype(F32), axis=0, keepdims=True)

            gb1 = lax.fori_loop(0, images // 4, tile, jnp.zeros((1, block), F32))
            tick_in(b, 1)
            r.gb1[pl.ds(t, 1), :] = lax.fori_loop(images // 4, images // 2, tile, gb1)
            tick_in(b, 2)

            def store(p, value):
                value = value.astype(BF16)
                if direct:
                    r.g[b % 3, p] = value.reshape(r.g.shape[2:])
                else:
                    slots[slot, p] = value
                    dst = (r.g1, r.g2)[p].at[pl.ds(pl.multiple_of(t * block, 16), block)]
                    copy = pltpu.make_async_copy(slots.at[slot, p], dst, sems.at[3, p])
                    copy.start()
                    copy.wait()

            second = dot_tn(r.act[...], r.db[...])
            store(1, second)
            tick_in(b, 3)
            store(0, dot_tn(r.dpre[...], r.n2[...]))
            tick_in(b, 4)
            return carry

        lax.fori_loop(0, steps, step, 0)
        r.small2[...] = jnp.zeros_like(r.small2)
        r.n2[...] = jnp.zeros_like(r.n2)

        def add(row, value):
            r.small2[row:row + 1, :] += jnp.sum(value, axis=0, keepdims=True)

        def finish(i, carry):
            span = pl.ds(at_image(i), rows)
            up = cot[i].astype(F32)
            mlp = branch[span, :] + r.fc2_bias[...]
            res = r.res[span, :]
            cot[i] = (res + r.gamma2[...] * mlp).astype(BF16)
            add(S_GA2, up * mlp)
            add(S_FB2, (up * r.gamma2[...]).astype(BF16).astype(F32))
            n, inv = norm_parts(res)
            dn = r.dn[span, :]
            add(S_LG2, dn * n)
            add(S_LB2, dn)
            dres = up + norm_back(n, inv, dn, r.ln2_gain[...])
            add(S_GA1, dres * (res - hidden_of(i)))
            r.res[span, :] = dres
            dproj = (dres * r.gamma1[...]).astype(BF16)
            r.n2[span, :] = dproj
            add(S_PB, dproj.astype(F32))
            return carry

        lax.fori_loop(0, images, finish, 0)
        r.small2[S_GA1:S_GA1 + 1, :] = r.small2[S_GA1:S_GA1 + 1, :] / r.gamma1[...]
        store_out = pltpu.make_async_copy(cot, r.out, sems.at[2, 1])
        store_out.start()
        store_out.wait()

    if direct:
        slots_shape = (2, 2) + r.w1.shape[1:]
    else:
        slots_shape = (2, 2, block, width)
    pl.run_scoped(
        feed_forward, pltpu.VMEM(r.cot.shape, BF16), pltpu.VMEM((flat, width), F32),
        pltpu.VMEM(slots_shape, BF16), pltpu.SemaphoreType.DMA((4, 2)),
    )
    plan = {}

    def attention_backward(pbuf, dpt, g, sems):
        nonlocal plan
        dqkv = (r.act, r.dpre, r.n2)
        pair_of = lambda s: (s % 2) * per + s // 2

        def fetch(t):
            src = r.p.at[t % images, pl.ds(2 * pair_of(t // images), 2)]
            return pltpu.make_async_copy(src, pbuf.at[t % 3], sems.at[t % 3])

        for t in range(2):
            fetch(t).start()
        if direct:
            ar, lines, gathers = [], [], []
            for m in range(per):
                ar.append(SquareSum(
                    wire,
                    theirs=lambda p, m=m: g.at[m, 1 - head, p],
                    mine=lambda p, yy, xx, m=m: g.at[m, head, p, :, :, every(yy), every(xx)],
                    pair_in=lambda p, m=m: r.ar_pair.at[m, p],
                    square_in=lambda p, m=m: r.ar_square.at[m, p], line_in=lambda p, m=m: r.ar_line.at[m, p],
                ))
                lines.append(ColumnSum(
                    wire, depth, part=lambda p, zz, m=m: g.at[m, head, p, :, zz, y, x],
                    column_in=lambda p, k, m=m: r.ar_column.at[m, p, k - 1],
                ))
                lanes_m = slice(m * LANES, (m + 1) * LANES)
                into = lambda p, zz, yy, xx, lanes_m=lanes_m: r.gathered.at[p, :, zz, yy, xx, :, lanes_m]
                gathers.append(gather_stages(wire, depth, own=lambda p, into=into: into(p, z, y, x), slot=into))

            def third(m):
                ar[m].third()
                for k in range(1, depth):
                    lines[m].send(k)

            def last(m):
                for p in range(2):
                    r.gathered[p, :, z, y, x, :, m * LANES:(m + 1) * LANES] = lines[m].total(p).astype(BF16)
                gathers[m]["begin"]()

            def ff_last():
                for p in range(2):
                    (r.gff1, r.gff2)[p][...] = column.total(p)

            def early_begin():
                def fill(ref):
                    ref[...] = jnp.zeros(ref.shape, F32)
                    ref[0:8] = r.small2[...]
                    ref[8:8 + steps] = r.gb1[...]
                early.begin(fill)

            g0, g1, g2 = gathers
            plan = {
                "start": [part(close, 1), squares[2].second, squares[3].first, early_begin],
                (0, 4): [part(close, 2)], (1, 1): [squares[3].second, early.meet], (1, 4): [ar[0].pair],
                (2, 2): [ar[0].first], (2, 3): [part(close, 3)],
                (3, 2): [ar[0].second], (3, 4): [ar[1].pair], (4, 1): [part(third, 0)], (4, 2): [ar[1].first],
                (5, 1): [part(last, 0)], (5, 2): [ar[1].second], (5, 4): [ar[2].pair, g0["z1"], g0["z2"], g0["z3"]],
                (5, 5): [ar[2].first, part(third, 1)], (5, 6): [g0["a0"], g0["a1"], g0["a2"], g0["a3"]],
                (5, 7): [part(last, 1)], (5, 8): [ar[2].second], (5, 9): [g1["z1"], g1["z2"], g1["z3"]],
                (5, 10): [part(third, 2)], (5, 11): [g0["d0"], g0["d1"], g0["d2"], g0["d3"]],
                (5, 12): [part(last, 2), tables.meet, g1["a0"], g1["a1"], g1["a2"], g1["a3"]],
            }

        tick("start")
        for t in range(images // 2):
            at = slice(2 * t * rp, 2 * (t + 1) * rp)
            r.db[at, :] = dot_nt(r.n2[at, :], r.wp[...]).astype(BF16)
        dpt[...] = r.n2[...].T
        r.small1[...] = jnp.zeros_like(r.small1)

        def step(s, carry):
            j = pair_of(s)
            tick_in(s, 1)
            lanes = pl.ds(pl.multiple_of(j * LANES, LANES), LANES)
            r.bias[2 * j] = jnp.zeros((rp, keys), F32)
            r.bias[2 * j + 1] = jnp.zeros((rp, keys), F32)

            def image(i, carry):
                t = s * images + i
                fetch(t).wait()

                @pl.when(t + 2 < pairs * images)
                def _():
                    fetch(t + 2).start()

                at = pl.ds(at_image(i), rp)
                qp = r.q[i, :, lanes]
                kp = r.k[i, :, lanes]
                vp = r.v[i, :, lanes]
                da = r.db[at, lanes]
                lo = low_half((rp, LANES))
                dv, dq, dk = [], [], []
                for n in range(2):
                    das = jnp.where(lo if n == 0 else jnp.logical_not(lo), da, jnp.zeros_like(da))
                    prob = pbuf[t % 3, n]
                    dp = dot_nt(das, vp)
                    dsc = prob * (dp - jnp.sum(prob * dp, axis=-1, keepdims=True))
                    dsb = dsc.astype(BF16)
                    r.bias[2 * j + n] += dsb.astype(F32)
                    dv.append(dot_tn(prob.astype(BF16), da))
                    dq.append(dot(dsb, kp))
                    dk.append(dot_tn(dsb, qp))
                lok = low_half((keys, LANES))
                dqkv[0][at, lanes] = (jnp.where(lo, dq[0], dq[1]) * scale).astype(BF16)
                dqkv[1][at, lanes] = jnp.where(lok, dk[0], dk[1])[:rp].astype(BF16)
                dqkv[2][at, lanes] = jnp.where(lok, dv[0], dv[1])[:rp].astype(BF16)
                return carry

            lax.fori_loop(0, images // 2, image, 0)
            tick_in(s, 2)
            lax.fori_loop(images // 2, images, image, 0)
            tick_in(s, 3)

            def store(c, value):
                value = value.astype(BF16)
                if direct:
                    g[s // 2, s % 2, c // 2, c % 2] = value.reshape(g.shape[4:])
                else:
                    g[...] = value
                    copy = pltpu.make_async_copy(g, r.gw.at[j, c], sems.at[3])
                    copy.start()
                    copy.wait()

            three = dot(r.nt[...], jnp.concatenate([dqkv[c][:, lanes] for c in range(3)], axis=1))
            for c in range(3):
                store(c, three[:, c * LANES:(c + 1) * LANES])
            store(3, dot(dpt[...], r.att[:, lanes]))
            tick_in(s, 4)
            return carry

        lax.fori_loop(0, pairs, step, 0)
        now = lambda point: run_all(plan.get((pairs - 1, point), ()))

        def total_rows(row, c):
            def add(i, acc):
                return acc + jnp.sum(dqkv[c][pl.ds(at_image(i), rp), :].astype(F32), axis=0, keepdims=True)
            r.small1[row:row + 1, :] = lax.fori_loop(0, images, add, jnp.zeros((1, width), F32))

        total_rows(T_QB, 0)
        total_rows(T_VB, 2)

        a_iota = lax.broadcasted_iota(jnp.int32, (8, keys), 0)
        b_iota = lax.broadcasted_iota(jnp.int32, (LANES, keys), 0)

        def scatter(t, acc):
            at = pl.ds(pl.multiple_of(t * 8, 8), 8)
            idx = r.idx[at, :]
            high, low = idx >> 7, idx & (LANES - 1)
            tiles = [r.bias[h, at, :] for h in range(heads)]
            lefts, rests, ones = [], [], []
            for n in range(8):
                pick = jnp.broadcast_to(high[n:n + 1], (8, keys)) == a_iota
                ones.append((jnp.broadcast_to(low[n:n + 1], (LANES, keys)) == b_iota).astype(F32).astype(BF16))
                left = jnp.concatenate(
                    [jnp.where(pick, jnp.broadcast_to(tile[n:n + 1], (8, keys)), 0.0) for tile in tiles], axis=0)
                top = left.astype(BF16)
                lefts.append(top)
                rests.append((left - top.astype(F32)).astype(BF16))
            one = jnp.concatenate(ones, axis=1)
            return acc + dot_nt(jnp.concatenate(lefts, axis=1), one) + dot_nt(jnp.concatenate(rests, axis=1), one)

        table = jnp.zeros((heads * 8, LANES), F32)
        blocks = rp // 8
        for n in range(5):
            table = lax.fori_loop(n * blocks // 5, (n + 1) * blocks // 5, scatter, table)
            now(5 + n)
        wide = width // LANES
        tall = heads * 8 // wide
        if direct:
            def fill_table(ref):
                for t in range(wide):
                    ref[:, t * LANES:(t + 1) * LANES] = table[t * tall:(t + 1) * tall]
            tables.begin(fill_table)
        def finish(i, carry):
            span = pl.ds(at_image(i), rp)
            dn = dot_nt(dqkv[0][span, :], r.w[0])
            dn += dot_nt(dqkv[1][span, :], r.w[1])
            dn += dot_nt(dqkv[2][span, :], r.w[2])
            dn = dn[:rows]
            ch = r.ch[i]
            n, inv = norm_parts(hidden_of(i))
            dh = r.res[pl.ds(at_image(i), rows), :] + norm_back(n, inv, dn, r.ln1_gain[...])
            r.dn[pl.ds(at_image(i), rows), :] = dh * (1.0 - ch)
            for row, value in ((T_MASK, dh * ch), (T_LG1, dn * n), (T_LB1, dn)):
                r.small1[row:row + 1, :] += jnp.sum(value, axis=0, keepdims=True)
            return carry

        leaving = []
        for i in range(images):
            lax.fori_loop(i, i + 1, finish, 0)
            leaving.append(local.start(lambda i=i: (r.dn.at[pl.ds(i * rp, rows)], r.gx.at[i])))
            now(10 + i)

        for wait in leaving:
            wait()
        if not direct:
            r.gt[...] = table
            r.small1_out[...] = r.small1[...]
            r.small2_out[...] = r.small2[...]
            r.gb1_out[...] = r.gb1[...]
            return

        def fill_late(ref):
            ref[...] = r.small1[...]

        late.begin(fill_late)
        r.small[...] = early.result()
        ff_last()
        run_all(g2["z%d" % k] for k in range(1, depth))
        late.meet()
        run_all(g1["d%d" % k] for k in range(depth))
        run_all(g2["a%d" % k] for k in range(depth))
        r.table[...] = tables.result()
        run_all(g2["d%d" % k] for k in range(depth))
        keep = [
            local.start(lambda: (r.gathered.at[0], r.full.at[0:2])),
            local.start(lambda: (r.gathered.at[1, 0], r.full.at[2])),
        ]
        tall_p = r.proj.shape[0]
        r.n2[0:tall_p, :] = r.gathered[1, 1].reshape(width, tall_p).T
        keep_proj = local.start(lambda: (r.n2.at[0:tall_p], r.proj))
        r.late[...] = late.result()
        keep_proj()
        for m in range(per):
            ar[m].sent()
        wire.sent()
        for wait in keep:
            wait()

    if direct:
        g_shape = (per, 2, 2, 2, depth, 2, 2) + r.gathered.shape[5:6] + (LANES,)
    else:
        g_shape = (width, LANES)
    pl.run_scoped(
        attention_backward, pltpu.VMEM((3, 2, rp, keys), F32), pltpu.VMEM((width, flat), BF16),
        pltpu.VMEM(g_shape, BF16), dma(4),
    )


def layer(direct, given, extra, heads, rp, keys, depth):
    x, kv = given[0], given[2]
    images, rows, width = x.shape
    flat = images * rp
    tall = -(-max(kv.shape[0], images) // 8) * 8
    steps = 4
    ff = extra[-1].size
    outs = [sd(x.shape, BF16), sd(x.shape, F32), sd((images, heads, rp, keys), F32)]
    out_specs = [ANY] * 3
    bf = lambda *shape: pltpu.VMEM(shape, BF16)
    fl = lambda *shape: pltpu.VMEM(shape, F32)
    scratch = [
        pltpu.VMEM((rp, keys), jnp.int32), pltpu.VMEM((tall, keys), jnp.int32), fl(tall, keys), fl(images, rows, 1),
        fl(heads, rp, keys), bf(width, flat), bf(images, rp, width), bf(images, keys, width), bf(images, keys, width),
        bf(flat, width), fl(flat, width), bf(flat, width), bf(flat, width), bf(flat, width), bf(flat, width),
        fl(flat, width), fl(8, width), fl(8, width), fl(steps, ff // steps), dma(24),
    ]
    in_specs = vmem(len(given) - 1) + [ANY]
    params = {}
    if direct:
        mixown, wown, wpown, own1, own2, spot = extra
        per = heads // 4
        share = own1.shape[0]
        own = width // (4 * depth)
        total = 8 + 8
        tall_t = heads * 8 * LANES // width
        big = sd((depth, 2, 2, 2) + own1.shape, BF16)
        outs += [big, big, sd((3, depth, 2, 2, own, per * LANES), BF16), sd((per * LANES, width), BF16)]
        outs += [sd((share, width), F32), sd((share, width), F32)]
        outs += [sd((total, width), F32), sd((tall_t, width), F32), sd((8, width), F32)]
        in_specs += vmem(6)
        out_specs += [ANY] * 4 + vmem(5)
        n = 4 + 2 * (4 * depth + 4) + 4 * (7 + depth) + 6 * steps + 2 * (depth - 1)
        n += per * (6 + 2 * (depth - 1) + 8 * depth)
        scratch += [
            bf(3, width, width), bf(width, width), fl(2, *mixown.shape), fl(2, 2, 2, *spot.shape), fl(depth, *spot.shape), fl(*spot.shape),
            bf(3, 2, 2, 2, 2, share, width), bf(2, 2, 2, 2, share, width), bf(2, 2, 2, share, width), bf(2, 2, share, width),
            bf(2, depth, share, width), bf(2, depth - 1, share, width),
            bf(per, 2, 2, depth, 2, 2, own, LANES), bf(per, 2, 2, depth, 2, own, LANES), bf(per, 2, 2, depth, own, LANES),
            bf(per, 2, depth - 1, 2, own, LANES), bf(2, 2, depth, 2, 2, own, per * LANES),
            fl(2, 2, 2, total, width), fl(depth, total, width), fl(2, 2, 2, tall_t, width), fl(depth, tall_t, width), fl(2, 2, 2, 8, width), fl(depth, 8, width), dma(n), dma(n),
        ]
        params = dict(collective_id=1, has_side_effects=True)
    else:
        part = sd((ff, width), BF16)
        outs += [part, part, sd((heads // 2, 4, width, LANES), BF16), sd((heads * 8, LANES), F32)]
        outs += [sd((8, width), F32), sd((8, width), F32), sd((steps, ff // steps), F32)]
        in_specs += vmem(3) + [ANY, ANY] + vmem(1)
        out_specs += [ANY] * 3 + vmem(4)
    return pl.pallas_call(
        functools.partial(layer_kernel, direct), name="layer",
        out_shape=tuple(outs), in_specs=in_specs, out_specs=out_specs, scratch_shapes=scratch,
        compiler_params=pltpu.CompilerParams(vmem_limit_bytes=63 * 2**20, **params),
    )(*given, *extra)


def shards(
    inputs, masked, key_valid, rel_index, mask_token, ln1_gain, ln1_bias, w_qkv, qv_bias, rel_table,
    w_proj, proj_bias, gamma1, ln2_gain, ln2_bias, w_fc1, fc1_bias, w_fc2, fc2_bias, gamma2, cotangent,
):
    images, rows, width = inputs.shape
    dp, hn = lax.axis_size("dp"), lax.axis_size("head")
    me, head = lax.axis_index("dp"), lax.axis_index("head")
    depth = dp // 4
    share = w_fc2.shape[0]
    ff = share * dp * hn
    entries, heads = rel_table.shape[0], rel_table.shape[1] * hn
    rp, keys = -(-rows // 16) * 16, -(-rows // LANES) * LANES
    direct = hn == 2 and dp == 16 and share % 16 == 0 and width % (16 * dp) == 0

    tab_rows = -(-entries // LANES)
    tab = jnp.pad(rel_table.T, ((0, 0), (0, tab_rows * LANES - entries)))
    mix = jnp.concatenate([tab.reshape(-1, LANES), qv_bias.reshape(-1, LANES)])
    vectors = (mask_token, ln1_gain, ln1_bias, proj_bias, gamma1, ln2_gain, ln2_bias, fc2_bias, gamma2)
    given = (inputs, masked, key_valid, rel_index) + vectors + (cotangent,)
    w3 = jnp.transpose(w_qkv, (1, 0, 2))
    if direct:
        spot_shape = (4, ff // 4)
        owner = (lax.broadcasted_iota(jnp.int32, spot_shape, 0) * (ff // 4) + lax.broadcasted_iota(jnp.int32, spot_shape, 1)) // share
        spot = jnp.where(owner == me * hn + head, jnp.tile(fc1_bias.astype(F32), ff // 4 // share)[None], 0.0)
        extra = (mix, w3, w_proj, w_fc1.T, w_fc2, spot)
        out, gx, _, _, _, full, proj, g_fc1, g_fc2, small, table, late = layer(True, given, extra, heads, rp, keys, depth)
        g_qkv, g_proj = full.reshape(3, width, -1).astype(F32), proj.astype(F32)
        s1, s2 = late, small[:8]
        wide = width // LANES
        tall = heads * 8 // wide
        table = jnp.transpose(table.reshape(tall, wide, LANES), (1, 0, 2)).reshape(heads, -1)
        g_b1 = small[8:12].reshape(-1)
    else:
        w = lax.all_gather(w3, "head", axis=2, tiled=True)
        wp = lax.all_gather(w_proj, "head", axis=0, tiled=True)
        w1 = lax.all_gather(w_fc1.T, ("dp", "head"), axis=0, tiled=True)
        w2 = lax.all_gather(w_fc2, ("dp", "head"), axis=0, tiled=True)
        b1 = lax.all_gather(fc1_bias, ("dp", "head"), axis=0, tiled=True).astype(F32).reshape(4, -1)
        extra = (lax.all_gather(mix, "head", axis=0), w, wp, w1, w2, b1)
        out, gx, _, ga, gb, gw, gt, s1, s2, gb1 = layer(False, given, extra, heads, rp, keys, depth)
        g_fc1 = lax.psum_scatter(ga.astype(F32), ("dp", "head"), scatter_dimension=0, tiled=True)
        g_fc2 = lax.psum_scatter(gb.astype(F32), ("dp", "head"), scatter_dimension=0, tiled=True)
        full = lax.psum(lax.psum_scatter(gw.astype(F32), "head", scatter_dimension=0, tiled=True), "dp")
        full = jnp.transpose(full, (1, 2, 0, 3)).reshape(4, width, -1)
        g_qkv, g_proj = full[:3], full[3].T
        s1, s2, table, g_b1 = lax.psum((s1, s2, gt.reshape(heads, -1), gb1.reshape(-1)), ("dp", "head"))
    g_table = lax.dynamic_slice_in_dim(table, head * (heads // hn), heads // hn, 0)[:, :entries].T
    g_b1 = lax.dynamic_slice_in_dim(g_b1, (me * hn + head) * share, share)
    g_qvb = lax.dynamic_slice_in_dim(s1[T_QB:T_VB + 1], head * (width // hn), width // hn, 1)
    return (
        out, gx, s1[T_MASK], s1[T_LG1], s1[T_LB1], jnp.transpose(g_qkv, (1, 0, 2)), g_qvb, g_table, g_proj,
        s2[S_PB], s2[S_GA1], s2[S_LG2], s2[S_LB2], g_fc1.T, g_b1, g_fc2, s2[S_FB2], s2[S_GA2],
    )


def solution(mesh):
    in_specs = (
        P(("dp", "head"), None, None),
        P(("dp", "head"), None),
        P("dp", None),
        P(),
        P(),
        P(),
        P(),
        P(None, None, "head"),
        P(None, "head"),
        P(None, "head"),
        P("head", None),
        P(),
        P(),
        P(),
        P(),
        P(None, ("dp", "head")),
        P(("dp", "head")),
        P(("dp", "head"), None),
        P(),
        P(),
        P(("dp", "head"), None, None),
    )
    out_specs = (
        P(("dp", "head"), None, None),
        P(("dp", "head"), None, None),
        P(),
        P(),
        P(),
        P(None, None, "head"),
        P(None, "head"),
        P(None, "head"),
        P("head", None),
        P(),
        P(),
        P(),
        P(),
        P(None, ("dp", "head")),
        P(("dp", "head")),
        P(("dp", "head"), None),
        P(),
        P(),
    )
    return jax.shard_map(shards, mesh=mesh, in_specs=in_specs, out_specs=out_specs, check_vma=False)
```

```python
import functools
import types
import jax
import jax.numpy as jnp
from jax import lax
from jax.experimental import pallas as pl
from jax.experimental.pallas import tpu as pltpu
from jax.sharding import PartitionSpec as P

F32 = jnp.float32
BF16 = jnp.bfloat16
EPS = 1e-06
LANES = 128
S_GA2, S_FB2, S_LG2, S_LB2, S_GA1, S_PB = range(6)
T_MASK, T_LG1, T_LB1, T_QB, T_VB = range(5)


def dot(a, b):
    return jnp.dot(a, b, preferred_element_type=F32)


def dot_nt(a, b):
    return lax.dot_general(a, b, (((1,), (1,)), ((), ())), preferred_element_type=F32)


def dot_tn(a, b):
    return lax.dot_general(a, b, (((0,), (0,)), ((), ())), preferred_element_type=F32)


def norm_parts(v):
    c = v - jnp.mean(v, axis=-1, keepdims=True)
    r = lax.rsqrt(jnp.mean(c * c, axis=-1, keepdims=True) + EPS)
    return c * r, r


def norm_back(n, r, y, gain):
    yg = y * gain
    return r * (
        yg - jnp.mean(yg, axis=-1, keepdims=True) - n * jnp.mean(yg * n, axis=-1, keepdims=True)
    )


def low_half(shape):
    return lax.broadcasted_iota(jnp.int32, shape, 1) < (LANES // 2)

MESHID = pl.DeviceIdType.MESH


def here():
    dp = lax.axis_index("dp")
    return dp // 4, (dp // 2) % 2, dp % 2, lax.axis_index("head")


def at_dp(z, y, x):
    return {"dp": (z * 2 + y) * 2 + x}


FLIPS = ((0, 0, 1), (0, 1, 0), (1, 0, 0), (0, 1, 1), (1, 0, 1), (1, 1, 0), (1, 1, 1))


def flipped(place, flip):
    z, y, x, head = place
    turn = lambda v, f: 1 - v if f else v
    fh, fy, fx = turn(head, flip[0]), turn(y, flip[1]), turn(x, flip[2])
    return dict(at_dp(z, fy, fx), head=fh), (fh, fy, fx)


def greet(depth):
    place = z, y, x, head = here()
    found = [flipped(place, flip)[0] for flip in FLIPS]
    found += [at_dp((z + k) % depth, y, x) for k in range(1, depth)]
    barrier = pltpu.get_barrier_semaphore()
    for dev in found:
        pl.semaphore_signal(barrier, inc=1, device_id=dev, device_id_type=MESHID)
    pl.semaphore_wait(barrier, len(found))


class Wire:
    def __init__(self, send, recv):
        self.send, self.recv, self.next, self.open = send, recv, 0, []

    def slot(self):
        self.next += 1
        return self.next - 1

    def copy(self, i, src, dst, dev):
        return pltpu.make_async_remote_copy(
            src_ref=src, dst_ref=dst, send_sem=self.send.at[i], recv_sem=self.recv.at[i],
            device_id=dev, device_id_type=MESHID,
        )

    def start(self, i, make):
        self.copy(i, *make()).start()
        self.open.append((i, make))

    def arrived(self, i, ref, dev):
        self.copy(i, ref, ref, dev).wait_recv()

    def sent(self):
        for i, make in self.open:
            self.copy(i, *make()).wait_send()
        self.open = []


class Local:
    def __init__(self, sems):
        self.sems, self.next, self.open = sems, 0, []

    def start(self, make):
        i = self.next
        self.next += 1
        pltpu.make_async_copy(*make(), self.sems.at[i]).start()
        wait = lambda: pltpu.make_async_copy(*make(), self.sems.at[i]).wait()
        self.open.append(wait)
        return wait


def hops(p, y, x):
    ey, ex = (1 - y, x), (y, 1 - x)
    return (ey, ex) if p == 0 else (ex, ey)


def gather_stages(wire, depth, own, slot, plane=None):
    z, y, x, head = here()
    ids = {}
    for p in range(2):
        for k in range(depth):
            for kind in "zabc" + ("" if plane is None else "s"):
                ids[p, kind, k] = wire.slot()
    up = lambda k: (z + k) % depth
    down = lambda k: (z + depth - k) % depth

    def columns(p):
        (ay, ax), (by, bx) = hops(p, y, x)
        return (y, x), (ay, ax), (by, bx), (1 - y, 1 - x)

    def send_up(k):
        for p in range(2):
            wire.start(ids[p, "z", k], lambda p=p: (own(p), slot(p, z, y, x), at_dp(up(k), y, x)))

    def send_square(p, k, kind, col, to, first=False):
        def make():
            cs = columns(p)
            dst = slot(p, down(k), *cs[col])
            return own(p) if first else dst, dst, at_dp(z, *cs[to])
        wire.start(ids[p, kind, k], make)

    def wait(p, k, kind, col, frm):
        cs = columns(p)
        dev = at_dp(down(k), y, x) if frm is None else at_dp(z, *cs[frm])
        wire.arrived(ids[p, kind, k], slot(p, down(k), *cs[col]), dev)

    def begin():
        send_up(1)
        for p in range(2):
            send_square(p, 0, "a", 0, 1, True)
            send_square(p, 0, "b", 0, 2, True)
        for k in range(2, depth if plane is None else 2):
            send_up(k)

    def from_column(k):
        for p in range(2):
            wait(p, k, "z", 0, None)
            send_square(p, k, "a", 0, 1)
        for p in range(2):
            send_square(p, k, "b", 0, 2)
        if plane is not None and k + 1 < depth:
            send_up(k + 1)

    def from_first(k):
        for p in range(2):
            wait(p, k, "a", 1, 1)
            send_square(p, k, "c", 1, 2)

    def from_second(k):
        for p in range(2):
            wait(p, k, "b", 2, 2)
            wait(p, k, "c", 3, 2)

    def across(k):
        from_second(k)
        for p in range(2):
            def make(p=p):
                block = plane(p, down(k), head)
                return block, block, {"head": 1 - head}
            wire.start(ids[p, "s", k], make)

    def crossed(k):
        for p in range(2):
            wire.arrived(ids[p, "s", k], plane(p, down(k), 1 - head), {"head": 1 - head})

    part = functools.partial
    stages = {"begin": begin}
    for k in range(depth):
        for name, stage in (("z", from_column), ("a", from_first), ("d", from_second), ("s", across), ("x", crossed)):
            stages[name + str(k)] = part(stage, k)
    return stages


def add_into(dst, src):
    dst[...] = (dst[...].astype(F32) + src[...].astype(F32)).astype(dst.dtype)


class SquareSum:
    def __init__(self, wire, theirs, mine, pair_in, square_in, line_in):
        self.wire, self.theirs, self.mine = wire, theirs, mine
        self.pair_in, self.square_in, self.line_in = pair_in, square_in, line_in
        self.ids = {(p, kind): wire.slot() for p in range(2) for kind in "hab"}
        self.place = here()

    def devices(self, p):
        z, y, x, head = self.place
        ex, ey = at_dp(z, y, 1 - x), at_dp(z, 1 - y, x)
        return (ex, ey) if p == 0 else (ey, ex)

    def copy(self, p, kind):
        z, y, x, head = self.place
        if kind == "h":
            src, dst, dev = self.theirs(p), self.pair_in(p), {"head": 1 - head}
        elif kind == "a":
            src = self.mine(p, None, 1 - x) if p == 0 else self.mine(p, 1 - y, None)
            dst, dev = self.square_in(p), self.devices(p)[0]
        else:
            src = self.mine(p, 1 - y, x) if p == 0 else self.mine(p, y, 1 - x)
            dst, dev = self.line_in(p), self.devices(p)[1]
        return self.wire.copy(self.ids[p, kind], src, dst, dev)

    def pair(self):
        for p in range(2):
            self.copy(p, "h").start()

    def first(self):
        for p in range(2):
            self.wire.arrived(self.ids[p, "h"], self.pair_in(p), {"head": 1 - self.place[3]})
            add_into(self.mine(p, None, None), self.pair_in(p))
            self.copy(p, "a").start()

    def second(self):
        z, y, x, head = self.place
        for p in range(2):
            self.wire.arrived(self.ids[p, "a"], self.square_in(p), self.devices(p)[0])
            add_into(self.mine(p, None, x) if p == 0 else self.mine(p, y, None), self.square_in(p))
            self.copy(p, "b").start()

    def third(self):
        z, y, x, head = self.place
        for p in range(2):
            self.wire.arrived(self.ids[p, "b"], self.line_in(p), self.devices(p)[1])
            add_into(self.mine(p, y, x), self.line_in(p))

    def sent(self):
        for p in range(2):
            for kind in "hab":
                self.copy(p, kind).wait_send()


class ColumnSum:
    def __init__(self, wire, depth, part, column_in):
        self.wire, self.depth, self.part, self.column_in = wire, depth, part, column_in
        self.ids = {(p, k): wire.slot() for p in range(2) for k in range(1, depth)}
        self.place = here()

    def send(self, k):
        def make(p):
            z, y, x, head = self.place
            to = (z + self.depth - k) % self.depth
            return self.part(p, to), self.column_in(p, k), at_dp(to, y, x)

        for p in range(2):
            self.wire.start(self.ids[p, k], functools.partial(make, p))

    def total(self, p):
        z, y, x, head = self.place
        acc = self.part(p, z)[...].astype(F32)
        for k in range(1, self.depth):
            back = at_dp((z + k) % self.depth, y, x)
            self.wire.arrived(self.ids[p, k], self.column_in(p, k), back)
            acc = acc + self.column_in(p, k)[...].astype(F32)
        return acc


class SmallSum:
    def __init__(self, wire, depth, level, line):
        self.wire, self.depth, self.level, self.line = wire, depth, level, line
        self.ids = {flip: wire.slot() for flip in FLIPS}
        self.ups = [wire.slot() for _ in range(depth)]
        self.place = here()

    def begin(self, fill):
        z, y, x, head = self.place
        fill(self.level.at[head, y, x])
        for flip in FLIPS:
            def make(flip=flip):
                own = self.level.at[head, y, x]
                return own, own, flipped(self.place, flip)[0]
            self.wire.start(self.ids[flip], make)

    def meet(self):
        z, y, x, head = self.place
        for flip in FLIPS:
            dev, spot = flipped(self.place, flip)
            self.wire.arrived(self.ids[flip], self.level.at[spot], dev)
        total = self.level[0, 0, 0]
        for n in range(1, 8):
            total = total + self.level[n // 4, n // 2 % 2, n % 2]
        self.line[z] = total
        for k in range(1, self.depth):
            self.wire.start(
                self.ups[k],
                lambda k=k: (self.line.at[z], self.line.at[z], at_dp((z + k) % self.depth, y, x)),
            )

    def result(self):
        z, y, x, head = self.place
        for k in range(1, self.depth):
            back = (z + self.depth - k) % self.depth
            self.wire.arrived(self.ups[k], self.line.at[back], at_dp(back, y, x))
        total = self.line[0]
        for n in range(1, self.depth):
            total = total + self.line[n]
        return total


def bind(names, refs):
    assert len(names) == len(refs)
    return types.SimpleNamespace(**dict(zip(names, refs)))


def spread_mask(masked, tmp, ch):
    images, rows = masked.shape
    tmp[...] = jnp.zeros_like(tmp)
    tmp[0:images, 0:rows] = masked[...].astype(F32)
    turned = tmp[...].T
    for i in range(images):
        ch[i] = turned[0:rows, i:i + 1]


def pad_index(raw, idx):
    idx[...] = jnp.zeros_like(idx)
    idx[0:raw.shape[0], 0:raw.shape[1]] = raw[...]


def run_all(stages):
    for stage in stages:
        stage()


def vmem(n):
    return [pl.BlockSpec(memory_space=pltpu.VMEM)] * n

ANY = pl.BlockSpec(memory_space=pl.ANY)
sd = jax.ShapeDtypeStruct
dma = lambda n: pltpu.SemaphoreType.DMA((n,))
VECTORS = ("mask_token", "ln1_gain", "ln1_bias", "proj_bias", "gamma1", "ln2_gain", "ln2_bias", "fc2_bias", "gamma2")
GIVEN = ("x", "masked", "kv", "raw") + VECTORS + ("cot",)
KEPT = (
    "idx", "valid", "tmp", "ch", "bias", "nt", "q", "k", "v", "att", "res", "n2", "db", "act", "dpre", "dn",
    "small1", "small2", "gb1", "lsem",
)
SHARED = (
    "w", "wp", "mix", "b1", "b1line", "b1row", "g", "pair_in", "square_in", "line_in", "column", "column_in",
    "ar_pair", "ar_square", "ar_line", "ar_column", "gathered", "bufs", "line", "tbufs", "tline", "lbufs", "lline", "send", "recv",
)


class Row:
    def __init__(self, ref):
        self.ref = ref

    def __getitem__(self, at):
        return self.ref[...].reshape(1, -1)


def layer_kernel(direct, *refs):
    if direct:
        names = GIVEN + ("mixown", "wown", "wpown", "own1", "own2", "spot")
        names += ("out", "gx", "p", "w1", "w2", "full", "proj", "gff1", "gff2", "small", "table", "late") + KEPT + SHARED
    else:
        names = GIVEN + ("mix", "w", "wp", "w1", "w2", "b1")
        names += ("out", "gx", "p", "g1", "g2", "gw", "gt", "small1_out", "small2_out", "gb1_out") + KEPT
    r = bind(names, refs)
    for name in VECTORS:
        setattr(r, name, Row(getattr(r, name)))
    images, rows, width = r.x.shape
    heads, rp, keys = r.bias.shape
    flat = images * rp
    scale = (width // heads) ** -0.5
    pairs, per = heads // 2, heads // 4
    steps, block = r.b1.shape[-2:]
    own_heads = heads // r.mix.shape[0]
    own_tiles = width // r.mix.shape[0] // LANES
    chunks = (r.mix.shape[1] - 2 * own_tiles) // own_heads
    local = Local(r.lsem)
    z, y, x, head = here()
    plan = {}
    part = functools.partial
    every = lambda v: slice(None) if v is None else v
    level = lambda b: (z + 2 * steps - b) % steps
    at_image = lambda i: pl.multiple_of(i * rp, 16)

    if direct:
        depth = r.w1.shape[0]
        half = r.wown.shape[2]
        lanes_of = lambda hd: pl.ds(pl.multiple_of(hd * half, LANES), half)
        full = (r.w1, r.w2)
        wire = Wire(r.send, r.recv)
        greet(depth)
        other = {"head": 1 - head}
        swaps = [
            (r.mixown, lambda hd: r.mix.at[hd]),
            (r.wown, lambda hd: r.w.at[:, :, lanes_of(hd)]),
            (r.wpown, lambda hd: r.wp.at[lanes_of(hd)]),
        ]
        swap_ids = [wire.slot() for _ in swaps]
        bias_id = wire.slot()
        bias_of = lambda hd: r.bias.at[pl.ds(hd * own_heads, own_heads)]
        for i, (src, place) in zip(swap_ids, swaps):
            wire.start(i, lambda src=src, place=place: (src, place(head), other))
        for src, place in swaps:
            local.start(lambda src=src, place=place: (src, place(head)))
        slot = lambda p, zz, yy, xx: full[p].at[zz, yy, xx, head]
        own = (r.own1, r.own2)
        for p in range(2):
            local.start(lambda p=p: (own[p], slot(p, z, y, x)))
        bias_sum = SmallSum(wire, depth, r.b1, r.b1line)
        ag = gather_stages(
            wire, depth, own=lambda p: own[p], slot=slot,
            plane=lambda p, zz, hd: full[p].at[zz, :, :, hd],
        )
        ag["begin"]()

        def fill_bias(ref):
            ref[...] = r.spot[...]

        bias_sum.begin(fill_bias)
        squares = [
            SquareSum(
                wire,
                theirs=lambda p, b=b: r.g.at[b % 3, p, :, :, 1 - head],
                mine=lambda p, yy, xx, b=b: r.g.at[b % 3, p, every(yy), every(xx), head],
                pair_in=lambda p, b=b: r.pair_in.at[b % 2, p],
                square_in=lambda p, b=b: r.square_in.at[b % 2, p],
                line_in=lambda p, b=b: r.line_in.at[b % 2, p],
            )
            for b in range(steps)
        ]
        column = ColumnSum(wire, depth, part=lambda p, zz: r.column.at[p, zz], column_in=lambda p, k: r.column_in.at[p, k - 1])

        def close(b):
            squares[b].third()
            for p in range(2):
                r.column[p, level(b)] = r.g[b % 3, p, y, x, head]
            if b:
                column.send(b)
            squares[b].sent()

        early = SmallSum(wire, depth, r.bufs, r.line)
        tables = SmallSum(wire, depth, r.tbufs, r.tline)
        late = SmallSum(wire, depth, r.lbufs, r.lline)
        plan = {
            "p2": [ag["z1"], ag["a0"]], "t0": [bias_sum.meet],
            "t2": [ag["s0"], ag["a1"]], "t5": [ag["z2"], ag["s1"]], "t7": [ag["a2"]],
        }

    def tick(point):
        run_all(plan.get(point, ()))

    def tick_in(step, point):
        for key, stages in plan.items():
            if isinstance(key, tuple) and key[1] == point:
                pl.when(step == key[0])(part(run_all, stages))

    spread_mask(r.masked, r.tmp, r.ch)
    pad_index(r.raw, r.idx)
    r.valid[...] = jnp.zeros_like(r.valid)
    r.valid[0:r.kv.shape[0], 0:rows] = r.kv[...]

    def hidden_of(i):
        ch = r.ch[i]
        return r.x[i].astype(F32) * (1.0 - ch) + ch * r.mask_token[...]

    def attention_forward(normed, pring):
        normed[...] = jnp.zeros_like(normed)
        r.n2[...] = jnp.zeros_like(r.n2)
        r.res[...] = jnp.zeros_like(r.res)

        def first_norm(i, carry):
            n, _ = norm_parts(hidden_of(i))
            normed[pl.ds(at_image(i), rows), :] = (n * r.ln1_gain[...] + r.ln1_bias[...]).astype(BF16)
            return carry

        lax.fori_loop(0, images, first_norm, 0)
        if direct:
            for wait in local.open:
                wait()
            local.open = []

        def gather_head(h, carry):
            for side in range(keys // LANES):
                idx = r.idx[:, side * LANES:(side + 1) * LANES]
                low = idx & (LANES - 1)
                high = idx >> 7
                acc = jnp.zeros(idx.shape, F32)
                for c in range(chunks):
                    if direct:
                        row = r.mixown[pl.ds(h * chunks + c, 1), :]
                    else:
                        row = r.mix[h // own_heads, pl.ds((h % own_heads) * chunks + c, 1), :]
                    got = jnp.take_along_axis(jnp.broadcast_to(row, idx.shape), low, axis=1)
                    acc = jnp.where(high == c, got, acc)
                r.bias[head * own_heads + h if direct else h, :, side * LANES:(side + 1) * LANES] = acc
            return carry

        some = own_heads if direct else heads
        for n in range(3):
            lax.fori_loop(n * some // 3, (n + 1) * some // 3, gather_head, 0)
            tick("g%d" % n)
        if direct:
            wire.copy(bias_id, bias_of(head), bias_of(head), other).start()
            for n in range(3):
                wire.arrived(swap_ids[n], swaps[n][1](1 - head), other)
        zeros_tail = jnp.zeros((images, keys - rp, width), BF16)
        r.k[:, rp:, :] = zeros_tail
        r.v[:, rp:, :] = zeros_tail

        def bias_row(kind, nb):
            tiles = []
            for t in (2 * nb, 2 * nb + 1):
                at = own_heads * chunks + kind * own_tiles + t % own_tiles
                tiles.append(r.mix[t // own_tiles, at:at + 1, :])
            return jnp.concatenate(tiles, axis=1)

        for c, (dst, kind) in enumerate(((r.q, 0), (r.k, None), (r.v, 1))):
            for nb in range(width // 256):
                cols = slice(nb * 256, (nb + 1) * 256)
                acc = dot(normed[...], r.w[c, :, cols])
                if kind is not None:
                    acc = acc + bias_row(kind, nb)
                acc = acc.astype(BF16)
                if kind == 0:
                    acc = acc * scale
                for i in range(images):
                    dst[i, :rp, cols] = acc[i * rp:(i + 1) * rp]
            tick("p%d" % c)
        r.nt[...] = normed[...].T
        if direct:
            wire.arrived(bias_id, bias_of(1 - head), other)

        def attend(t, carry):
            i = t // pairs
            j = t % pairs
            lanes = pl.ds(pl.multiple_of(j * LANES, LANES), LANES)
            qp = r.q[i, :, lanes]
            kp = r.k[i, :, lanes]
            vp = r.v[i, :, lanes]
            lo = low_half((rp, LANES))
            ok = r.valid[pl.ds(head * images + i, 1), :] > 0
            outs = []
            for s in range(2):
                qs = jnp.where(lo if s == 0 else jnp.logical_not(lo), qp, jnp.zeros_like(qp))
                sc = dot_nt(qs, kp) + r.bias[2 * j + s]
                sc = jnp.where(ok, sc, -1e30)
                e = jnp.exp(sc - jnp.max(sc, axis=-1, keepdims=True))
                prob = e * (1.0 / jnp.sum(e, axis=-1, keepdims=True))
                pring[i % 2, 2 * j + s] = prob
                outs.append(dot(prob.astype(BF16), vp))
            r.att[pl.ds(at_image(i), rp), lanes] = jnp.where(lo, outs[0], outs[1]).astype(BF16)
            return carry

        stored = {}
        for n in range(2 * images):
            i = n // 2
            if n % 2 == 0 and i >= 2:
                stored[i - 2]()
            lax.fori_loop(n * pairs // 2, (n + 1) * pairs // 2, attend, 0)
            if n % 2:
                stored[i] = local.start(lambda i=i: (pring.at[i % 2], r.p.at[i]))
            tick("t%d" % n)

        def finish(t, carry):
            both = dot(r.att[pl.ds(at_image(2 * t), 2 * rp), :], r.wp[...]) + r.proj_bias[...]
            for side in range(2):
                i = 2 * t + side
                res = hidden_of(i) + r.gamma1[...] * both[side * rp:side * rp + rows]
                r.res[pl.ds(at_image(i), rows), :] = res
                n, _ = norm_parts(res)
                r.n2[pl.ds(at_image(i), rows), :] = (n * r.ln2_gain[...] + r.ln2_bias[...]).astype(BF16)
            return carry

        lax.fori_loop(0, images // 2, finish, 0)
        stored[images - 2]()
        stored[images - 1]()

    pl.run_scoped(attention_forward, pltpu.VMEM((flat, width), BF16), pltpu.VMEM((2, heads, rp, keys), F32))

    if direct:
        wire.copy(bias_id, bias_of(head), bias_of(head), other).wait_send()
        ag["x0"]()
        r.b1row[...] = bias_sum.result()
        plan = {
            (0, 0): [ag["x1"]], (0, 1): [ag["z3"]], (0, 2): [ag["s2"]], (0, 4): [ag["a3"], squares[0].pair],
            (1, 0): [ag["x2"]], (1, 1): [squares[0].first, ag["s3"]], (1, 4): [squares[1].pair],
            (2, 0): [ag["x3"]], (2, 1): [squares[0].second, squares[1].first], (2, 4): [squares[2].pair],
            (3, 1): [part(close, 0), squares[1].second, squares[2].first], (3, 4): [squares[3].pair],
        }

    def feed_forward(cot, branch, slots, sems):
        def weights(b, into):
            copies = []
            for p, src in enumerate((r.w1, r.w2)):
                if direct:
                    view = src.at[level(b)]
                else:
                    view = src.at[pl.ds(pl.multiple_of(level(b) * block, 16), block)]
                copies.append(pltpu.make_async_copy(view, slots.at[into, p], sems.at[into, p]))
            return copies

        for copy in weights(0, 0):
            copy.start()
        fetch = pltpu.make_async_copy(r.cot, cot, sems.at[2, 0])
        fetch.start()
        r.db[...] = jnp.zeros_like(r.db)
        branch[...] = jnp.zeros_like(branch)
        r.dn[...] = jnp.zeros_like(r.dn)
        fetch.wait()

        def fill(i, carry):
            r.db[pl.ds(at_image(i), rows), :] = (cot[i].astype(F32) * r.gamma2[...]).astype(BF16)
            return carry

        lax.fori_loop(0, images, fill, 0)

        def step(b, carry):
            slot = b % 2
            t = level(b)
            for copy in weights(b, slot):
                copy.wait()
            tick_in(b, 0)

            @pl.when(b + 1 < steps)
            def _():
                for copy in weights(b + 1, 1 - slot):
                    copy.start()

            w1 = lambda: slots[slot, 0].reshape(block, width)
            w2 = lambda: slots[slot, 1].reshape(block, width)
            b1 = (r.b1row if direct else r.b1)[pl.ds(t, 1), :]

            def tile(i, gb1):
                at = pl.ds(pl.multiple_of(i * 2 * rp, 16), 2 * rp)
                pre = dot_nt(r.n2[at, :], w1()) + b1
                cdf = 0.5 * (1.0 + lax.erf(pre * 0.7071067811865476))
                slope = cdf + pre * (0.3989422804014327 * jnp.exp(-0.5 * pre * pre))
                act = (pre * cdf).astype(BF16)
                r.act[at, :] = act
                dpre = (dot_nt(r.db[at, :], w2()) * slope).astype(BF16)
                r.dpre[at, :] = dpre
                branch[at, :] += dot(act, w2())
                r.dn[at, :] += dot(dpre, w1())
                return gb1 + jnp.sum(dpre.astype(F32), axis=0, keepdims=True)

            gb1 = lax.fori_loop(0, images // 4, tile, jnp.zeros((1, block), F32))
            tick_in(b, 1)
            r.gb1[pl.ds(t, 1), :] = lax.fori_loop(images // 4, images // 2, tile, gb1)
            tick_in(b, 2)

            def store(p, value):
                value = value.astype(BF16)
                if direct:
                    r.g[b % 3, p] = value.reshape(r.g.shape[2:])
                else:
                    slots[slot, p] = value
                    dst = (r.g1, r.g2)[p].at[pl.ds(pl.multiple_of(t * block, 16), block)]
                    copy = pltpu.make_async_copy(slots.at[slot, p], dst, sems.at[3, p])
                    copy.start()
                    copy.wait()

            second = dot_tn(r.act[...], r.db[...])
            store(1, second)
            tick_in(b, 3)
            store(0, dot_tn(r.dpre[...], r.n2[...]))
            tick_in(b, 4)
            return carry

        lax.fori_loop(0, steps, step, 0)
        r.small2[...] = jnp.zeros_like(r.small2)
        r.n2[...] = jnp.zeros_like(r.n2)

        def add(row, value):
            r.small2[row:row + 1, :] += jnp.sum(value, axis=0, keepdims=True)

        def finish(i, carry):
            span = pl.ds(at_image(i), rows)
            up = cot[i].astype(F32)
            mlp = branch[span, :] + r.fc2_bias[...]
            res = r.res[span, :]
            cot[i] = (res + r.gamma2[...] * mlp).astype(BF16)
            add(S_GA2, up * mlp)
            add(S_FB2, (up * r.gamma2[...]).astype(BF16).astype(F32))
            n, inv = norm_parts(res)
            dn = r.dn[span, :]
            add(S_LG2, dn * n)
            add(S_LB2, dn)
            dres = up + norm_back(n, inv, dn, r.ln2_gain[...])
            add(S_GA1, dres * (res - hidden_of(i)))
            r.res[span, :] = dres
            dproj = (dres * r.gamma1[...]).astype(BF16)
            r.n2[span, :] = dproj
            add(S_PB, dproj.astype(F32))
            return carry

        lax.fori_loop(0, images, finish, 0)
        r.small2[S_GA1:S_GA1 + 1, :] = r.small2[S_GA1:S_GA1 + 1, :] / r.gamma1[...]
        store_out = pltpu.make_async_copy(cot, r.out, sems.at[2, 1])
        store_out.start()
        store_out.wait()

    if direct:
        slots_shape = (2, 2) + r.w1.shape[1:]
    else:
        slots_shape = (2, 2, block, width)
    pl.run_scoped(
        feed_forward, pltpu.VMEM(r.cot.shape, BF16), pltpu.VMEM((flat, width), F32),
        pltpu.VMEM(slots_shape, BF16), pltpu.SemaphoreType.DMA((4, 2)),
    )
    plan = {}

    def attention_backward(pbuf, dpt, g, sems):
        nonlocal plan
        dqkv = (r.act, r.dpre, r.n2)
        pair_of = lambda s: (s % 2) * per + s // 2

        def fetch(t):
            src = r.p.at[t % images, pl.ds(2 * pair_of(t // images), 2)]
            return pltpu.make_async_copy(src, pbuf.at[t % 3], sems.at[t % 3])

        for t in range(2):
            fetch(t).start()
        if direct:
            ar, lines, gathers = [], [], []
            for m in range(per):
                ar.append(SquareSum(
                    wire,
                    theirs=lambda p, m=m: g.at[m, 1 - head, p],
                    mine=lambda p, yy, xx, m=m: g.at[m, head, p, :, :, every(yy), every(xx)],
                    pair_in=lambda p, m=m: r.ar_pair.at[m, p],
                    square_in=lambda p, m=m: r.ar_square.at[m, p], line_in=lambda p, m=m: r.ar_line.at[m, p],
                ))
                lines.append(ColumnSum(
                    wire, depth, part=lambda p, zz, m=m: g.at[m, head, p, :, zz, y, x],
                    column_in=lambda p, k, m=m: r.ar_column.at[m, p, k - 1],
                ))
                lanes_m = slice(m * LANES, (m + 1) * LANES)
                into = lambda p, zz, yy, xx, lanes_m=lanes_m: r.gathered.at[p, :, zz, yy, xx, :, lanes_m]
                gathers.append(gather_stages(wire, depth, own=lambda p, into=into: into(p, z, y, x), slot=into))

            def third(m):
                ar[m].third()
                for k in range(1, depth):
                    lines[m].send(k)

            def last(m):
                for p in range(2):
                    r.gathered[p, :, z, y, x, :, m * LANES:(m + 1) * LANES] = lines[m].total(p).astype(BF16)
                gathers[m]["begin"]()

            def ff_last():
                for p in range(2):
                    (r.gff1, r.gff2)[p][...] = column.total(p)

            def early_begin():
                def fill(ref):
                    ref[...] = jnp.zeros(ref.shape, F32)
                    ref[0:8] = r.small2[...]
                    ref[8:8 + steps] = r.gb1[...]
                early.begin(fill)

            g0, g1, g2 = gathers
            plan = {
                "start": [part(close, 1), squares[2].second, squares[3].first, early_begin],
                (0, 4): [part(close, 2)], (1, 1): [squares[3].second, early.meet], (1, 4): [ar[0].pair],
                (2, 2): [ar[0].first], (2, 3): [part(close, 3)],
                (3, 2): [ar[0].second], (3, 4): [ar[1].pair], (4, 1): [part(third, 0)], (4, 2): [ar[1].first],
                (5, 1): [part(last, 0)], (5, 2): [ar[1].second], (5, 4): [ar[2].pair, g0["z1"], g0["z2"], g0["z3"]],
                (5, 5): [ar[2].first, part(third, 1)], (5, 6): [g0["a0"], g0["a1"], g0["a2"], g0["a3"]],
                (5, 7): [part(last, 1)], (5, 8): [ar[2].second], (5, 9): [g1["z1"], g1["z2"], g1["z3"]],
                (5, 10): [part(third, 2)], (5, 11): [g0["d0"], g0["d1"], g0["d2"], g0["d3"]],
                (5, 12): [part(last, 2), tables.meet, g1["a0"], g1["a1"], g1["a2"], g1["a3"]],
            }

        tick("start")
        for t in range(images // 2):
            at = slice(2 * t * rp, 2 * (t + 1) * rp)
            r.db[at, :] = dot_nt(r.n2[at, :], r.wp[...]).astype(BF16)
        dpt[...] = r.n2[...].T
        r.small1[...] = jnp.zeros_like(r.small1)

        def step(s, carry):
            j = pair_of(s)
            tick_in(s, 1)
            lanes = pl.ds(pl.multiple_of(j * LANES, LANES), LANES)
            r.bias[2 * j] = jnp.zeros((rp, keys), F32)
            r.bias[2 * j + 1] = jnp.zeros((rp, keys), F32)

            def image(i, carry):
                t = s * images + i
                fetch(t).wait()

                @pl.when(t + 2 < pairs * images)
                def _():
                    fetch(t + 2).start()

                at = pl.ds(at_image(i), rp)
                qp = r.q[i, :, lanes]
                kp = r.k[i, :, lanes]
                vp = r.v[i, :, lanes]
                da = r.db[at, lanes]
                lo = low_half((rp, LANES))
                dv, dq, dk = [], [], []
                for n in range(2):
                    das = jnp.where(lo if n == 0 else jnp.logical_not(lo), da, jnp.zeros_like(da))
                    prob = pbuf[t % 3, n]
                    dp = dot_nt(das, vp)
                    dsc = prob * (dp - jnp.sum(prob * dp, axis=-1, keepdims=True))
                    dsb = dsc.astype(BF16)
                    r.bias[2 * j + n] += dsb.astype(F32)
                    dv.append(dot_tn(prob.astype(BF16), da))
                    dq.append(dot(dsb, kp))
                    dk.append(dot_tn(dsb, qp))
                lok = low_half((keys, LANES))
                dqkv[0][at, lanes] = (jnp.where(lo, dq[0], dq[1]) * scale).astype(BF16)
                dqkv[1][at, lanes] = jnp.where(lok, dk[0], dk[1])[:rp].astype(BF16)
                dqkv[2][at, lanes] = jnp.where(lok, dv[0], dv[1])[:rp].astype(BF16)
                return carry

            lax.fori_loop(0, images // 2, image, 0, unroll=True)
            tick_in(s, 2)
            lax.fori_loop(images // 2, images, image, 0, unroll=True)
            tick_in(s, 3)

            def store(c, value):
                value = value.astype(BF16)
                if direct:
                    g[s // 2, s % 2, c // 2, c % 2] = value.reshape(g.shape[4:])
                else:
                    g[...] = value
                    copy = pltpu.make_async_copy(g, r.gw.at[j, c], sems.at[3])
                    copy.start()
                    copy.wait()

            three = dot(r.nt[...], jnp.concatenate([dqkv[c][:, lanes] for c in range(3)], axis=1))
            for c in range(3):
                store(c, three[:, c * LANES:(c + 1) * LANES])
            store(3, dot(dpt[...], r.att[:, lanes]))
            tick_in(s, 4)
            return carry

        lax.fori_loop(0, pairs, step, 0)
        now = lambda point: run_all(plan.get((pairs - 1, point), ()))

        def total_rows(row, c):
            def add(i, acc):
                return acc + jnp.sum(dqkv[c][pl.ds(at_image(i), rp), :].astype(F32), axis=0, keepdims=True)
            r.small1[row:row + 1, :] = lax.fori_loop(0, images, add, jnp.zeros((1, width), F32))

        total_rows(T_QB, 0)
        total_rows(T_VB, 2)

        a_iota = lax.broadcasted_iota(jnp.int32, (8, keys), 0)
        b_iota = lax.broadcasted_iota(jnp.int32, (LANES, keys), 0)

        def scatter(t, acc):
            at = pl.ds(pl.multiple_of(t * 8, 8), 8)
            idx = r.idx[at, :]
            high, low = idx >> 7, idx & (LANES - 1)
            tiles = [r.bias[h, at, :] for h in range(heads)]
            lefts, rests, ones = [], [], []
            for n in range(8):
                pick = jnp.broadcast_to(high[n:n + 1], (8, keys)) == a_iota
                ones.append((jnp.broadcast_to(low[n:n + 1], (LANES, keys)) == b_iota).astype(F32).astype(BF16))
                left = jnp.concatenate(
                    [jnp.where(pick, jnp.broadcast_to(tile[n:n + 1], (8, keys)), 0.0) for tile in tiles], axis=0)
                top = left.astype(BF16)
                lefts.append(top)
                rests.append((left - top.astype(F32)).astype(BF16))
            one = jnp.concatenate(ones, axis=1)
            return acc + dot_nt(jnp.concatenate(lefts, axis=1), one) + dot_nt(jnp.concatenate(rests, axis=1), one)

        table = jnp.zeros((heads * 8, LANES), F32)
        blocks = rp // 8
        for n in range(5):
            table = lax.fori_loop(n * blocks // 5, (n + 1) * blocks // 5, scatter, table)
            now(5 + n)
        wide = width // LANES
        tall = heads * 8 // wide
        if direct:
            def fill_table(ref):
                for t in range(wide):
                    ref[:, t * LANES:(t + 1) * LANES] = table[t * tall:(t + 1) * tall]
            tables.begin(fill_table)
        def finish(i, carry):
            span = pl.ds(at_image(i), rp)
            dn = dot_nt(dqkv[0][span, :], r.w[0])
            dn += dot_nt(dqkv[1][span, :], r.w[1])
            dn += dot_nt(dqkv[2][span, :], r.w[2])
            dn = dn[:rows]
            ch = r.ch[i]
            n, inv = norm_parts(hidden_of(i))
            dh = r.res[pl.ds(at_image(i), rows), :] + norm_back(n, inv, dn, r.ln1_gain[...])
            r.dn[pl.ds(at_image(i), rows), :] = dh * (1.0 - ch)
            for row, value in ((T_MASK, dh * ch), (T_LG1, dn * n), (T_LB1, dn)):
                r.small1[row:row + 1, :] += jnp.sum(value, axis=0, keepdims=True)
            return carry

        leaving = []
        for i in range(images):
            lax.fori_loop(i, i + 1, finish, 0)
            leaving.append(local.start(lambda i=i: (r.dn.at[pl.ds(i * rp, rows)], r.gx.at[i])))
            now(10 + i)

        for wait in leaving:
            wait()
        if not direct:
            r.gt[...] = table
            r.small1_out[...] = r.small1[...]
            r.small2_out[...] = r.small2[...]
            r.gb1_out[...] = r.gb1[...]
            return

        def fill_late(ref):
            ref[...] = r.small1[...]

        late.begin(fill_late)
        r.small[...] = early.result()
        ff_last()
        run_all(g2["z%d" % k] for k in range(1, depth))
        late.meet()
        run_all(g1["d%d" % k] for k in range(depth))
        run_all(g2["a%d" % k] for k in range(depth))
        r.table[...] = tables.result()
        run_all(g2["d%d" % k] for k in range(depth))
        keep = [
            local.start(lambda: (r.gathered.at[0], r.full.at[0:2])),
            local.start(lambda: (r.gathered.at[1, 0], r.full.at[2])),
        ]
        tall_p = r.proj.shape[0]
        r.n2[0:tall_p, :] = r.gathered[1, 1].reshape(width, tall_p).T
        keep_proj = local.start(lambda: (r.n2.at[0:tall_p], r.proj))
        r.late[...] = late.result()
        keep_proj()
        for m in range(per):
            ar[m].sent()
        wire.sent()
        for wait in keep:
            wait()

    if direct:
        g_shape = (per, 2, 2, 2, depth, 2, 2) + r.gathered.shape[5:6] + (LANES,)
    else:
        g_shape = (width, LANES)
    pl.run_scoped(
        attention_backward, pltpu.VMEM((3, 2, rp, keys), F32), pltpu.VMEM((width, flat), BF16),
        pltpu.VMEM(g_shape, BF16), dma(4),
    )


def layer(direct, given, extra, heads, rp, keys, depth):
    x, kv = given[0], given[2]
    images, rows, width = x.shape
    flat = images * rp
    tall = -(-max(kv.shape[0], images) // 8) * 8
    steps = 4
    ff = extra[-1].size
    outs = [sd(x.shape, BF16), sd(x.shape, F32), sd((images, heads, rp, keys), F32)]
    out_specs = [ANY] * 3
    bf = lambda *shape: pltpu.VMEM(shape, BF16)
    fl = lambda *shape: pltpu.VMEM(shape, F32)
    scratch = [
        pltpu.VMEM((rp, keys), jnp.int32), pltpu.VMEM((tall, keys), jnp.int32), fl(tall, keys), fl(images, rows, 1),
        fl(heads, rp, keys), bf(width, flat), bf(images, rp, width), bf(images, keys, width), bf(images, keys, width),
        bf(flat, width), fl(flat, width), bf(flat, width), bf(flat, width), bf(flat, width), bf(flat, width),
        fl(flat, width), fl(8, width), fl(8, width), fl(steps, ff // steps), dma(24),
    ]
    in_specs = vmem(len(given) - 1) + [ANY]
    params = {}
    if direct:
        mixown, wown, wpown, own1, own2, spot = extra
        per = heads // 4
        share = own1.shape[0]
        own = width // (4 * depth)
        total = 8 + 8
        tall_t = heads * 8 * LANES // width
        big = sd((depth, 2, 2, 2) + own1.shape, BF16)
        outs += [big, big, sd((3, depth, 2, 2, own, per * LANES), BF16), sd((per * LANES, width), BF16)]
        outs += [sd((share, width), F32), sd((share, width), F32)]
        outs += [sd((total, width), F32), sd((tall_t, width), F32), sd((8, width), F32)]
        in_specs += vmem(6)
        out_specs += [ANY] * 4 + vmem(5)
        n = 4 + 2 * (4 * depth + 4) + 4 * (7 + depth) + 6 * steps + 2 * (depth - 1)
        n += per * (6 + 2 * (depth - 1) + 8 * depth)
        scratch += [
            bf(3, width, width), bf(width, width), fl(2, *mixown.shape), fl(2, 2, 2, *spot.shape), fl(depth, *spot.shape), fl(*spot.shape),
            bf(3, 2, 2, 2, 2, share, width), bf(2, 2, 2, 2, share, width), bf(2, 2, 2, share, width), bf(2, 2, share, width),
            bf(2, depth, share, width), bf(2, depth - 1, share, width),
            bf(per, 2, 2, depth, 2, 2, own, LANES), bf(per, 2, 2, depth, 2, own, LANES), bf(per, 2, 2, depth, own, LANES),
            bf(per, 2, depth - 1, 2, own, LANES), bf(2, 2, depth, 2, 2, own, per * LANES),
            fl(2, 2, 2, total, width), fl(depth, total, width), fl(2, 2, 2, tall_t, width), fl(depth, tall_t, width), fl(2, 2, 2, 8, width), fl(depth, 8, width), dma(n), dma(n),
        ]
        params = dict(collective_id=1, has_side_effects=True)
    else:
        part = sd((ff, width), BF16)
        outs += [part, part, sd((heads // 2, 4, width, LANES), BF16), sd((heads * 8, LANES), F32)]
        outs += [sd((8, width), F32), sd((8, width), F32), sd((steps, ff // steps), F32)]
        in_specs += vmem(3) + [ANY, ANY] + vmem(1)
        out_specs += [ANY] * 3 + vmem(4)
    return pl.pallas_call(
        functools.partial(layer_kernel, direct), name="layer",
        out_shape=tuple(outs), in_specs=in_specs, out_specs=out_specs, scratch_shapes=scratch,
        compiler_params=pltpu.CompilerParams(vmem_limit_bytes=63 * 2**20, **params),
    )(*given, *extra)


def shards(
    inputs, masked, key_valid, rel_index, mask_token, ln1_gain, ln1_bias, w_qkv, qv_bias, rel_table,
    w_proj, proj_bias, gamma1, ln2_gain, ln2_bias, w_fc1, fc1_bias, w_fc2, fc2_bias, gamma2, cotangent,
):
    images, rows, width = inputs.shape
    dp, hn = lax.axis_size("dp"), lax.axis_size("head")
    me, head = lax.axis_index("dp"), lax.axis_index("head")
    depth = dp // 4
    share = w_fc2.shape[0]
    ff = share * dp * hn
    entries, heads = rel_table.shape[0], rel_table.shape[1] * hn
    rp, keys = -(-rows // 16) * 16, -(-rows // LANES) * LANES
    direct = hn == 2 and dp == 16 and share % 16 == 0 and width % (16 * dp) == 0

    tab_rows = -(-entries // LANES)
    tab = jnp.pad(rel_table.T, ((0, 0), (0, tab_rows * LANES - entries)))
    mix = jnp.concatenate([tab.reshape(-1, LANES), qv_bias.reshape(-1, LANES)])
    vectors = (mask_token, ln1_gain, ln1_bias, proj_bias, gamma1, ln2_gain, ln2_bias, fc2_bias, gamma2)
    given = (inputs, masked, key_valid, rel_index) + vectors + (cotangent,)
    w3 = jnp.transpose(w_qkv, (1, 0, 2))
    if direct:
        spot_shape = (4, ff // 4)
        owner = (lax.broadcasted_iota(jnp.int32, spot_shape, 0) * (ff // 4) + lax.broadcasted_iota(jnp.int32, spot_shape, 1)) // share
        spot = jnp.where(owner == me * hn + head, jnp.tile(fc1_bias.astype(F32), ff // 4 // share)[None], 0.0)
        extra = (mix, w3, w_proj, w_fc1.T, w_fc2, spot)
        out, gx, _, _, _, full, proj, g_fc1, g_fc2, small, table, late = layer(True, given, extra, heads, rp, keys, depth)
        g_qkv, g_proj = full.reshape(3, width, -1).astype(F32), proj.astype(F32)
        s1, s2 = late, small[:8]
        wide = width // LANES
        tall = heads * 8 // wide
        table = jnp.transpose(table.reshape(tall, wide, LANES), (1, 0, 2)).reshape(heads, -1)
        g_b1 = small[8:12].reshape(-1)
    else:
        w = lax.all_gather(w3, "head", axis=2, tiled=True)
        wp = lax.all_gather(w_proj, "head", axis=0, tiled=True)
        w1 = lax.all_gather(w_fc1.T, ("dp", "head"), axis=0, tiled=True)
        w2 = lax.all_gather(w_fc2, ("dp", "head"), axis=0, tiled=True)
        b1 = lax.all_gather(fc1_bias, ("dp", "head"), axis=0, tiled=True).astype(F32).reshape(4, -1)
        extra = (lax.all_gather(mix, "head", axis=0), w, wp, w1, w2, b1)
        out, gx, _, ga, gb, gw, gt, s1, s2, gb1 = layer(False, given, extra, heads, rp, keys, depth)
        g_fc1 = lax.psum_scatter(ga.astype(F32), ("dp", "head"), scatter_dimension=0, tiled=True)
        g_fc2 = lax.psum_scatter(gb.astype(F32), ("dp", "head"), scatter_dimension=0, tiled=True)
        full = lax.psum(lax.psum_scatter(gw.astype(F32), "head", scatter_dimension=0, tiled=True), "dp")
        full = jnp.transpose(full, (1, 2, 0, 3)).reshape(4, width, -1)
        g_qkv, g_proj = full[:3], full[3].T
        s1, s2, table, g_b1 = lax.psum((s1, s2, gt.reshape(heads, -1), gb1.reshape(-1)), ("dp", "head"))
    g_table = lax.dynamic_slice_in_dim(table, head * (heads // hn), heads // hn, 0)[:, :entries].T
    g_b1 = lax.dynamic_slice_in_dim(g_b1, (me * hn + head) * share, share)
    g_qvb = lax.dynamic_slice_in_dim(s1[T_QB:T_VB + 1], head * (width // hn), width // hn, 1)
    return (
        out, gx, s1[T_MASK], s1[T_LG1], s1[T_LB1], jnp.transpose(g_qkv, (1, 0, 2)), g_qvb, g_table, g_proj,
        s2[S_PB], s2[S_GA1], s2[S_LG2], s2[S_LB2], g_fc1.T, g_b1, g_fc2, s2[S_FB2], s2[S_GA2],
    )


def solution(mesh):
    in_specs = (
        P(("dp", "head"), None, None),
        P(("dp", "head"), None),
        P("dp", None),
        P(),
        P(),
        P(),
        P(),
        P(None, None, "head"),
        P(None, "head"),
        P(None, "head"),
        P("head", None),
        P(),
        P(),
        P(),
        P(),
        P(None, ("dp", "head")),
        P(("dp", "head")),
        P(("dp", "head"), None),
        P(),
        P(),
        P(("dp", "head"), None, None),
    )
    out_specs = (
        P(("dp", "head"), None, None),
        P(("dp", "head"), None, None),
        P(),
        P(),
        P(),
        P(None, None, "head"),
        P(None, "head"),
        P(None, "head"),
        P("head", None),
        P(),
        P(),
        P(),
        P(),
        P(None, ("dp", "head")),
        P(("dp", "head")),
        P(("dp", "head"), None),
        P(),
        P(),
    )
    return jax.shard_map(shards, mesh=mesh, in_specs=in_specs, out_specs=out_specs, check_vma=False)
```
